256 devices in a mesh: gx: 8 (over z_hi, core), gy: 16 (over y, x), gz: 2 (over z_lo).
Axes of the slice: x: 4, y: 4, z: 8 (z_hi: 4, z_lo: 2; z = z_hi * 2 + z_lo), core: 2. Of those that a mesh axis runs over, the one named last changes fastest.
Arguments:
- right_side: float32 [64, 512, 512], P('gx', 'gy', 'gz'), may hold values from -4 to 4
- volscale: float32 [64, 512, 512], P('gx', 'gy', 'gz'), may hold values from 0.5 to 2
Outputs:
- solution: float32 [64, 512, 512], P('gx', 'gy', 'gz')
- residual: float32 [64, 512, 512], P('gx', 'gy', 'gz')
The draws below stay inside these ranges and needn't reach their ends.
All inputs are finite; a program needn't handle non-finite values.
Results may differ from the reference program's by a relative error of at most 0.000047.
Values sent between devices are 32-bit elements; how exact they have to be, the bound alone decides.
A program may use at most 64 MiB of HBM per device.

```python
import math
import jax
import jax.numpy as jnp
from jax import lax

NX = 64
NY = 512
NZ = 512


def draw_right_side(key, part):
    base = jnp.clip(jax.random.normal(key, (NX, NY, NZ), jnp.float32), -4.0, 4.0)
    return base


def block_scale(rng, dims, pieces, smallest, largest):
    def one(position, parts):
        draws = jax.random.uniform(jax.random.fold_in(jax.random.fold_in(rng, 6), position), (parts,), jnp.float32, smallest / len(pieces), largest / len(pieces))
        return jnp.repeat(jnp.exp(draws), dims[position] // parts).reshape((-1,) + (1,) * (len(dims) - position - 1))

    gain = one(*pieces[0])
    for cut in pieces[1:]:
        gain = gain * one(*cut)
    return gain


def setup_inputs(seed: int = 0) -> dict:
    keys = jax.random.split(jax.random.key(seed), 3)
    return {
        "right_side": draw_right_side(jax.random.fold_in(keys[2], 71), 0),
        "volscale": jnp.clip(jnp.exp(math.log(2.0) - 1.3862944 * jax.random.uniform(keys[1], (NX, NY, NZ), jnp.float32) ** block_scale(keys[1], (NX, NY, NZ), ((0, 8), (1, 16), (2, 2)), -0.2, 0.2)), 0.5, 2.0),
    }


diffusion_rates = (48.0, 40.0, 32.0)
cross_rates = (8.0, 6.0, -6.0)
drift_rates = (3.0, -2.0, 1.5)
total_rate = 120.0
discount = 0.05
damping = 0.6


def operate(padded, local_scale, spacing):
    extent = local_scale.shape

    def shifted(offset):
        starts = tuple(1 + offset[dim_index] for dim_index in range(3))
        stops = tuple(starts[dim_index] + extent[dim_index] for dim_index in range(3))
        return lax.slice(padded, starts, stops)

    center = shifted((0, 0, 0))
    curvature_factor = 1.0 / (spacing * spacing)
    slope_factor = 0.5 / spacing
    second = jnp.zeros_like(center)
    slopes = jnp.zeros_like(center)
    for dim_index in range(3):
        forward = shifted(tuple(1 if other == dim_index else 0 for other in range(3)))
        backward = shifted(tuple(-1 if other == dim_index else 0 for other in range(3)))
        second = second + diffusion_rates[dim_index] * curvature_factor * (forward + backward - 2.0 * center)
        slopes = slopes + drift_rates[dim_index] * slope_factor * (forward - backward)
    pairs_list = ((0, 1), (0, 2), (1, 2))
    for pair_index in range(3):
        first_axis, second_axis = pairs_list[pair_index]

        def corner(sign_first, sign_second):
            offset = [0, 0, 0]
            offset[first_axis] = sign_first
            offset[second_axis] = sign_second
            return shifted(tuple(offset))

        mixed = corner(1, 1) - corner(1, -1) - corner(-1, 1) + corner(-1, -1)
        second = second + cross_rates[pair_index] * 0.25 * curvature_factor * mixed
    return (1.0 + discount) * center - local_scale * second - slopes


def diagonal_of(local_scale, spacing):
    return (1.0 + discount) + 2.0 * total_rate * local_scale / (spacing * spacing)


def relax_step(current, applied, source, local_scale, spacing):
    return current + damping * (source - applied) / diagonal_of(local_scale, spacing)


def coarsen(values):
    size_x, size_y, size_z = values.shape
    return values.reshape(size_x // 2, 2, size_y // 2, 2, size_z // 2, 2).sum(axis=(1, 3, 5)) * 0.125


def refine(values):
    size_x, size_y, size_z = values.shape
    copies = jnp.broadcast_to(values[:, None, :, None, :, None], (size_x, 2, size_y, 2, size_z, 2))
    return copies.reshape(2 * size_x, 2 * size_y, 2 * size_z)


def plain_sweep(current, source, local_scale, spacing):
    applied = operate(jnp.pad(current, 1), local_scale, spacing)
    return relax_step(current, applied, source, local_scale, spacing)


def reference(right_side, volscale):
    smoothed = right_side
    for sweep_index in range(2):
        smoothed = plain_sweep(smoothed, right_side, volscale, 1.0)
    residue = right_side - operate(jnp.pad(smoothed, 1), volscale, 1.0)
    coarse_rhs = coarsen(residue)
    coarse_scale = coarsen(volscale)
    correction = damping * coarse_rhs / diagonal_of(coarse_scale, 2.0)
    for sweep_index in range(3):
        correction = plain_sweep(correction, coarse_rhs, coarse_scale, 2.0)
    solution = smoothed + refine(correction)
    for sweep_index in range(2):
        solution = plain_sweep(solution, right_side, volscale, 1.0)
    residual = right_side - operate(jnp.pad(solution, 1), volscale, 1.0)
    return solution, residual
```

```python
import jax
import jax.numpy as jnp
from jax import lax
from jax.experimental import pallas as pl
from jax.experimental.pallas import tpu as pltpu
from jax.sharding import PartitionSpec as P

MESH = pl.DeviceIdType.MESH
F32 = jnp.float32
NXD, NYD = 8, 16
BX, BY = 8, 32
HALO = 5
PX = BX + 2 * HALO
ROWS = BY + 16
CX = BX // 2 + 2 * HALO
CROWS = BY // 2 + 16
DAMP = 0.6


def main_messages():
    out = []
    for dx in (1, -1, 0):
        for dy in (0, 1, -1):
            if dx == 0 and dy == 0:
                continue
            if dy == 0:
                rs, rd = (8, 32), (8, 32)
            elif dy == 1:
                rs, rd = (35, 5), (3, 5)
            else:
                rs, rd = (8, 5), (40, 5)
            if dx == 0:
                for a in (0, 1):
                    out.append((0, dx, dy, a, (5, 8), (5, 8), rs, rd))
            elif dx == 1:
                out.append((0, dx, dy, 0, (10, 3), (2, 3), rs, rd))
                out.append((0, dx, dy, 1, (11, 2), (3, 2), rs, rd))
                out.append((1, dx, dy, 0, (8, 2), (0, 2), rs, rd))
                out.append((1, dx, dy, 1, (9, 2), (1, 2), rs, rd))
            else:
                out.append((0, dx, dy, 0, (5, 3), (13, 3), rs, rd))
                out.append((0, dx, dy, 1, (5, 2), (13, 2), rs, rd))
                out.append((1, dx, dy, 0, (8, 2), (16, 2), rs, rd))
                out.append((1, dx, dy, 1, (7, 2), (15, 2), rs, rd))
    return out


def pack_messages():
    out = []
    for dx in (1, -1, 0):
        for dy in (0, 1, -1):
            ps, pd = {0: ((0, 8), (5, 8)), 1: ((3, 5), (0, 5)), -1: ((0, 5), (13, 5))}[dx]
            rs = {0: (0, 8), 1: (3, 5), -1: (0, 5)}[dy]
            out.append((dx, dy, ps, pd, rs))
    return out


def coarse_messages():
    out = []
    for dz in (0, 1):
        for dx in (1, -1, 2, -2, 0):
            for dy in (0, 1, -1):
                if dx == 0 and dy == 0 and dz == 0:
                    continue
                ps, pd = {
                    0: ((5, 4), (5, 4)),
                    1: ((5, 4), (1, 4)),
                    -1: ((5, 4), (9, 4)),
                    2: ((8, 1), (0, 1)),
                    -2: ((5, 1), (13, 1)),
                }[dx]
                rs, rd = {0: ((8, 16), (8, 16)), 1: ((19, 5), (3, 5)), -1: ((8, 5), (24, 5))}[dy]
                out.append((dx, dy, dz, ps, pd, rs, rd))
    return out


MAIN = main_messages()
PACK = pack_messages()
COARSE = coarse_messages()
NM, NP, NC = len(MAIN), len(PACK), len(COARSE)


def ds(pair):
    return pl.ds(pair[0], pair[1])


def up(x):
    return pltpu.roll(x, 127, 1)


def down(x):
    return pltpu.roll(x, 1, 1)


def shifts(vals, lane, circular):
    count = len(vals)
    ups = [up(v) for v in vals]
    downs = [down(v) for v in vals]
    zero = jnp.zeros_like(vals[0])
    plus, minus = [], []
    for t in range(count):
        nxt = ups[(t + 1) % count] if circular or t + 1 < count else zero
        prv = downs[t - 1] if circular or t > 0 else zero
        plus.append(jnp.where(lane == 127, nxt, ups[t]))
        minus.append(jnp.where(lane == 0, prv, downs[t]))
    return plus, minus


def stencil(ref, p, r, tiles, outs, circular, lane, h):
    sf = 1.0 / (h * h)
    bf = 1.0 / h
    centre, parts, mixed = [], [], []
    for t in range(tiles):
        v = ref[p, t, pl.ds(r, 8), :]
        xm = ref[p - 1, t, pl.ds(r, 8), :]
        xp = ref[p + 1, t, pl.ds(r, 8), :]
        ym = ref[p, t, pl.ds(r - 1, 8), :]
        yp = ref[p, t, pl.ds(r + 1, 8), :]
        d = xp - xm
        fy = yp - ym
        centre.append(v)
        mixed.append(d - fy)
        if t in outs:
            dyy = (ref[p + 1, t, pl.ds(r + 1, 8), :] - ref[p - 1, t, pl.ds(r + 1, 8), :]) - (
                ref[p + 1, t, pl.ds(r - 1, 8), :] - ref[p - 1, t, pl.ds(r - 1, 8), :]
            )
            s = (48.0 * sf) * (xp + xm) + (40.0 * sf) * (yp + ym) + (2.0 * sf) * dyy
            b = (1.5 * bf) * d - bf * fy
        else:
            s = b = None
        parts.append((s, b))
    vp, vm = shifts(centre, lane, circular)
    hp, hm = shifts(mixed, lane, circular)
    result = []
    for t in outs:
        s, b = parts[t]
        s = s + (32.0 * sf) * (vp[t] + vm[t]) + (1.5 * sf) * (hp[t] - hm[t])
        b = b + (0.75 * bf) * (vp[t] - vm[t])
        result.append((centre[t], s, b))
    return result


def kernel(g_hbm, c_hbm, sol_hbm, res_hbm, GC, PS, PR, W, A, B, RX, CO, CW, CA, CB, UPS, OUT,
           load_sem, m_send, m_recv, p_send, p_recv, c_send, c_recv, out_sem):
    gx, gy, gz = lax.axis_index("gx"), lax.axis_index("gy"), lax.axis_index("gz")

    def peer(dx, dy, dz):
        return (
            lax.rem(gx + (dx + NXD), NXD),
            lax.rem(gy + (dy + NYD), NYD),
            lax.rem(gz + dz, 2),
        )

    loads = []
    for a, src in ((0, g_hbm), (1, c_hbm)):
        for t in range(2):
            cp = pltpu.make_async_copy(
                src.at[:, :, pl.ds(128 * t, 128)],
                GC.at[a, pl.ds(5, 8), t, pl.ds(8, 32), :],
                load_sem.at[2 * a + t],
            )
            cp.start()
            loads.append(cp)

    barrier = pltpu.get_barrier_semaphore()
    for dx, dy, dz, *_ in COARSE:
        pl.semaphore_signal(barrier, inc=1, device_id=peer(dx, dy, dz), device_id_type=MESH)

    for cp in loads:
        cp.wait()

    lane = lax.broadcasted_iota(jnp.int32, (8, 128), 1)
    sub = lax.broadcasted_iota(jnp.int32, (8, 128), 0)
    zfirst = 120 * gz
    zmask = (lane >= zfirst) & (lane < zfirst + 8)

    def pack_plane(x, _):
        acc = jnp.zeros((8, 128), F32)
        for a in range(2):
            for j in range(4):
                m = 4 * a + j
                t0 = GC[a, 5 + x, 0, pl.ds(8 + 8 * j, 8), :]
                t1 = GC[a, 5 + x, 1, pl.ds(8 + 8 * j, 8), :]
                both = pltpu.roll(jnp.where(lane >= 64, t1, t0), (16 * m + 8) % 128, 1)
                acc = jnp.where((lane >= 16 * m) & (lane < 16 * m + 16), both, acc)
        PS[x] = acc
        return 0

    lax.fori_loop(0, 8, pack_plane, 0)

    row_i = lax.broadcasted_iota(jnp.int32, (256, 128), 0)
    col_i = lax.broadcasted_iota(jnp.int32, (256, 128), 1)
    pool = jnp.where(row_i // 2 == col_i, 0.125, 0.0).astype(F32)

    def coarsen_rows(k):
        pieces = []
        for i in range(4):
            cols = []
            for t in range(2):
                cols.append(RX[i, t, pl.ds(0, 16, stride=2), :] + RX[i, t, pl.ds(1, 16, stride=2), :])
            pieces.append(jnp.concatenate(cols, axis=1))
        allp = jnp.concatenate(pieces, axis=0)
        q = jnp.dot(allp, pool, preferred_element_type=F32, precision=lax.Precision.HIGHEST)
        for i in range(4):
            CO[k, 5 + i, gz, pl.ds(8, 16), :] = q[16 * i : 16 * i + 16]

    def pair_scale(i, _):
        for t in range(2):
            RX[i, t] = GC[1, 5 + 2 * i, t, pl.ds(8, 32), :] + GC[1, 6 + 2 * i, t, pl.ds(8, 32), :]
        return 0

    lax.fori_loop(0, 4, pair_scale, 0)
    coarsen_rows(1)

    pl.semaphore_wait(barrier, NC)

    def main_copy(i):
        _, dx, dy, a, ps, pd, rs, rd = MAIN[i]
        return pltpu.make_async_remote_copy(
            src_ref=GC.at[a, ds(ps), pl.ds(0, 2), ds(rs), :],
            dst_ref=GC.at[a, ds(pd), pl.ds(0, 2), ds(rd), :],
            send_sem=m_send.at[i],
            recv_sem=m_recv.at[i],
            device_id=peer(dx, dy, 0),
            device_id_type=MESH,
        )

    def pack_copy(i):
        dx, dy, ps, pd, rs = PACK[i]
        return pltpu.make_async_remote_copy(
            src_ref=PS.at[ds(ps), ds(rs), :],
            dst_ref=PR.at[1 - dy, ds(pd), ds(rs), :],
            send_sem=p_send.at[i],
            recv_sem=p_recv.at[i],
            device_id=peer(dx, dy, 1),
            device_id_type=MESH,
        )

    def coarse_copy(k, i, arriving=False):
        dx, dy, dz, ps, pd, rs, rd = COARSE[i]
        tile = lax.rem(gz + dz, 2) if arriving else gz
        return pltpu.make_async_remote_copy(
            src_ref=CO.at[k, ds(ps), tile, ds(rs), :],
            dst_ref=CO.at[k, ds(pd), tile, ds(rd), :],
            send_sem=c_send.at[k * NC + i],
            recv_sem=c_recv.at[k * NC + i],
            device_id=peer(dx, dy, dz),
            device_id_type=MESH,
        )

    early = [i for i in range(NM) if MAIN[i][0] == 0]
    late = [i for i in range(NM) if MAIN[i][0] == 1]
    for i in range(NP):
        pack_copy(i).start()
    for i in early:
        main_copy(i).start()
    for i in late:
        main_copy(i).start()
    for i in range(NC):
        coarse_copy(1, i).start()

    for i in range(NP):
        pack_copy(i).wait_recv()
    for i in early:
        main_copy(i).wait_recv()
    for i in late:
        main_copy(i).wait_recv()

    def unpack_plane(p, _):
        for a in range(2):
            for r in range(6):
                slot, j = (0, 3) if r == 0 else (2, 0) if r == 5 else (1, r - 1)
                m = 4 * a + j
                v = pltpu.roll(PR[slot, p], (128 - 16 * m - 8) % 128, 1)
                GC[a, p, 2, pl.ds(8 * r, 8), :] = jnp.where(zmask, v, 0.0)
        return 0

    lax.fori_loop(0, PX, unpack_plane, 0)

    def clear_planes(first):
        def one(p, _):
            GC[0, p] = jnp.zeros((3, ROWS, 128), F32)
            return 0
        lax.fori_loop(first, first + 5, one, 0)

    def clear_rows(first):
        def one(p, _):
            for t in range(3):
                GC[0, p, t, pl.ds(first, 8), :] = jnp.zeros((8, 128), F32)
            return 0
        lax.fori_loop(0, PX, one, 0)

    @pl.when(gx == 0)
    def _():
        clear_planes(0)

    @pl.when(gx == NXD - 1)
    def _():
        clear_planes(13)

    @pl.when(gy == 0)
    def _():
        clear_rows(0)

    @pl.when(gy == NYD - 1)
    def _():
        clear_rows(40)

    starts = [4, 12, 20, 28, 36]
    ylow = (gy * 32 + sub - 4) >= 0
    yhigh = (gy * 32 + sub + 28) < 512

    def weights(p, _):
        place = gx * 8 + p - 5
        scale = jnp.where((place >= 0) & (place < 64), DAMP, 0.0).astype(F32)
        for r in starts:
            for t in range(3):
                w = scale / (1.05 + 240.0 * GC[1, p, t, pl.ds(r, 8), :])
                if r == 4:
                    w = jnp.where(ylow, w, 0.0)
                if r == 36:
                    w = jnp.where(yhigh, w, 0.0)
                if t == 2:
                    w = jnp.where(zmask, w, 0.0)
                W[p, t, pl.ds(r, 8), :] = w
        return 0

    lax.fori_loop(1, 17, weights, 0)

    def fine_sweep(src, dst, low, high, src_index=None):
        view = src if src_index is None else src.at[src_index]

        def one(p, _):
            for r in starts:
                for t, (v, s, b) in enumerate(stencil(view, p, r, 3, (0, 1, 2), True, lane, 1.0)):
                    rows = pl.ds(r, 8)
                    dst[p, t, rows, :] = 0.4 * v + W[p, t, rows, :] * (
                        GC[0, p, t, rows, :] + GC[1, p, t, rows, :] * s + b
                    )
            return 0

        lax.fori_loop(low, high, one, 0)

    def fine_residue(src, p):
        out = []
        for r in (8, 16, 24, 32):
            for t, (v, s, b) in enumerate(stencil(src, p, r, 3, (0, 1), True, lane, 1.0)):
                rows = pl.ds(r, 8)
                out.append(
                    GC[0, p, t, rows, :] - 1.05 * v + GC[1, p, t, rows, :] * (s - 240.0 * v) + b
                )
        return out

    fine_sweep(GC, A, 1, 17, 0)
    fine_sweep(A, B, 2, 16)

    def residue_pair(i, _):
        one = fine_residue(B, 5 + 2 * i)
        two = fine_residue(B, 6 + 2 * i)
        for n in range(8):
            RX[i, n % 2, pl.ds(8 * (n // 2), 8), :] = one[n] + two[n]
        return 0

    lax.fori_loop(0, 4, residue_pair, 0)
    coarsen_rows(0)

    for i in range(NC):
        coarse_copy(0, i).start()

    for i in range(NC):
        coarse_copy(1, i, True).wait_recv()
    for i in range(NC):
        coarse_copy(0, i, True).wait_recv()

    cylow = [(gy * 16 + sub + (r - 8)) >= 0 for r in (0, 24)]
    cyhigh = [(gy * 16 + sub + (r - 8)) < 256 for r in (0, 24)]

    def coarse_weights(p, _):
        place = gx * 4 + p - 5
        scale = jnp.where((place >= 0) & (place < 32), DAMP, 0.0).astype(F32)
        for n, r in enumerate((0, 8, 16, 24)):
            for t in range(2):
                w = scale / (1.05 + 60.0 * CO[1, p, t, pl.ds(r, 8), :])
                if r == 0:
                    w = jnp.where(cylow[0], w, 0.0)
                if r == 24:
                    w = jnp.where(cyhigh[1], w, 0.0)
                CW[p, t, pl.ds(r, 8), :] = w
                CA[p, t, pl.ds(r, 8), :] = w * CO[0, p, t, pl.ds(r, 8), :]
        return 0

    lax.fori_loop(0, CX, coarse_weights, 0)

    def coarse_sweep(src, dst, low, high):
        def one(p, _):
            for r in (4, 12, 20):
                for t, (v, s, b) in enumerate(stencil(src, p, r, 2, (0, 1), False, lane, 2.0)):
                    rows = pl.ds(r, 8)
                    dst[p, t, rows, :] = 0.4 * v + CW[p, t, rows, :] * (
                        CO[0, p, t, rows, :] + CO[1, p, t, rows, :] * s + b
                    )
            return 0

        lax.fori_loop(low, high, one, 0)

    coarse_sweep(CA, CB, 1, 13)
    coarse_sweep(CB, CA, 2, 12)
    coarse_sweep(CA, CB, 3, 11)

    ri = lax.broadcasted_iota(jnp.int32, (128, 256), 0)
    ci = lax.broadcasted_iota(jnp.int32, (128, 256), 1)
    spread = jnp.where(ci // 2 == ri, 1.0, 0.0).astype(F32)
    rh = lax.broadcasted_iota(jnp.int32, (128, 128), 0)
    ch = lax.broadcasted_iota(jnp.int32, (128, 128), 1)
    source = ch // 2 + 64 * gz
    keep = (ch >= zfirst) & (ch < zfirst + 8)
    spread_h = jnp.where((source == rh) & keep, 1.0, 0.0).astype(F32)
    mine = jnp.concatenate([CB[3 + q, gz, pl.ds(4, 24), :] for q in range(8)], axis=0)
    other = jnp.concatenate([CB[3 + q, 1 - gz, pl.ds(4, 24), :] for q in range(8)], axis=0)
    fine = jnp.dot(mine, spread, preferred_element_type=F32, precision=lax.Precision.HIGHEST)
    fine_h = jnp.dot(other, spread_h, preferred_element_type=F32, precision=lax.Precision.HIGHEST)
    for q in range(8):
        for t in range(3):
            part = (fine[24 * q : 24 * q + 24, 128 * t : 128 * t + 128] if t < 2
                    else fine_h[24 * q : 24 * q + 24])
            UPS[q, t, pl.ds(0, 24, stride=2), :] = part
            UPS[q, t, pl.ds(1, 24, stride=2), :] = part

    def add_up(q, _):
        for half in range(2):
            for r in range(6):
                for t in range(3):
                    rows = pl.ds(8 * r, 8)
                    p = 2 * q + 1 + half
                    A[p, t, rows, :] = B[p, t, rows, :] + UPS[q, t, rows, :]
        return 0

    lax.fori_loop(0, 8, add_up, 0)

    fine_sweep(A, B, 3, 15)
    fine_sweep(B, A, 4, 14)

    def finish(x, _):
        vals = fine_residue(A, 5 + x)
        for n in range(8):
            OUT[1, x, n % 2, pl.ds(8 * (n // 2), 8), :] = vals[n]
        for t in range(2):
            OUT[0, x, t] = A[5 + x, t, pl.ds(8, 32), :]
        return 0

    lax.fori_loop(0, 8, finish, 0)
    stores = []
    for a, dst in ((0, sol_hbm), (1, res_hbm)):
        for t in range(2):
            cp = pltpu.make_async_copy(
                OUT.at[a, :, t], dst.at[:, :, pl.ds(128 * t, 128)], out_sem.at[2 * a + t]
            )
            cp.start()
            stores.append(cp)

    for i in range(NM):
        main_copy(i).wait_send()
    for i in range(NP):
        pack_copy(i).wait_send()
    for k in range(2):
        for i in range(NC):
            coarse_copy(k, i).wait_send()
    for cp in stores:
        cp.wait()


def on_device(right_side, volscale):
    shape = jax.ShapeDtypeStruct(right_side.shape, F32)
    fine = pltpu.VMEM((PX, 3, ROWS, 128), F32)
    coarse = pltpu.VMEM((CX, 2, CROWS, 128), F32)
    any_space = pl.BlockSpec(memory_space=pl.ANY)
    return pl.pallas_call(
        kernel,
        out_shape=(shape, shape),
        in_specs=[any_space] * 2,
        out_specs=(any_space, any_space),
        scratch_shapes=[
            pltpu.VMEM((2, PX, 3, ROWS, 128), F32),
            pltpu.VMEM((8, 8, 128), F32),
            pltpu.VMEM((3, PX, 8, 128), F32),
            fine,
            fine,
            fine,
            pltpu.VMEM((4, 2, 32, 128), F32),
            pltpu.VMEM((2, CX, 2, CROWS, 128), F32),
            coarse,
            coarse,
            coarse,
            pltpu.VMEM((8, 3, ROWS, 128), F32),
            pltpu.VMEM((2, 8, 2, 32, 128), F32),
            pltpu.SemaphoreType.DMA((4,)),
            pltpu.SemaphoreType.DMA((NM,)),
            pltpu.SemaphoreType.DMA((NM,)),
            pltpu.SemaphoreType.DMA((NP,)),
            pltpu.SemaphoreType.DMA((NP,)),
            pltpu.SemaphoreType.DMA((2 * NC,)),
            pltpu.SemaphoreType.DMA((2 * NC,)),
            pltpu.SemaphoreType.DMA((4,)),
        ],
        compiler_params=pltpu.CompilerParams(collective_id=0, has_side_effects=True),
    )(right_side, volscale)


def solution(mesh):
    placed = (P("gx", "gy", "gz"), P("gx", "gy", "gz"))
    return jax.shard_map(
        on_device,
        mesh=mesh,
        in_specs=placed,
        out_specs=(P("gx", "gy", "gz"), P("gx", "gy", "gz")),
        check_vma=False,
    )
```

```python
import jax
import jax.numpy as jnp
from jax import lax
from jax.experimental import pallas as pl
from jax.experimental.pallas import tpu as pltpu
from jax.sharding import PartitionSpec as P

MESH = pl.DeviceIdType.MESH
F32 = jnp.float32
NXD, NYD = 8, 16
BX, BY = 8, 32
HALO = 5
PX = BX + 2 * HALO
ROWS = BY + 16
CX = BX // 2 + 2 * HALO
CROWS = BY // 2 + 16
DAMP = 0.6


def main_messages():
    out = []
    for dx in (1, -1, 0):
        for dy in (0, 1, -1):
            if dx == 0 and dy == 0:
                continue
            if dy == 0:
                rs, rd = (8, 32), (8, 32)
            elif dy == 1:
                rs, rd = (35, 5), (3, 5)
            else:
                rs, rd = (8, 5), (40, 5)
            if dx == 0:
                for a in (0, 1):
                    out.append((0, dx, dy, a, (5, 8), (5, 8), rs, rd))
            elif dx == 1:
                out.append((0, dx, dy, 0, (10, 3), (2, 3), rs, rd))
                out.append((0, dx, dy, 1, (11, 2), (3, 2), rs, rd))
                out.append((1, dx, dy, 0, (8, 2), (0, 2), rs, rd))
                out.append((1, dx, dy, 1, (9, 2), (1, 2), rs, rd))
            else:
                out.append((0, dx, dy, 0, (5, 3), (13, 3), rs, rd))
                out.append((0, dx, dy, 1, (5, 2), (13, 2), rs, rd))
                out.append((1, dx, dy, 0, (8, 2), (16, 2), rs, rd))
                out.append((1, dx, dy, 1, (7, 2), (15, 2), rs, rd))
    return out


def pack_messages():
    out = []
    for dx in (1, -1, 0):
        for dy in (0, 1, -1):
            ps, pd = {0: ((0, 8), (5, 8)), 1: ((3, 5), (0, 5)), -1: ((0, 5), (13, 5))}[dx]
            rs = {0: (0, 8), 1: (3, 5), -1: (0, 5)}[dy]
            out.append((dx, dy, ps, pd, rs))
    return out


def coarse_messages():
    out = []
    for dz in (0, 1):
        for dx in (1, -1, 2, -2, 0):
            for dy in (0, 1, -1):
                if dx == 0 and dy == 0 and dz == 0:
                    continue
                ps, pd = {
                    0: ((5, 4), (5, 4)),
                    1: ((5, 4), (1, 4)),
                    -1: ((5, 4), (9, 4)),
                    2: ((8, 1), (0, 1)),
                    -2: ((5, 1), (13, 1)),
                }[dx]
                rs, rd = {0: ((8, 16), (8, 16)), 1: ((19, 5), (3, 5)), -1: ((8, 5), (24, 5))}[dy]
                out.append((dx, dy, dz, ps, pd, rs, rd))
    return out


MAIN = main_messages()
PACK = pack_messages()
COARSE = coarse_messages()
NM, NP, NC = len(MAIN), len(PACK), len(COARSE)


def ds(pair):
    return pl.ds(pair[0], pair[1])


def up(x):
    return pltpu.roll(x, 127, 1)


def down(x):
    return pltpu.roll(x, 1, 1)


def shifts(vals, lane, circular):
    count = len(vals)
    ups = [up(v) for v in vals]
    downs = [down(v) for v in vals]
    zero = jnp.zeros_like(vals[0])
    plus, minus = [], []
    for t in range(count):
        nxt = ups[(t + 1) % count] if circular or t + 1 < count else zero
        prv = downs[t - 1] if circular or t > 0 else zero
        plus.append(jnp.where(lane == 127, nxt, ups[t]))
        minus.append(jnp.where(lane == 0, prv, downs[t]))
    return plus, minus


def stencil(ref, p, r, tiles, outs, circular, lane, h):
    sf = 1.0 / (h * h)
    bf = 1.0 / h
    centre, parts, mixed = [], [], []
    for t in range(tiles):
        v = ref[p, t, pl.ds(r, 8), :]
        xm = ref[p - 1, t, pl.ds(r, 8), :]
        xp = ref[p + 1, t, pl.ds(r, 8), :]
        ym = ref[p, t, pl.ds(r - 1, 8), :]
        yp = ref[p, t, pl.ds(r + 1, 8), :]
        d = xp - xm
        fy = yp - ym
        centre.append(v)
        mixed.append(d - fy)
        if t in outs:
            dyy = (ref[p + 1, t, pl.ds(r + 1, 8), :] - ref[p - 1, t, pl.ds(r + 1, 8), :]) - (
                ref[p + 1, t, pl.ds(r - 1, 8), :] - ref[p - 1, t, pl.ds(r - 1, 8), :]
            )
            s = (48.0 * sf) * (xp + xm) + (40.0 * sf) * (yp + ym) + (2.0 * sf) * dyy
            b = (1.5 * bf) * d - bf * fy
        else:
            s = b = None
        parts.append((s, b))
    vp, vm = shifts(centre, lane, circular)
    hp, hm = shifts(mixed, lane, circular)
    result = []
    for t in outs:
        s, b = parts[t]
        s = s + (32.0 * sf) * (vp[t] + vm[t]) + (1.5 * sf) * (hp[t] - hm[t])
        b = b + (0.75 * bf) * (vp[t] - vm[t])
        result.append((centre[t], s, b))
    return result


def kernel(g_hbm, c_hbm, sol_hbm, res_hbm, GC, PS, PR, W, A, B, RX, CO, CW, CA, CB, UPS, OUT,
           load_sem, m_send, m_recv, p_send, p_recv, c_send, c_recv, out_sem):
    gx, gy, gz = lax.axis_index("gx"), lax.axis_index("gy"), lax.axis_index("gz")

    def peer(dx, dy, dz):
        return (gx + dx, gy + dy, lax.rem(gz + dz, 2))

    def inside(dx, dy):
        tests = []
        if dx > 0:
            tests.append(gx < NXD - dx)
        if dx < 0:
            tests.append(gx >= -dx)
        if dy > 0:
            tests.append(gy < NYD - dy)
        if dy < 0:
            tests.append(gy >= -dy)
        if not tests:
            return None
        return tests[0] if len(tests) == 1 else tests[0] & tests[1]

    def guarded(dx, dy, act):
        test = inside(dx, dy)
        if test is None:
            act()
        else:
            pl.when(test)(act)

    loads = []
    for a, src in ((0, g_hbm), (1, c_hbm)):
        for t in range(2):
            cp = pltpu.make_async_copy(
                src.at[:, :, pl.ds(128 * t, 128)],
                GC.at[a, pl.ds(5, 8), t, pl.ds(8, 32), :],
                load_sem.at[2 * a + t],
            )
            cp.start()
            loads.append(cp)

    barrier = pltpu.get_barrier_semaphore()
    partners = 0
    for dx in (2, 1, 0, -1, -2):
        for dy in (1, 0, -1):

            def greet():
                for dz in (0, 1):
                    if (dx, dy, dz) != (0, 0, 0):
                        pl.semaphore_signal(
                            barrier, inc=1, device_id=peer(dx, dy, dz), device_id_type=MESH
                        )

            guarded(dx, dy, greet)
            test = inside(dx, dy)
            if test is None:
                partners = partners + 1
            else:
                partners = partners + jnp.where(test, 2, 0)

    lane = lax.broadcasted_iota(jnp.int32, (8, 128), 1)
    sub = lax.broadcasted_iota(jnp.int32, (8, 128), 0)
    zfirst = 120 * gz
    zmask = (lane >= zfirst) & (lane < zfirst + 8)
    blank = jnp.zeros((8, 128), F32)

    def clear_fine(low, high, rows):
        def one(p, _):
            for a in range(2):
                for t in range(2):
                    for r in rows:
                        GC[a, p, t, pl.ds(r, 8), :] = blank
            return 0
        lax.fori_loop(low, high, one, 0)

    def clear_pack(slots, low, high):
        def one(p, _):
            for n in slots:
                PR[n, p] = blank
            return 0
        lax.fori_loop(low, high, one, 0)

    def clear_coarse(low, high, rows):
        def one(p, _):
            for k in range(2):
                for t in range(2):
                    for r in rows:
                        CO[k, p, t, pl.ds(r, 8), :] = blank
            return 0
        lax.fori_loop(low, high, one, 0)

    all_rows = (0, 8, 16, 24, 32, 40)

    @pl.when(gx == 0)
    def _():
        clear_fine(0, 5, all_rows)
        clear_pack((0, 1, 2), 0, 5)
        clear_coarse(0, 5, (0, 8, 16, 24))

    @pl.when(gx == 1)
    def _():
        clear_coarse(0, 1, (0, 8, 16, 24))

    @pl.when(gx == NXD - 1)
    def _():
        clear_fine(13, 18, all_rows)
        clear_pack((0, 1, 2), 13, 18)
        clear_coarse(9, 14, (0, 8, 16, 24))

    @pl.when(gx == NXD - 2)
    def _():
        clear_coarse(13, 14, (0, 8, 16, 24))

    @pl.when(gy == 0)
    def _():
        clear_fine(0, 18, (0,))
        clear_pack((0,), 0, 18)
        clear_coarse(0, 14, (0,))

    @pl.when(gy == NYD - 1)
    def _():
        clear_fine(0, 18, (40,))
        clear_pack((2,), 0, 18)
        clear_coarse(0, 14, (24,))

    for cp in loads:
        cp.wait()

    def pack_plane(x, _):
        acc = blank
        for a in range(2):
            for j in range(4):
                m = 4 * a + j
                t0 = GC[a, 5 + x, 0, pl.ds(8 + 8 * j, 8), :]
                t1 = GC[a, 5 + x, 1, pl.ds(8 + 8 * j, 8), :]
                both = pltpu.roll(jnp.where(lane >= 64, t1, t0), (16 * m + 8) % 128, 1)
                acc = jnp.where((lane >= 16 * m) & (lane < 16 * m + 16), both, acc)
        PS[x] = acc
        return 0

    lax.fori_loop(0, 8, pack_plane, 0)

    row_i = lax.broadcasted_iota(jnp.int32, (256, 128), 0)
    col_i = lax.broadcasted_iota(jnp.int32, (256, 128), 1)
    pool = jnp.where(row_i // 2 == col_i, 0.125, 0.0).astype(F32)

    def coarsen_rows(k):
        pieces = []
        for i in range(4):
            cols = []
            for t in range(2):
                cols.append(RX[i, t, pl.ds(0, 16, stride=2), :] + RX[i, t, pl.ds(1, 16, stride=2), :])
            pieces.append(jnp.concatenate(cols, axis=1))
        allp = jnp.concatenate(pieces, axis=0)
        q = jnp.dot(allp, pool, preferred_element_type=F32, precision=lax.Precision.HIGHEST)
        for i in range(4):
            CO[k, 5 + i, gz, pl.ds(8, 16), :] = q[16 * i : 16 * i + 16]

    def pair_scale(i, _):
        for t in range(2):
            RX[i, t] = GC[1, 5 + 2 * i, t, pl.ds(8, 32), :] + GC[1, 6 + 2 * i, t, pl.ds(8, 32), :]
        return 0

    lax.fori_loop(0, 4, pair_scale, 0)
    coarsen_rows(1)

    starts = [4, 12, 20, 28, 36]
    ylow = (gy * 32 + sub - 4) >= 0
    yhigh = (gy * 32 + sub + 28) < 512

    def main_copy(i):
        _, dx, dy, a, ps, pd, rs, rd = MAIN[i]
        return pltpu.make_async_remote_copy(
            src_ref=GC.at[a, ds(ps), pl.ds(0, 2), ds(rs), :],
            dst_ref=GC.at[a, ds(pd), pl.ds(0, 2), ds(rd), :],
            send_sem=m_send.at[i],
            recv_sem=m_recv.at[i],
            device_id=peer(dx, dy, 0),
            device_id_type=MESH,
        )

    def pack_copy(i):
        dx, dy, ps, pd, rs = PACK[i]
        return pltpu.make_async_remote_copy(
            src_ref=PS.at[ds(ps), ds(rs), :],
            dst_ref=PR.at[1 - dy, ds(pd), ds(rs), :],
            send_sem=p_send.at[i],
            recv_sem=p_recv.at[i],
            device_id=peer(dx, dy, 1),
            device_id_type=MESH,
        )

    def coarse_copy(k, i, arriving=False):
        dx, dy, dz, ps, pd, rs, rd = COARSE[i]
        tile = lax.rem(gz + dz, 2) if arriving else gz
        return pltpu.make_async_remote_copy(
            src_ref=CO.at[k, ds(ps), tile, ds(rs), :],
            dst_ref=CO.at[k, ds(pd), tile, ds(rd), :],
            send_sem=c_send.at[k * NC + i],
            recv_sem=c_recv.at[k * NC + i],
            device_id=peer(dx, dy, dz),
            device_id_type=MESH,
        )

    def fine_group(dx, dy, late):
        copies = [main_copy(i) for i in range(NM)
                  if MAIN[i][1:3] == (dx, dy) and MAIN[i][0] == late]
        if not late:
            copies = [pack_copy(i) for i in range(NP) if PACK[i][:2] == (dx, dy)] + copies
        return copies

    def coarse_group(k, dx, dy, arriving=False):
        return [coarse_copy(k, i, arriving) for i in range(NC) if COARSE[i][:2] == (dx, dy)]

    CORNERS = [(1, 1), (1, -1), (-1, 1), (-1, -1)]
    SIDES = [(1, 0), (-1, 0)]
    ROWSIDES = [(0, 1), (0, -1), (0, 0)]
    FAR = [(2, 1), (2, -1), (-2, 1), (-2, -1)] + CORNERS + [(2, 0), (-2, 0)] + SIDES + ROWSIDES

    def send(dx, dy, make):
        def act():
            for cp in make(dx, dy):
                cp.start()
        guarded(dx, dy, act)

    def receive(dx, dy, make):
        def act():
            for cp in make(dx, dy):
                cp.wait_recv()
        guarded(-dx, -dy, act)

    def sent(dx, dy, make):
        def act():
            for cp in make(dx, dy):
                cp.wait_send()
        guarded(dx, dy, act)

    def early_copies(dx, dy):
        return fine_group(dx, dy, 0)

    def late_copies(dx, dy):
        return fine_group(dx, dy, 1)

    def scale_copies(dx, dy):
        return coarse_group(1, dx, dy)

    def rhs_copies(dx, dy):
        return coarse_group(0, dx, dy)

    pl.semaphore_wait(barrier, partners)

    for d in CORNERS + ROWSIDES + SIDES:
        send(*d, early_copies)
    for d in CORNERS + SIDES:
        send(*d, late_copies)
    for d in FAR:
        send(*d, scale_copies)

    def unpack(low, high):
        def unpack_plane(p, _):
            for a in range(2):
                for r in range(6):
                    slot, j = (0, 3) if r == 0 else (2, 0) if r == 5 else (1, r - 1)
                    m = 4 * a + j
                    v = pltpu.roll(PR[slot, p], (128 - 16 * m - 8) % 128, 1)
                    GC[a, p, 2, pl.ds(8 * r, 8), :] = jnp.where(zmask, v, 0.0)
            return 0

        lax.fori_loop(low, high, unpack_plane, 0)

    def weights(low, high):
        def one(p, _):
            place = gx * 8 + p - 5
            scale = jnp.where((place >= 0) & (place < 64), DAMP, 0.0).astype(F32)
            for r in starts:
                for t in range(3):
                    w = scale / (1.05 + 240.0 * GC[1, p, t, pl.ds(r, 8), :])
                    if r == 4:
                        w = jnp.where(ylow, w, 0.0)
                    if r == 36:
                        w = jnp.where(yhigh, w, 0.0)
                    if t == 2:
                        w = jnp.where(zmask, w, 0.0)
                    W[p, t, pl.ds(r, 8), :] = w
            return 0

        lax.fori_loop(low, high, one, 0)

    def fine_plane(view, dst, p):
        for r in starts:
            for t, (v, s, b) in enumerate(stencil(view, p, r, 3, (0, 1, 2), True, lane, 1.0)):
                rows = pl.ds(r, 8)
                dst[p, t, rows, :] = 0.4 * v + W[p, t, rows, :] * (
                    GC[0, p, t, rows, :] + GC[1, p, t, rows, :] * s + b
                )

    def fine_sweep(src, dst, low, high, src_index=None):
        view = src if src_index is None else src.at[src_index]

        def one(p, _):
            fine_plane(view, dst, p)
            return 0

        lax.fori_loop(low, high, one, 0)

    def fine_sides(src, dst, low, high, count, src_index=None):
        view = src if src_index is None else src.at[src_index]

        def one(n, _):
            fine_plane(view, dst, jnp.where(n < count, low + n, high + n - count))
            return 0

        lax.fori_loop(0, 2 * count, one, 0)

    def fine_residue(src, p):
        out = []
        for r in (8, 16, 24, 32):
            for t, (v, s, b) in enumerate(stencil(src, p, r, 3, (0, 1), True, lane, 1.0)):
                rows = pl.ds(r, 8)
                out.append(
                    GC[0, p, t, rows, :] - 1.05 * v + GC[1, p, t, rows, :] * (s - 240.0 * v) + b
                )
        return out

    for d in ROWSIDES:
        receive(*d, early_copies)
    unpack(5, 13)
    weights(5, 13)
    fine_sweep(GC, A, 6, 12, 0)
    fine_sweep(A, B, 7, 11)
    for d in CORNERS + SIDES:
        receive(*d, early_copies)
    unpack(2, 5)
    unpack(13, 16)
    weights(3, 5)
    weights(13, 15)
    fine_sides(GC, A, 3, 12, 3, 0)
    fine_sides(A, B, 4, 11, 3)

    def residue_pair(i, _):
        one = fine_residue(B, 5 + 2 * i)
        two = fine_residue(B, 6 + 2 * i)
        for n in range(8):
            RX[i, n % 2, pl.ds(8 * (n // 2), 8), :] = one[n] + two[n]
        return 0

    lax.fori_loop(0, 4, residue_pair, 0)
    coarsen_rows(0)

    for d in FAR:
        send(*d, rhs_copies)

    for d in CORNERS + SIDES:
        receive(*d, late_copies)
    unpack(0, 2)
    unpack(16, 18)
    weights(1, 3)
    weights(15, 17)
    fine_sides(GC, A, 1, 15, 2, 0)
    fine_sides(A, B, 2, 14, 2)

    cylow = (gy * 16 + sub - 8) >= 0
    cyhigh = (gy * 16 + sub + 16) < 256

    for d in FAR:
        receive(*d, lambda dx, dy: coarse_group(1, dx, dy, True))

    def coarse_weights(p, _):
        place = gx * 4 + p - 5
        scale = jnp.where((place >= 0) & (place < 32), DAMP, 0.0).astype(F32)
        for n, r in enumerate((0, 8, 16, 24)):
            for t in range(2):
                w = scale / (1.05 + 60.0 * CO[1, p, t, pl.ds(r, 8), :])
                if r == 0:
                    w = jnp.where(cylow, w, 0.0)
                if r == 24:
                    w = jnp.where(cyhigh, w, 0.0)
                CW[p, t, pl.ds(r, 8), :] = w
        return 0

    lax.fori_loop(0, CX, coarse_weights, 0)

    for d in FAR:
        receive(*d, lambda dx, dy: coarse_group(0, dx, dy, True))

    def coarse_first(p, _):
        for r in (0, 8, 16, 24):
            for t in range(2):
                rows = pl.ds(r, 8)
                CA[p, t, rows, :] = CW[p, t, rows, :] * CO[0, p, t, rows, :]
        return 0

    lax.fori_loop(0, CX, coarse_first, 0)

    def coarse_sweep(src, dst, low, high):
        def one(p, _):
            for r in (4, 12, 20):
                for t, (v, s, b) in enumerate(stencil(src, p, r, 2, (0, 1), False, lane, 2.0)):
                    rows = pl.ds(r, 8)
                    dst[p, t, rows, :] = 0.4 * v + CW[p, t, rows, :] * (
                        CO[0, p, t, rows, :] + CO[1, p, t, rows, :] * s + b
                    )
            return 0

        lax.fori_loop(low, high, one, 0)

    coarse_sweep(CA, CB, 1, 13)
    coarse_sweep(CB, CA, 2, 12)
    coarse_sweep(CA, CB, 3, 11)

    ri = lax.broadcasted_iota(jnp.int32, (128, 256), 0)
    ci = lax.broadcasted_iota(jnp.int32, (128, 256), 1)
    spread = jnp.where(ci // 2 == ri, 1.0, 0.0).astype(F32)
    rh = lax.broadcasted_iota(jnp.int32, (128, 128), 0)
    ch = lax.broadcasted_iota(jnp.int32, (128, 128), 1)
    source = ch // 2 + 64 * gz
    keep = (ch >= zfirst) & (ch < zfirst + 8)
    spread_h = jnp.where((source == rh) & keep, 1.0, 0.0).astype(F32)
    mine = jnp.concatenate([CB[3 + q, gz, pl.ds(4, 24), :] for q in range(8)], axis=0)
    other = jnp.concatenate([CB[3 + q, 1 - gz, pl.ds(4, 24), :] for q in range(8)], axis=0)
    fine = jnp.dot(mine, spread, preferred_element_type=F32, precision=lax.Precision.HIGHEST)
    fine_h = jnp.dot(other, spread_h, preferred_element_type=F32, precision=lax.Precision.HIGHEST)
    for q in range(8):
        for t in range(3):
            part = (fine[24 * q : 24 * q + 24, 128 * t : 128 * t + 128] if t < 2
                    else fine_h[24 * q : 24 * q + 24])
            UPS[q, t, pl.ds(0, 24, stride=2), :] = part
            UPS[q, t, pl.ds(1, 24, stride=2), :] = part

    def add_up(q, _):
        for half in range(2):
            for r in range(6):
                for t in range(3):
                    rows = pl.ds(8 * r, 8)
                    p = 2 * q + 1 + half
                    A[p, t, rows, :] = B[p, t, rows, :] + UPS[q, t, rows, :]
        return 0

    lax.fori_loop(0, 8, add_up, 0)

    fine_sweep(A, B, 3, 15)
    fine_sweep(B, A, 4, 14)

    stores = []

    def store(a, dst):
        for t in range(2):
            src = OUT.at[:, t] if a else A.at[pl.ds(5, 8), t, pl.ds(8, 32), :]
            cp = pltpu.make_async_copy(src, dst.at[:, :, pl.ds(128 * t, 128)], out_sem.at[2 * a + t])
            cp.start()
            stores.append(cp)

    store(0, sol_hbm)

    def finish(x, _):
        vals = fine_residue(A, 5 + x)
        for n in range(8):
            OUT[x, n % 2, pl.ds(8 * (n // 2), 8), :] = vals[n]
        return 0

    lax.fori_loop(0, 8, finish, 0)
    store(1, res_hbm)

    for d in CORNERS + ROWSIDES + SIDES:
        sent(*d, early_copies)
    for d in CORNERS + SIDES:
        sent(*d, late_copies)
    for d in FAR:
        sent(*d, scale_copies)
        sent(*d, rhs_copies)
    for cp in stores:
        cp.wait()


def on_device(right_side, volscale):
    shape = jax.ShapeDtypeStruct(right_side.shape, F32)
    fine = pltpu.VMEM((PX, 3, ROWS, 128), F32)
    coarse = pltpu.VMEM((CX, 2, CROWS, 128), F32)
    any_space = pl.BlockSpec(memory_space=pl.ANY)
    return pl.pallas_call(
        kernel,
        out_shape=(shape, shape),
        in_specs=[any_space] * 2,
        out_specs=(any_space, any_space),
        scratch_shapes=[
            pltpu.VMEM((2, PX, 3, ROWS, 128), F32),
            pltpu.VMEM((8, 8, 128), F32),
            pltpu.VMEM((3, PX, 8, 128), F32),
            fine,
            fine,
            fine,
            pltpu.VMEM((4, 2, 32, 128), F32),
            pltpu.VMEM((2, CX, 2, CROWS, 128), F32),
            coarse,
            coarse,
            coarse,
            pltpu.VMEM((8, 3, ROWS, 128), F32),
            pltpu.VMEM((8, 2, 32, 128), F32),
            pltpu.SemaphoreType.DMA((4,)),
            pltpu.SemaphoreType.DMA((NM,)),
            pltpu.SemaphoreType.DMA((NM,)),
            pltpu.SemaphoreType.DMA((NP,)),
            pltpu.SemaphoreType.DMA((NP,)),
            pltpu.SemaphoreType.DMA((2 * NC,)),
            pltpu.SemaphoreType.DMA((2 * NC,)),
            pltpu.SemaphoreType.DMA((4,)),
        ],
        compiler_params=pltpu.CompilerParams(collective_id=0, has_side_effects=True),
    )(right_side, volscale)


def solution(mesh):
    placed = (P("gx", "gy", "gz"), P("gx", "gy", "gz"))
    return jax.shard_map(
        on_device,
        mesh=mesh,
        in_specs=placed,
        out_specs=(P("gx", "gy", "gz"), P("gx", "gy", "gz")),
        check_vma=False,
    )
```

```python
import jax
import jax.numpy as jnp
from jax import lax
from jax.experimental import pallas as pl
from jax.experimental.pallas import tpu as pltpu
from jax.sharding import PartitionSpec as P

MESH = pl.DeviceIdType.MESH
F32 = jnp.float32
NXD, NYD = 8, 16
BX, BY = 8, 32
HALO = 5
PX = BX + 2 * HALO
ROWS = BY + 16
CX = BX // 2 + 2 * HALO
CROWS = BY // 2 + 16
DAMP = 0.6


def fine_messages():
    out = [("z", 0, 0, 1, ("PS",), ("PR", 1, (5, 8), (0, 8)))]
    lo, mid, hi = (3, 5), (8, 32), (40, 5)
    for dx in (1, -1):
        sg, dg = ((10, 3), (2, 3)) if dx == 1 else ((5, 3), (13, 3))
        sc, dc = ((11, 2), (3, 2)) if dx == 1 else ((5, 2), (13, 2))
        out.append(("x", dx, 0, 0, ("GC", 0, sg, mid), ("GC", 0, dg, mid)))
        out.append(("x", dx, 0, 0, ("GC", 1, sc, mid), ("GC", 1, dc, mid)))
        for rows in (lo, hi):
            out.append(("xc", dx, 0, 0, ("GC", 0, sg, rows), ("GC", 0, dg, rows)))
            out.append(("xc", dx, 0, 0, ("GC", 1, sc, rows), ("GC", 1, dc, rows)))
        out.append(("xc", dx, 0, 0, ("PA", sg), ("PA", dg)))
        sg, dg = ((8, 2), (0, 2)) if dx == 1 else ((8, 2), (16, 2))
        sc, dc = ((9, 2), (1, 2)) if dx == 1 else ((7, 2), (15, 2))
        out.append(("xl", dx, 0, 0, ("GC", 0, sg, (3, 42)), ("GC", 0, dg, (3, 42))))
        out.append(("xl", dx, 0, 0, ("GC", 1, sc, (3, 42)), ("GC", 1, dc, (3, 42))))
        out.append(("xl", dx, 0, 0, ("PA", sg), ("PA", dg)))
    for dy in (1, -1):
        rs, rd, pr = ((35, 5), lo, (3, 5)) if dy == 1 else ((8, 5), hi, (0, 5))
        out.append(("y", 0, dy, 0, ("GC", 0, (5, 8), rs), ("GC", 0, (5, 8), rd)))
        out.append(("y", 0, dy, 0, ("GC", 1, (5, 8), rs), ("GC", 1, (5, 8), rd)))
        out.append(("yz", 0, dy, 0, ("PR", 1, (5, 8), pr), ("PR", 1 - dy, (5, 8), pr)))
    return out


def coarse_messages():
    out = []
    for dx in (2, 1, 0, -1, -2):
        for dy in (1, 0, -1):
            ps, pd = {
                0: ((5, 4), (5, 4)),
                1: ((5, 4), (1, 4)),
                -1: ((5, 4), (9, 4)),
                2: ((8, 1), (0, 1)),
                -2: ((5, 1), (13, 1)),
            }[dx]
            rs, rd = {0: ((8, 16), (8, 16)), 1: ((19, 5), (3, 5)), -1: ((8, 5), (24, 5))}[dy]
            if (dx, dy) != (0, 0):
                out.append((dx, dy, 0, ps, pd, rs, rd))
            out.append((dx, dy, 1, None, None, {0: (0, 8), 1: (3, 5), -1: (0, 5)}[dy], None))
    return out


FINE = fine_messages()
COARSE = coarse_messages()
NF, NC = len(FINE), len(COARSE)


def ds(pair):
    return pl.ds(pair[0], pair[1])


def up(x):
    return pltpu.roll(x, 127, 1)


def down(x):
    return pltpu.roll(x, 1, 1)


def shifts(vals, lane, circular):
    count = len(vals)
    ups = [up(v) for v in vals]
    downs = [down(v) for v in vals]
    zero = jnp.zeros_like(vals[0])
    plus, minus = [], []
    for t in range(count):
        nxt = ups[(t + 1) % count] if circular or t + 1 < count else zero
        prv = downs[t - 1] if circular or t > 0 else zero
        plus.append(jnp.where(lane == 127, nxt, ups[t]))
        minus.append(jnp.where(lane == 0, prv, downs[t]))
    return plus, minus


def stencil(ref, p, r, tiles, outs, circular, lane, h):
    sf = 1.0 / (h * h)
    bf = 1.0 / h
    centre, parts, mixed = [], [], []
    for t in range(tiles):
        v = ref[p, t, pl.ds(r, 8), :]
        xm = ref[p - 1, t, pl.ds(r, 8), :]
        xp = ref[p + 1, t, pl.ds(r, 8), :]
        ym = ref[p, t, pl.ds(r - 1, 8), :]
        yp = ref[p, t, pl.ds(r + 1, 8), :]
        d = xp - xm
        fy = yp - ym
        centre.append(v)
        mixed.append(d - fy)
        if t in outs:
            dyy = (ref[p + 1, t, pl.ds(r + 1, 8), :] - ref[p - 1, t, pl.ds(r + 1, 8), :]) - (
                ref[p + 1, t, pl.ds(r - 1, 8), :] - ref[p - 1, t, pl.ds(r - 1, 8), :]
            )
            s = (48.0 * sf) * (xp + xm) + (40.0 * sf) * (yp + ym) + (2.0 * sf) * dyy
            b = (1.5 * bf) * d - bf * fy
        else:
            s = b = None
        parts.append((s, b))
    vp, vm = shifts(centre, lane, circular)
    hp, hm = shifts(mixed, lane, circular)
    result = []
    for t in outs:
        s, b = parts[t]
        s = s + (32.0 * sf) * (vp[t] + vm[t]) + (1.5 * sf) * (hp[t] - hm[t])
        b = b + (0.75 * bf) * (vp[t] - vm[t])
        result.append((centre[t], s, b))
    return result


def kernel(g_hbm, c_hbm, sol_hbm, res_hbm, GC, PS, PR, W, A, B, RX, CO, QS, QR, CW, CA, CB, UPS,
           OUT, load_sem, f_send, f_recv, c_send, c_recv, out_sem):
    gx, gy, gz = lax.axis_index("gx"), lax.axis_index("gy"), lax.axis_index("gz")

    def peer(dx, dy, dz):
        return (gx + dx, gy + dy, lax.rem(gz + dz, 2))

    def inside(dx, dy):
        tests = []
        if dx > 0:
            tests.append(gx < NXD - dx)
        if dx < 0:
            tests.append(gx >= -dx)
        if dy > 0:
            tests.append(gy < NYD - dy)
        if dy < 0:
            tests.append(gy >= -dy)
        if not tests:
            return None
        return tests[0] if len(tests) == 1 else tests[0] & tests[1]

    def guarded(dx, dy, act):
        test = inside(dx, dy)
        if test is None:
            act()
        else:
            pl.when(test)(act)

    loads = []
    for a, src in ((0, g_hbm), (1, c_hbm)):
        for t in range(2):
            cp = pltpu.make_async_copy(
                src.at[:, :, pl.ds(128 * t, 128)],
                GC.at[a, pl.ds(5, 8), t, pl.ds(8, 32), :],
                load_sem.at[2 * a + t],
            )
            cp.start()
            loads.append(cp)

    barrier = pltpu.get_barrier_semaphore()
    partners = 1
    for dx, dy, dz in ((1, 0, 0), (-1, 0, 0), (0, 1, 0), (0, -1, 0), (0, 0, 1)):

        def greet():
            pl.semaphore_signal(barrier, inc=1, device_id=peer(dx, dy, dz), device_id_type=MESH)

        guarded(dx, dy, greet)
        if not dz:
            partners = partners + jnp.where(inside(dx, dy), 1, 0)

    lane = lax.broadcasted_iota(jnp.int32, (8, 128), 1)
    sub = lax.broadcasted_iota(jnp.int32, (8, 128), 0)
    zfirst = 120 * gz
    zmask = (lane >= zfirst) & (lane < zfirst + 8)
    blank = jnp.zeros((8, 128), F32)

    def clear_fine(low, high, rows):
        def one(p, _):
            for a in range(2):
                for t in range(2):
                    for r in rows:
                        GC[a, p, t, pl.ds(r, 8), :] = blank
            return 0
        lax.fori_loop(low, high, one, 0)

    def clear_pack(slots, low, high):
        def one(p, _):
            for n in slots:
                PR[n, p] = blank
            return 0
        lax.fori_loop(low, high, one, 0)

    def clear_coarse(low, high, rows):
        def one(p, _):
            for k in range(2):
                for r in rows:
                    CO[k, p, 0, pl.ds(r, 8), :] = blank
            return 0
        lax.fori_loop(low, high, one, 0)

    all_rows = (0, 8, 16, 24, 32, 40)

    def clear_edge(cols, rows):
        for k in range(2):
            for n in cols:
                for m in rows:
                    QR[k, n, m] = blank

    @pl.when(gx == 0)
    def _():
        clear_fine(0, 5, all_rows)
        clear_pack((0, 1, 2), 0, 5)
        clear_coarse(0, 5, (0, 8, 16, 24))
        clear_edge((0, 1), (0, 1, 2))

    @pl.when(gx == 1)
    def _():
        clear_coarse(0, 1, (0, 8, 16, 24))
        clear_edge((0,), (0, 1, 2))

    @pl.when(gx == NXD - 1)
    def _():
        clear_fine(13, 18, all_rows)
        clear_pack((0, 1, 2), 13, 18)
        clear_coarse(9, 14, (0, 8, 16, 24))
        clear_edge((3, 4), (0, 1, 2))

    @pl.when(gx == NXD - 2)
    def _():
        clear_coarse(13, 14, (0, 8, 16, 24))
        clear_edge((4,), (0, 1, 2))

    @pl.when(gy == 0)
    def _():
        clear_fine(5, 13, (0,))
        clear_pack((0,), 5, 13)
        clear_coarse(0, 14, (0,))
        clear_edge((0, 1, 2, 3, 4), (0,))

    @pl.when(gy == NYD - 1)
    def _():
        clear_fine(5, 13, (40,))
        clear_pack((2,), 5, 13)
        clear_coarse(0, 14, (24,))
        clear_edge((0, 1, 2, 3, 4), (2,))

    for cp in loads:
        cp.wait()

    def pack_plane(x, _):
        acc = blank
        for a in range(2):
            for j in range(4):
                m = 4 * a + j
                t0 = GC[a, 5 + x, 0, pl.ds(8 + 8 * j, 8), :]
                t1 = GC[a, 5 + x, 1, pl.ds(8 + 8 * j, 8), :]
                both = pltpu.roll(jnp.where(lane >= 64, t1, t0), (16 * m + 8) % 128, 1)
                acc = jnp.where((lane >= 16 * m) & (lane < 16 * m + 16), both, acc)
        PS[x] = acc
        return 0

    lax.fori_loop(0, 8, pack_plane, 0)

    row_i = lax.broadcasted_iota(jnp.int32, (256, 128), 0)
    col_i = lax.broadcasted_iota(jnp.int32, (256, 128), 1)
    pool = jnp.where(row_i // 2 == col_i, 0.125, 0.0).astype(F32)

    def coarsen_rows(k):
        pieces = []
        for i in range(4):
            cols = []
            for t in range(2):
                cols.append(RX[i, t, pl.ds(0, 16, stride=2), :] + RX[i, t, pl.ds(1, 16, stride=2), :])
            pieces.append(jnp.concatenate(cols, axis=1))
        allp = jnp.concatenate(pieces, axis=0)
        q = jnp.dot(allp, pool, preferred_element_type=F32, precision=lax.Precision.HIGHEST)
        acc = blank
        for i in range(4):
            CO[k, 5 + i, 0, pl.ds(8, 16), :] = q[16 * i : 16 * i + 16]
            for j in range(2):
                m = 2 * i + j
                turned = pltpu.roll(q[8 * m : 8 * m + 8], (16 * m + 8) % 128, 1)
                acc = jnp.where((lane >= 16 * m) & (lane < 16 * m + 16), turned, acc)
        QS[k] = acc

    def pair_scale(i, _):
        for t in range(2):
            RX[i, t] = GC[1, 5 + 2 * i, t, pl.ds(8, 32), :] + GC[1, 6 + 2 * i, t, pl.ds(8, 32), :]
        return 0

    lax.fori_loop(0, 4, pair_scale, 0)
    coarsen_rows(1)

    starts = [4, 12, 20, 28, 36]
    ylow = (gy * 32 + sub - 4) >= 0
    yhigh = (gy * 32 + sub + 28) < 512

    def place(where):
        if where[0] == "PS":
            return PS
        if where[0] == "PR":
            return PR.at[where[1], ds(where[2]), ds(where[3]), :]
        if where[0] == "PA":
            return PR.at[:, ds(where[1])]
        return GC.at[where[1], ds(where[2]), pl.ds(0, 2), ds(where[3]), :]

    def fine_copy(i):
        _, dx, dy, dz, src, dst = FINE[i]
        return pltpu.make_async_remote_copy(
            src_ref=place(src),
            dst_ref=place(dst),
            send_sem=f_send.at[i],
            recv_sem=f_recv.at[i],
            device_id=peer(dx, dy, dz),
            device_id_type=MESH,
        )

    def coarse_copy(k, i):
        dx, dy, dz, ps, pd, rs, rd = COARSE[i]
        if dz:
            src, dst = QS.at[k, ds(rs), :], QR.at[k, 2 - dx, 1 - dy, ds(rs), :]
        else:
            src, dst = CO.at[k, ds(ps), 0, ds(rs), :], CO.at[k, ds(pd), 0, ds(rd), :]
        return pltpu.make_async_remote_copy(
            src_ref=src,
            dst_ref=dst,
            send_sem=c_send.at[k * NC + i],
            recv_sem=c_recv.at[k * NC + i],
            device_id=peer(dx, dy, dz),
            device_id_type=MESH,
        )

    FAR = [(2, 1), (2, -1), (-2, 1), (-2, -1), (1, 1), (1, -1), (-1, 1), (-1, -1),
           (2, 0), (-2, 0), (1, 0), (-1, 0), (0, 1), (0, -1), (0, 0)]
    NEAR = [(1, 0), (-1, 0), (0, 1), (0, -1), (0, 0)]

    def run(direction, copies, method, back):
        if copies:
            dx, dy = direction
            def act():
                for cp in copies:
                    getattr(cp, method)()
            guarded(-dx if back else dx, -dy if back else dy, act)

    def fine(phase, method):
        for d in NEAR:
            run(d, [fine_copy(i) for i in range(NF) if FINE[i][0] in phase and FINE[i][1:3] == d],
                method, method == "wait_recv")

    def coarse(k, method):
        for d in FAR:
            run(d, [coarse_copy(k, i) for i in range(NC) if COARSE[i][:2] == d],
                method, method == "wait_recv")

    pl.semaphore_wait(barrier, partners)

    fine(("z",), "start")
    fine(("x", "y"), "start")

    def unpack(low, high):
        def unpack_plane(p, _):
            for a in range(2):
                for r in range(6):
                    slot, j = (0, 3) if r == 0 else (2, 0) if r == 5 else (1, r - 1)
                    m = 4 * a + j
                    v = pltpu.roll(PR[slot, p], (128 - 16 * m - 8) % 128, 1)
                    GC[a, p, 2, pl.ds(8 * r, 8), :] = jnp.where(zmask, v, 0.0)
            return 0

        lax.fori_loop(low, high, unpack_plane, 0)

    def weights(low, high):
        def one(p, _):
            at = gx * 8 + p - 5
            scale = jnp.where((at >= 0) & (at < 64), DAMP, 0.0).astype(F32)
            for r in starts:
                for t in range(3):
                    w = scale / (1.05 + 240.0 * GC[1, p, t, pl.ds(r, 8), :])
                    if r == 4:
                        w = jnp.where(ylow, w, 0.0)
                    if r == 36:
                        w = jnp.where(yhigh, w, 0.0)
                    if t == 2:
                        w = jnp.where(zmask, w, 0.0)
                    W[p, t, pl.ds(r, 8), :] = w
            return 0

        lax.fori_loop(low, high, one, 0)

    def fine_plane(view, dst, p):
        for r in starts:
            for t, (v, s, b) in enumerate(stencil(view, p, r, 3, (0, 1, 2), True, lane, 1.0)):
                rows = pl.ds(r, 8)
                dst[p, t, rows, :] = 0.4 * v + W[p, t, rows, :] * (
                    GC[0, p, t, rows, :] + GC[1, p, t, rows, :] * s + b
                )

    def fine_sweep(src, dst, low, high, src_index=None):
        view = src if src_index is None else src.at[src_index]

        def one(p, _):
            fine_plane(view, dst, p)
            return 0

        lax.fori_loop(low, high, one, 0)

    def fine_sides(src, dst, low, high, count, src_index=None):
        view = src if src_index is None else src.at[src_index]

        def one(n, _):
            fine_plane(view, dst, jnp.where(n < count, low + n, high + n - count))
            return 0

        lax.fori_loop(0, 2 * count, one, 0)

    def fine_residue(src, p):
        out = []
        for r in (8, 16, 24, 32):
            for t, (v, s, b) in enumerate(stencil(src, p, r, 3, (0, 1), True, lane, 1.0)):
                rows = pl.ds(r, 8)
                out.append(
                    GC[0, p, t, rows, :] - 1.05 * v + GC[1, p, t, rows, :] * (s - 240.0 * v) + b
                )
        return out

    fine(("z",), "wait_recv")
    fine(("yz",), "start")
    fine(("y", "yz"), "wait_recv")
    fine(("xc",), "start")
    fine(("xl",), "start")
    unpack(5, 13)
    weights(5, 13)
    fine_sweep(GC, A, 6, 12, 0)
    fine_sweep(A, B, 7, 11)
    fine(("x", "xc"), "wait_recv")
    coarse(1, "start")
    unpack(2, 5)
    unpack(13, 16)
    weights(3, 5)
    weights(13, 15)
    fine_sides(GC, A, 3, 12, 3, 0)
    fine_sides(A, B, 4, 11, 3)

    def residue_pair(i, _):
        one = fine_residue(B, 5 + 2 * i)
        two = fine_residue(B, 6 + 2 * i)
        for n in range(8):
            RX[i, n % 2, pl.ds(8 * (n // 2), 8), :] = one[n] + two[n]
        return 0

    lax.fori_loop(0, 4, residue_pair, 0)
    coarsen_rows(0)

    coarse(0, "start")

    fine(("xl",), "wait_recv")
    unpack(0, 2)
    unpack(16, 18)
    weights(1, 3)
    weights(15, 17)
    fine_sides(GC, A, 1, 15, 2, 0)
    fine_sides(A, B, 2, 14, 2)

    cylow = (gy * 16 + sub - 8) >= 0
    cyhigh = (gy * 16 + sub + 16) < 256

    coarse(1, "wait_recv")

    def coarse_unpack(k):
        for p in range(CX):
            col, i = [(0, 3), (1, 0), (1, 1), (1, 2), (1, 3), (2, 0), (2, 1), (2, 2), (2, 3),
                      (3, 0), (3, 1), (3, 2), (3, 3), (4, 0)][p]
            for r, (row, j) in enumerate(((0, 1), (1, 0), (1, 1), (2, 0))):
                m = 2 * i + j
                turned = pltpu.roll(QR[k, col, row], (128 - 16 * m - 8) % 128, 1)
                CO[k, p, 1, pl.ds(8 * r, 8), :] = jnp.where(zmask, turned, 0.0)

    coarse_unpack(1)

    def coarse_weights(p, _):
        at = gx * 4 + p - 5
        scale = jnp.where((at >= 0) & (at < 32), DAMP, 0.0).astype(F32)
        for n, r in enumerate((0, 8, 16, 24)):
            for t in range(2):
                w = scale / (1.05 + 60.0 * CO[1, p, t, pl.ds(r, 8), :])
                if r == 0:
                    w = jnp.where(cylow, w, 0.0)
                if r == 24:
                    w = jnp.where(cyhigh, w, 0.0)
                if t == 1:
                    w = jnp.where(zmask, w, 0.0)
                CW[p, t, pl.ds(r, 8), :] = w
        return 0

    lax.fori_loop(0, CX, coarse_weights, 0)

    coarse(0, "wait_recv")
    coarse_unpack(0)

    def coarse_first(p, _):
        for r in (0, 8, 16, 24):
            for t in range(2):
                rows = pl.ds(r, 8)
                CA[p, t, rows, :] = CW[p, t, rows, :] * CO[0, p, t, rows, :]
        return 0

    lax.fori_loop(0, CX, coarse_first, 0)

    def coarse_sweep(src, dst, low, high):
        def one(p, _):
            for r in (4, 12, 20):
                for t, (v, s, b) in enumerate(stencil(src, p, r, 2, (0, 1), True, lane, 2.0)):
                    rows = pl.ds(r, 8)
                    dst[p, t, rows, :] = 0.4 * v + CW[p, t, rows, :] * (
                        CO[0, p, t, rows, :] + CO[1, p, t, rows, :] * s + b
                    )
            return 0

        lax.fori_loop(low, high, one, 0)

    coarse_sweep(CA, CB, 1, 13)
    coarse_sweep(CB, CA, 2, 12)
    coarse_sweep(CA, CB, 3, 11)

    ri = lax.broadcasted_iota(jnp.int32, (128, 256), 0)
    ci = lax.broadcasted_iota(jnp.int32, (128, 256), 1)
    spread = jnp.where(ci // 2 == ri, 1.0, 0.0).astype(F32)
    rh = lax.broadcasted_iota(jnp.int32, (128, 128), 0)
    ch = lax.broadcasted_iota(jnp.int32, (128, 128), 1)
    source = ch // 2 + 64 * gz
    keep = (ch >= zfirst) & (ch < zfirst + 8)
    spread_h = jnp.where((source == rh) & keep, 1.0, 0.0).astype(F32)
    mine = jnp.concatenate([CB[3 + q, 0, pl.ds(4, 24), :] for q in range(8)], axis=0)
    other = jnp.concatenate([CB[3 + q, 1, pl.ds(4, 24), :] for q in range(8)], axis=0)
    wide = jnp.dot(mine, spread, preferred_element_type=F32, precision=lax.Precision.HIGHEST)
    wide_h = jnp.dot(other, spread_h, preferred_element_type=F32, precision=lax.Precision.HIGHEST)
    for q in range(8):
        for t in range(3):
            part = (wide[24 * q : 24 * q + 24, 128 * t : 128 * t + 128] if t < 2
                    else wide_h[24 * q : 24 * q + 24])
            UPS[q, t, pl.ds(0, 24, stride=2), :] = part
            UPS[q, t, pl.ds(1, 24, stride=2), :] = part

    def add_up(q, _):
        for half in range(2):
            for r in range(6):
                for t in range(3):
                    rows = pl.ds(8 * r, 8)
                    p = 2 * q + 1 + half
                    A[p, t, rows, :] = B[p, t, rows, :] + UPS[q, t, rows, :]
        return 0

    lax.fori_loop(0, 8, add_up, 0)

    fine_sweep(A, B, 3, 15)
    fine_sweep(B, A, 4, 14)

    stores = []

    def store(a, dst):
        for t in range(2):
            src = OUT.at[:, t] if a else A.at[pl.ds(5, 8), t, pl.ds(8, 32), :]
            cp = pltpu.make_async_copy(src, dst.at[:, :, pl.ds(128 * t, 128)], out_sem.at[2 * a + t])
            cp.start()
            stores.append(cp)

    store(0, sol_hbm)

    def finish(x, _):
        vals = fine_residue(A, 5 + x)
        for n in range(8):
            OUT[x, n % 2, pl.ds(8 * (n // 2), 8), :] = vals[n]
        return 0

    lax.fori_loop(0, 8, finish, 0)
    store(1, res_hbm)

    fine(("z", "x", "y", "yz", "xc", "xl"), "wait_send")
    coarse(1, "wait_send")
    coarse(0, "wait_send")
    for cp in stores:
        cp.wait()


def on_device(right_side, volscale):
    shape = jax.ShapeDtypeStruct(right_side.shape, F32)
    fine = pltpu.VMEM((PX, 3, ROWS, 128), F32)
    coarse = pltpu.VMEM((CX, 2, CROWS, 128), F32)
    any_space = pl.BlockSpec(memory_space=pl.ANY)
    return pl.pallas_call(
        kernel,
        out_shape=(shape, shape),
        in_specs=[any_space] * 2,
        out_specs=(any_space, any_space),
        scratch_shapes=[
            pltpu.VMEM((2, PX, 3, ROWS, 128), F32),
            pltpu.VMEM((8, 8, 128), F32),
            pltpu.VMEM((3, PX, 8, 128), F32),
            fine,
            fine,
            fine,
            pltpu.VMEM((4, 2, 32, 128), F32),
            pltpu.VMEM((2, CX, 2, CROWS, 128), F32),
            pltpu.VMEM((2, 8, 128), F32),
            pltpu.VMEM((2, 5, 3, 8, 128), F32),
            coarse,
            coarse,
            coarse,
            pltpu.VMEM((8, 3, ROWS, 128), F32),
            pltpu.VMEM((8, 2, 32, 128), F32),
            pltpu.SemaphoreType.DMA((4,)),
            pltpu.SemaphoreType.DMA((NF,)),
            pltpu.SemaphoreType.DMA((NF,)),
            pltpu.SemaphoreType.DMA((2 * NC,)),
            pltpu.SemaphoreType.DMA((2 * NC,)),
            pltpu.SemaphoreType.DMA((4,)),
        ],
        compiler_params=pltpu.CompilerParams(collective_id=0, has_side_effects=True),
    )(right_side, volscale)


def solution(mesh):
    placed = (P("gx", "gy", "gz"), P("gx", "gy", "gz"))
    return jax.shard_map(
        on_device,
        mesh=mesh,
        in_specs=placed,
        out_specs=(P("gx", "gy", "gz"), P("gx", "gy", "gz")),
        check_vma=False,
    )
```

```python
import jax
import jax.numpy as jnp
from jax import lax
from jax.experimental import pallas as pl
from jax.experimental.pallas import tpu as pltpu
from jax.sharding import PartitionSpec as P

MESH = pl.DeviceIdType.MESH
F32 = jnp.float32
NXD, NYD = 8, 16
BX, BY = 8, 32
HALO = 5
PX = BX + 2 * HALO
ROWS = BY + 16
CX = BX // 2 + 2 * HALO
CROWS = BY // 2 + 16
DAMP = 0.6


def fine_messages():
    out = [("z", 0, 0, 1, ("PS",), ("PR", 1, (5, 8), (0, 8)))]
    lo, mid, hi = (3, 5), (8, 32), (40, 5)
    for dx in (1, -1):
        sg, dg = ((10, 3), (2, 3)) if dx == 1 else ((5, 3), (13, 3))
        sc, dc = ((11, 2), (3, 2)) if dx == 1 else ((5, 2), (13, 2))
        out.append(("x", dx, 0, 0, ("GC", 0, sg, mid), ("GC", 0, dg, mid)))
        out.append(("x", dx, 0, 0, ("GC", 1, sc, mid), ("GC", 1, dc, mid)))
        for rows in (lo, hi):
            out.append(("xc", dx, 0, 0, ("GC", 0, sg, rows), ("GC", 0, dg, rows)))
            out.append(("xc", dx, 0, 0, ("GC", 1, sc, rows), ("GC", 1, dc, rows)))
        out.append(("xc", dx, 0, 0, ("PA", sg), ("PA", dg)))
        sg, dg = ((8, 2), (0, 2)) if dx == 1 else ((8, 2), (16, 2))
        sc, dc = ((9, 2), (1, 2)) if dx == 1 else ((7, 2), (15, 2))
        out.append(("xl", dx, 0, 0, ("GC", 0, sg, (3, 42)), ("GC", 0, dg, (3, 42))))
        out.append(("xl", dx, 0, 0, ("GC", 1, sc, (3, 42)), ("GC", 1, dc, (3, 42))))
        out.append(("xl", dx, 0, 0, ("PA", sg), ("PA", dg)))
    for dy in (1, -1):
        rs, rd, pr = ((35, 5), lo, (3, 5)) if dy == 1 else ((8, 5), hi, (0, 5))
        out.append(("y", 0, dy, 0, ("GC", 0, (5, 8), rs), ("GC", 0, (5, 8), rd)))
        out.append(("y", 0, dy, 0, ("GC", 1, (5, 8), rs), ("GC", 1, (5, 8), rd)))
        out.append(("yz", 0, dy, 0, ("PR", 1, (5, 8), pr), ("PR", 1 - dy, (5, 8), pr)))
    return out


def coarse_messages():
    out = []
    for dx in (2, 1, 0, -1, -2):
        for dy in (1, 0, -1):
            ps, pd = {
                0: ((5, 4), (5, 4)),
                1: ((5, 4), (1, 4)),
                -1: ((5, 4), (9, 4)),
                2: ((8, 1), (0, 1)),
                -2: ((5, 1), (13, 1)),
            }[dx]
            rs, rd = {0: ((8, 16), (8, 16)), 1: ((19, 5), (3, 5)), -1: ((8, 5), (24, 5))}[dy]
            if (dx, dy) != (0, 0):
                out.append((dx, dy, 0, ps, pd, rs, rd))
            out.append((dx, dy, 1, None, None, {0: (0, 8), 1: (3, 5), -1: (0, 5)}[dy], None))
    return out


FINE = fine_messages()
COARSE = coarse_messages()
NF, NC = len(FINE), len(COARSE)


def ds(pair):
    return pl.ds(pair[0], pair[1])


def up(x):
    return pltpu.roll(x, 127, 1)


def down(x):
    return pltpu.roll(x, 1, 1)


def stencil(ref, before, after, p, r, tiles, outs, lane, h):
    sf = 1.0 / (h * h)
    bf = 1.0 / h
    rows = pl.ds(r, 8)
    centre, straight, drift, plus, minus = [], [], [], [], []
    for t in range(tiles):
        v = ref[p, t, rows, :]
        xm = ref[p - 1, t, rows, :]
        xp = ref[p + 1, t, rows, :]
        ym = ref[p, t, pl.ds(r - 1, 8), :]
        yp = ref[p, t, pl.ds(r + 1, 8), :]
        d = xp - xm
        fy = yp - ym
        flat = (32.0 * sf) * v
        mixed = (1.5 * sf) * (d - fy)
        slope = (0.75 * bf) * v
        plus.append(before[p, t, rows, :] * (flat + mixed) + slope)
        minus.append(after[p, t, rows, :] * (flat - mixed) - slope)
        centre.append(v)
        if t in outs:
            dyy = (ref[p + 1, t, pl.ds(r + 1, 8), :] - ref[p - 1, t, pl.ds(r + 1, 8), :]) - (
                ref[p + 1, t, pl.ds(r - 1, 8), :] - ref[p - 1, t, pl.ds(r - 1, 8), :]
            )
            straight.append((48.0 * sf) * (xp + xm) + (40.0 * sf) * (yp + ym) + (2.0 * sf) * dyy)
            drift.append((1.5 * bf) * d - bf * fy)
        else:
            straight.append(None)
            drift.append(None)
    result = []
    for t in outs:
        b = (
            drift[t]
            + up(jnp.where(lane == 0, plus[(t + 1) % tiles], plus[t]))
            + down(jnp.where(lane == 127, minus[t - 1], minus[t]))
        )
        result.append((centre[t], straight[t], b))
    return result


def shifted_scales(values, lane):
    count = len(values)
    before = [down(jnp.where(lane == 127, values[t - 1], values[t])) for t in range(count)]
    after = [up(jnp.where(lane == 0, values[(t + 1) % count], values[t])) for t in range(count)]
    return before, after


def kernel(g_hbm, c_hbm, sol_ref, res_ref, GC, PS, PR, W, FB, FA, A, B, RX, CO, QS, QR,
           CW, KB, KA, CA, CB, UPS, load_sem, f_send, f_recv, c_send, c_recv):
    gx, gy, gz = lax.axis_index("gx"), lax.axis_index("gy"), lax.axis_index("gz")

    def peer(dx, dy, dz):
        return (gx + dx, gy + dy, lax.rem(gz + dz, 2))

    def inside(dx, dy):
        tests = []
        if dx > 0:
            tests.append(gx < NXD - dx)
        if dx < 0:
            tests.append(gx >= -dx)
        if dy > 0:
            tests.append(gy < NYD - dy)
        if dy < 0:
            tests.append(gy >= -dy)
        if not tests:
            return None
        return tests[0] if len(tests) == 1 else tests[0] & tests[1]

    def guarded(dx, dy, act):
        test = inside(dx, dy)
        if test is None:
            act()
        else:
            pl.when(test)(act)

    loads = []
    for a, src in ((0, g_hbm), (1, c_hbm)):
        for t in range(2):
            cp = pltpu.make_async_copy(
                src.at[:, :, pl.ds(128 * t, 128)],
                GC.at[a, pl.ds(5, 8), t, pl.ds(8, 32), :],
                load_sem.at[2 * a + t],
            )
            cp.start()
            loads.append(cp)

    barrier = pltpu.get_barrier_semaphore()
    partners = 1
    for dx, dy, dz in ((1, 0, 0), (-1, 0, 0), (0, 1, 0), (0, -1, 0), (0, 0, 1)):

        def greet():
            pl.semaphore_signal(barrier, inc=1, device_id=peer(dx, dy, dz), device_id_type=MESH)

        guarded(dx, dy, greet)
        if not dz:
            partners = partners + jnp.where(inside(dx, dy), 1, 0)

    lane = lax.broadcasted_iota(jnp.int32, (8, 128), 1)
    sub = lax.broadcasted_iota(jnp.int32, (8, 128), 0)
    zfirst = 120 * gz
    zmask = (lane >= zfirst) & (lane < zfirst + 8)
    blank = jnp.zeros((8, 128), F32)

    def clear_fine(low, high, rows):
        def one(p, _):
            for a in range(2):
                for t in range(2):
                    for r in rows:
                        GC[a, p, t, pl.ds(r, 8), :] = blank
            return 0
        lax.fori_loop(low, high, one, 0)

    def clear_pack(slots, low, high):
        def one(p, _):
            for n in slots:
                PR[n, p] = blank
            return 0
        lax.fori_loop(low, high, one, 0)

    def clear_coarse(low, high, rows):
        def one(p, _):
            for k in range(2):
                for r in rows:
                    CO[k, p, 0, pl.ds(r, 8), :] = blank
            return 0
        lax.fori_loop(low, high, one, 0)

    all_rows = (0, 8, 16, 24, 32, 40)

    def clear_edge(cols, rows):
        for k in range(2):
            for n in cols:
                for m in rows:
                    QR[k, n, m] = blank

    @pl.when(gx == 0)
    def _():
        clear_fine(0, 5, all_rows)
        clear_pack((0, 1, 2), 0, 5)
        clear_coarse(0, 5, (0, 8, 16, 24))
        clear_edge((0, 1), (0, 1, 2))

    @pl.when(gx == 1)
    def _():
        clear_coarse(0, 1, (0, 8, 16, 24))
        clear_edge((0,), (0, 1, 2))

    @pl.when(gx == NXD - 1)
    def _():
        clear_fine(13, 18, all_rows)
        clear_pack((0, 1, 2), 13, 18)
        clear_coarse(9, 14, (0, 8, 16, 24))
        clear_edge((3, 4), (0, 1, 2))

    @pl.when(gx == NXD - 2)
    def _():
        clear_coarse(13, 14, (0, 8, 16, 24))
        clear_edge((4,), (0, 1, 2))

    @pl.when(gy == 0)
    def _():
        clear_fine(5, 13, (0,))
        clear_pack((0,), 5, 13)
        clear_coarse(0, 14, (0,))
        clear_edge((0, 1, 2, 3, 4), (0,))

    @pl.when(gy == NYD - 1)
    def _():
        clear_fine(5, 13, (40,))
        clear_pack((2,), 5, 13)
        clear_coarse(0, 14, (24,))
        clear_edge((0, 1, 2, 3, 4), (2,))

    for cp in loads:
        cp.wait()

    def pack_plane(x, _):
        acc = blank
        for a in range(2):
            for j in range(4):
                m = 4 * a + j
                t0 = GC[a, 5 + x, 0, pl.ds(8 + 8 * j, 8), :]
                t1 = GC[a, 5 + x, 1, pl.ds(8 + 8 * j, 8), :]
                both = pltpu.roll(jnp.where(lane >= 64, t1, t0), (16 * m + 8) % 128, 1)
                acc = jnp.where((lane >= 16 * m) & (lane < 16 * m + 16), both, acc)
        PS[x] = acc
        return 0

    lax.fori_loop(0, 8, pack_plane, 0)

    row_i = lax.broadcasted_iota(jnp.int32, (256, 128), 0)
    col_i = lax.broadcasted_iota(jnp.int32, (256, 128), 1)
    pool = jnp.where(row_i // 2 == col_i, 0.125, 0.0).astype(F32)

    def coarsen_rows(k):
        pieces = []
        for i in range(4):
            cols = []
            for t in range(2):
                cols.append(RX[i, t, pl.ds(0, 16, stride=2), :] + RX[i, t, pl.ds(1, 16, stride=2), :])
            pieces.append(jnp.concatenate(cols, axis=1))
        allp = jnp.concatenate(pieces, axis=0)
        q = jnp.dot(allp, pool, preferred_element_type=F32, precision=lax.Precision.HIGHEST)
        acc = blank
        for i in range(4):
            CO[k, 5 + i, 0, pl.ds(8, 16), :] = q[16 * i : 16 * i + 16]
            for j in range(2):
                m = 2 * i + j
                turned = pltpu.roll(q[8 * m : 8 * m + 8], (16 * m + 8) % 128, 1)
                acc = jnp.where((lane >= 16 * m) & (lane < 16 * m + 16), turned, acc)
        QS[k] = acc

    def pair_scale(i, _):
        for t in range(2):
            RX[i, t] = GC[1, 5 + 2 * i, t, pl.ds(8, 32), :] + GC[1, 6 + 2 * i, t, pl.ds(8, 32), :]
        return 0

    lax.fori_loop(0, 4, pair_scale, 0)
    coarsen_rows(1)

    starts = [4, 12, 20, 28, 36]
    ylow = (gy * 32 + sub - 4) >= 0
    yhigh = (gy * 32 + sub + 28) < 512

    def place(where):
        if where[0] == "PS":
            return PS
        if where[0] == "PR":
            return PR.at[where[1], ds(where[2]), ds(where[3]), :]
        if where[0] == "PA":
            return PR.at[:, ds(where[1])]
        return GC.at[where[1], ds(where[2]), pl.ds(0, 2), ds(where[3]), :]

    def fine_copy(i):
        _, dx, dy, dz, src, dst = FINE[i]
        return pltpu.make_async_remote_copy(
            src_ref=place(src),
            dst_ref=place(dst),
            send_sem=f_send.at[i],
            recv_sem=f_recv.at[i],
            device_id=peer(dx, dy, dz),
            device_id_type=MESH,
        )

    def coarse_copy(k, i):
        dx, dy, dz, ps, pd, rs, rd = COARSE[i]
        if dz:
            src, dst = QS.at[k, ds(rs), :], QR.at[k, 2 - dx, 1 - dy, ds(rs), :]
        else:
            src, dst = CO.at[k, ds(ps), 0, ds(rs), :], CO.at[k, ds(pd), 0, ds(rd), :]
        return pltpu.make_async_remote_copy(
            src_ref=src,
            dst_ref=dst,
            send_sem=c_send.at[k * NC + i],
            recv_sem=c_recv.at[k * NC + i],
            device_id=peer(dx, dy, dz),
            device_id_type=MESH,
        )

    FAR = [(2, 1), (2, -1), (-2, 1), (-2, -1), (1, 1), (1, -1), (-1, 1), (-1, -1),
           (2, 0), (-2, 0), (1, 0), (-1, 0), (0, 1), (0, -1), (0, 0)]
    NEAR = [(1, 0), (-1, 0), (0, 1), (0, -1), (0, 0)]

    def run(direction, copies, method, back):
        if copies:
            dx, dy = direction
            def act():
                for cp in copies:
                    getattr(cp, method)()
            guarded(-dx if back else dx, -dy if back else dy, act)

    def fine(phase, method):
        for d in NEAR:
            run(d, [fine_copy(i) for i in range(NF) if FINE[i][0] in phase and FINE[i][1:3] == d],
                method, method == "wait_recv")

    def coarse(k, method):
        for d in FAR:
            run(d, [coarse_copy(k, i) for i in range(NC) if COARSE[i][:2] == d],
                method, method == "wait_recv")

    pl.semaphore_wait(barrier, partners)

    fine(("z",), "start")
    fine(("x", "y"), "start")

    def unpack(low, high):
        def unpack_plane(p, _):
            for a in range(2):
                for r in range(6):
                    slot, j = (0, 3) if r == 0 else (2, 0) if r == 5 else (1, r - 1)
                    m = 4 * a + j
                    v = pltpu.roll(PR[slot, p], (128 - 16 * m - 8) % 128, 1)
                    GC[a, p, 2, pl.ds(8 * r, 8), :] = jnp.where(zmask, v, 0.0)
            return 0

        lax.fori_loop(low, high, unpack_plane, 0)

    def weights(low, high):
        def one(p, _):
            at = gx * 8 + p - 5
            scale = jnp.where((at >= 0) & (at < 64), DAMP, 0.0).astype(F32)
            for r in starts:
                scales = [GC[1, p, t, pl.ds(r, 8), :] for t in range(3)]
                before, after = shifted_scales(scales, lane)
                for t in range(3):
                    FB[p, t, pl.ds(r, 8), :] = before[t]
                    FA[p, t, pl.ds(r, 8), :] = after[t]
                    w = scale / (1.05 + 240.0 * scales[t])
                    if r == 4:
                        w = jnp.where(ylow, w, 0.0)
                    if r == 36:
                        w = jnp.where(yhigh, w, 0.0)
                    if t == 2:
                        w = jnp.where(zmask, w, 0.0)
                    W[p, t, pl.ds(r, 8), :] = w
            return 0

        lax.fori_loop(low, high, one, 0)

    def fine_plane(view, dst, p):
        for r in starts:
            for t, (v, s, b) in enumerate(stencil(view, FB, FA, p, r, 3, (0, 1, 2), lane, 1.0)):
                rows = pl.ds(r, 8)
                dst[p, t, rows, :] = 0.4 * v + W[p, t, rows, :] * (
                    GC[0, p, t, rows, :] + GC[1, p, t, rows, :] * s + b
                )

    def fine_sweep(src, dst, low, high, src_index=None):
        view = src if src_index is None else src.at[src_index]

        def one(n, _):
            fine_plane(view, dst, low + 2 * n)
            fine_plane(view, dst, low + 2 * n + 1)
            return 0

        lax.fori_loop(0, (high - low) // 2, one, 0)

    def fine_sides(src, dst, low, high, count, src_index=None):
        view = src if src_index is None else src.at[src_index]

        def one(n, _):
            fine_plane(view, dst, low + n)
            fine_plane(view, dst, high + n)
            return 0

        lax.fori_loop(0, count, one, 0)

    def fine_residue(src, p):
        out = []
        for r in (8, 16, 24, 32):
            for t, (v, s, b) in enumerate(stencil(src, FB, FA, p, r, 3, (0, 1), lane, 1.0)):
                rows = pl.ds(r, 8)
                out.append(
                    GC[0, p, t, rows, :] - 1.05 * v + GC[1, p, t, rows, :] * (s - 240.0 * v) + b
                )
        return out

    fine(("z",), "wait_recv")
    fine(("yz",), "start")
    fine(("y", "yz"), "wait_recv")
    fine(("xc",), "start")
    fine(("xl",), "start")
    unpack(5, 13)
    weights(5, 13)
    fine_sweep(GC, A, 6, 12, 0)
    fine_sweep(A, B, 7, 11)
    fine(("x", "xc"), "wait_recv")
    coarse(1, "start")
    unpack(2, 5)
    unpack(13, 16)
    weights(3, 5)
    weights(13, 15)
    fine_sides(GC, A, 3, 12, 3, 0)
    fine_sides(A, B, 4, 11, 3)

    def residue_pair(i, _):
        one = fine_residue(B, 5 + 2 * i)
        two = fine_residue(B, 6 + 2 * i)
        for n in range(8):
            RX[i, n % 2, pl.ds(8 * (n // 2), 8), :] = one[n] + two[n]
        return 0

    lax.fori_loop(0, 4, residue_pair, 0)
    coarsen_rows(0)

    coarse(0, "start")

    fine(("xl",), "wait_recv")
    unpack(0, 2)
    unpack(16, 18)
    weights(1, 3)
    weights(15, 17)
    fine_sides(GC, A, 1, 15, 2, 0)
    fine_sides(A, B, 2, 14, 2)

    cylow = (gy * 16 + sub - 8) >= 0
    cyhigh = (gy * 16 + sub + 16) < 256

    coarse(1, "wait_recv")

    def coarse_unpack(k):
        for p in range(CX):
            col, i = [(0, 3), (1, 0), (1, 1), (1, 2), (1, 3), (2, 0), (2, 1), (2, 2), (2, 3),
                      (3, 0), (3, 1), (3, 2), (3, 3), (4, 0)][p]
            for r, (row, j) in enumerate(((0, 1), (1, 0), (1, 1), (2, 0))):
                m = 2 * i + j
                turned = pltpu.roll(QR[k, col, row], (128 - 16 * m - 8) % 128, 1)
                CO[k, p, 1, pl.ds(8 * r, 8), :] = jnp.where(zmask, turned, 0.0)

    coarse_unpack(1)

    def coarse_weights(p, _):
        at = gx * 4 + p - 5
        scale = jnp.where((at >= 0) & (at < 32), DAMP, 0.0).astype(F32)
        for n, r in enumerate((0, 8, 16, 24)):
            scales = [CO[1, p, t, pl.ds(r, 8), :] for t in range(2)]
            before, after = shifted_scales(scales, lane)
            for t in range(2):
                KB[p, t, pl.ds(r, 8), :] = before[t]
                KA[p, t, pl.ds(r, 8), :] = after[t]
                w = scale / (1.05 + 60.0 * scales[t])
                if r == 0:
                    w = jnp.where(cylow, w, 0.0)
                if r == 24:
                    w = jnp.where(cyhigh, w, 0.0)
                if t == 1:
                    w = jnp.where(zmask, w, 0.0)
                CW[p, t, pl.ds(r, 8), :] = w
        return 0

    lax.fori_loop(0, CX, coarse_weights, 0)

    coarse(0, "wait_recv")
    coarse_unpack(0)

    def coarse_first(p, _):
        for r in (0, 8, 16, 24):
            for t in range(2):
                rows = pl.ds(r, 8)
                CA[p, t, rows, :] = CW[p, t, rows, :] * CO[0, p, t, rows, :]
        return 0

    lax.fori_loop(0, CX, coarse_first, 0)

    def coarse_sweep(src, dst, low, high):
        def one(n, _):
            for half in range(2):
                p = low + 2 * n + half
                for r in (4, 12, 20):
                    for t, (v, s, b) in enumerate(
                        stencil(src, KB, KA, p, r, 2, (0, 1), lane, 2.0)
                    ):
                        rows = pl.ds(r, 8)
                        dst[p, t, rows, :] = 0.4 * v + CW[p, t, rows, :] * (
                            CO[0, p, t, rows, :] + CO[1, p, t, rows, :] * s + b
                        )
            return 0

        lax.fori_loop(0, (high - low) // 2, one, 0)

    coarse_sweep(CA, CB, 1, 13)
    coarse_sweep(CB, CA, 2, 12)
    coarse_sweep(CA, CB, 3, 11)

    ri = lax.broadcasted_iota(jnp.int32, (128, 256), 0)
    ci = lax.broadcasted_iota(jnp.int32, (128, 256), 1)
    spread = jnp.where(ci // 2 == ri, 1.0, 0.0).astype(F32)
    rh = lax.broadcasted_iota(jnp.int32, (128, 128), 0)
    ch = lax.broadcasted_iota(jnp.int32, (128, 128), 1)
    source = ch // 2 + 64 * gz
    keep = (ch >= zfirst) & (ch < zfirst + 8)
    spread_h = jnp.where((source == rh) & keep, 1.0, 0.0).astype(F32)
    mine = jnp.concatenate([CB[3 + q, 0, pl.ds(4, 24), :] for q in range(8)], axis=0)
    other = jnp.concatenate([CB[3 + q, 1, pl.ds(4, 24), :] for q in range(8)], axis=0)
    wide = jnp.dot(mine, spread, preferred_element_type=F32, precision=lax.Precision.HIGHEST)
    wide_h = jnp.dot(other, spread_h, preferred_element_type=F32, precision=lax.Precision.HIGHEST)
    for q in range(8):
        for t in range(3):
            part = (wide[24 * q : 24 * q + 24, 128 * t : 128 * t + 128] if t < 2
                    else wide_h[24 * q : 24 * q + 24])
            UPS[q, t, pl.ds(0, 24, stride=2), :] = part
            UPS[q, t, pl.ds(1, 24, stride=2), :] = part

    def add_up(q, _):
        for half in range(2):
            for r in range(6):
                for t in range(3):
                    rows = pl.ds(8 * r, 8)
                    p = 2 * q + 1 + half
                    A[p, t, rows, :] = B[p, t, rows, :] + UPS[q, t, rows, :]
        return 0

    lax.fori_loop(0, 8, add_up, 0)

    fine_sweep(A, B, 3, 15)
    fine_sweep(B, A, 4, 14)

    def finish(x, _):
        vals = fine_residue(A, 5 + x)
        for n in range(8):
            t, r = n % 2, 8 * (n // 2)
            res_ref[x, pl.ds(r, 8), pl.ds(128 * t, 128)] = vals[n]
            sol_ref[x, pl.ds(r, 8), pl.ds(128 * t, 128)] = A[5 + x, t, pl.ds(8 + r, 8), :]
        return 0

    lax.fori_loop(0, 8, finish, 0)

    fine(("z", "x", "y", "yz", "xc", "xl"), "wait_send")
    coarse(1, "wait_send")
    coarse(0, "wait_send")


def on_device(right_side, volscale):
    shape = pltpu.VMEM(right_side.shape, F32)
    fine = pltpu.VMEM((PX, 3, ROWS, 128), F32)
    coarse = pltpu.VMEM((CX, 2, CROWS, 128), F32)
    any_space = pl.BlockSpec(memory_space=pl.ANY)
    return pl.pallas_call(
        kernel,
        out_shape=(shape, shape),
        in_specs=[any_space] * 2,
        out_specs=(pl.BlockSpec(memory_space=pltpu.VMEM),) * 2,
        scratch_shapes=[
            pltpu.VMEM((2, PX, 3, ROWS, 128), F32),
            pltpu.VMEM((8, 8, 128), F32),
            pltpu.VMEM((3, PX, 8, 128), F32),
            fine,
            fine,
            fine,
            fine,
            fine,
            pltpu.VMEM((4, 2, 32, 128), F32),
            pltpu.VMEM((2, CX, 2, CROWS, 128), F32),
            pltpu.VMEM((2, 8, 128), F32),
            pltpu.VMEM((2, 5, 3, 8, 128), F32),
            coarse,
            coarse,
            coarse,
            coarse,
            coarse,
            pltpu.VMEM((8, 3, ROWS, 128), F32),
            pltpu.SemaphoreType.DMA((4,)),
            pltpu.SemaphoreType.DMA((NF,)),
            pltpu.SemaphoreType.DMA((NF,)),
            pltpu.SemaphoreType.DMA((2 * NC,)),
            pltpu.SemaphoreType.DMA((2 * NC,)),
        ],
        compiler_params=pltpu.CompilerParams(collective_id=0, has_side_effects=True),
    )(right_side, volscale)


def solution(mesh):
    placed = (P("gx", "gy", "gz"), P("gx", "gy", "gz"))
    return jax.shard_map(
        on_device,
        mesh=mesh,
        in_specs=placed,
        out_specs=(P("gx", "gy", "gz"), P("gx", "gy", "gz")),
        check_vma=False,
    )
```

```python
import jax
import jax.numpy as jnp
from jax import lax
from jax.experimental import pallas as pl
from jax.experimental.pallas import tpu as pltpu
from jax.sharding import PartitionSpec as P

MESH = pl.DeviceIdType.MESH
F32 = jnp.float32
NXD, NYD = 8, 16
BX, BY = 8, 32
HALO = 5
PX = BX + 2 * HALO
ROWS = BY + 16
CX = BX // 2 + 2 * HALO
CROWS = BY // 2 + 16
DAMP = 0.6


def fine_messages():
    lo, mid, hi = (3, 5), (8, 32), (40, 5)
    every = (0, 3)
    out = [
        ("z", 0, 0, 1, ("PS",), ("PR", (1, 1), (5, 8), (0, 8))),
        ("z", 0, 0, 1, ("QS", 1), ("QR", 2, (1, 1), (0, 8))),
    ]
    for dx in (1, -1):
        side, far = 2 - dx, 2 - 2 * dx
        sg, dg = ((10, 3), (2, 3)) if dx == 1 else ((5, 3), (13, 3))
        sc, dc = ((11, 2), (3, 2)) if dx == 1 else ((5, 2), (13, 2))
        out.append(("x", dx, 0, 0, ("GC", 0, sg, mid), ("GC", 0, dg, mid)))
        out.append(("x", dx, 0, 0, ("GC", 1, sc, mid), ("GC", 1, dc, mid)))
        out.append(("xz", dx, 0, 0, ("PR", (1, 1), sg, (0, 8)), ("PR", (1, 1), dg, (0, 8))))
        for rows in (lo, hi):
            out.append(("xy", dx, 0, 0, ("GC", 0, sg, rows), ("GC", 0, dg, rows)))
            out.append(("xy", dx, 0, 0, ("GC", 1, sc, rows), ("GC", 1, dc, rows)))
        for slot, rows in ((0, (3, 5)), (2, (0, 5))):
            out.append(("xyz", dx, 0, 0, ("PR", (slot, 1), sg, rows), ("PR", (slot, 1), dg, rows)))
        out.append(("cx", dx, 0, 0, ("CO", (5, 4), (3, 26)), ("CO", (1 if dx == 1 else 9, 4), (3, 26))))
        out.append(("cx", dx, 0, 0, ("QR", 2, every, (0, 8)), ("QR", side, every, (0, 8))))
        near, last = (4, 0) if dx == 1 else (9, 13)
        out.append(("cxx", dx, 0, 0, ("CO", (near, 1), (3, 26)), ("CO", (last, 1), (3, 26))))
        out.append(("cxx", dx, 0, 0, ("QR", side, every, (0, 8)), ("QR", far, every, (0, 8))))
        sb, db = ((10, 2), (2, 2)) if dx == 1 else ((6, 2), (14, 2))
        out.append(("s", dx, 0, 0, ("B", sb), ("B", db)))
        out.append(("s", dx, 0, 0, ("SS", (1 - dx) // 2), ("SR", (1 - dx) // 2)))
    for dy in (1, -1):
        rs, rd, pr = ((35, 5), lo, (3, 5)) if dy == 1 else ((8, 5), hi, (0, 5))
        cs, cd = ((19, 5), (3, 5)) if dy == 1 else ((8, 5), (24, 5))
        out.append(("y", 0, dy, 0, ("GC", 0, (5, 8), rs), ("GC", 0, (5, 8), rd)))
        out.append(("y", 0, dy, 0, ("GC", 1, (5, 8), rs), ("GC", 1, (5, 8), rd)))
        out.append(("yz", 0, dy, 0, ("PR", (1, 1), (5, 8), pr), ("PR", (1 - dy, 1), (5, 8), pr)))
        out.append(("cy", 0, dy, 0, ("CO", (5, 4), cs), ("CO", (5, 4), cd)))
        out.append(("cy", 0, dy, 0, ("QR", 2, (1, 1), pr), ("QR", 2, (1 - dy, 1), pr)))
    return out


def coarse_messages():
    out = []
    for dx in (2, 1, 0, -1, -2):
        for dy in (1, 0, -1):
            ps, pd = {
                0: ((5, 4), (5, 4)),
                1: ((5, 4), (1, 4)),
                -1: ((5, 4), (9, 4)),
                2: ((8, 1), (0, 1)),
                -2: ((5, 1), (13, 1)),
            }[dx]
            rs, rd = {0: ((8, 16), (8, 16)), 1: ((19, 5), (3, 5)), -1: ((8, 5), (24, 5))}[dy]
            if (dx, dy) != (0, 0):
                out.append((dx, dy, 0, ps, pd, rs, rd))
            out.append((dx, dy, 1, None, None, {0: (0, 8), 1: (3, 5), -1: (0, 5)}[dy], None))
    return out


FINE = fine_messages()
COARSE = coarse_messages()
NF, NC = len(FINE), len(COARSE)


def ds(pair):
    return pl.ds(pair[0], pair[1])


def up(x):
    return pltpu.roll(x, 127, 1)


def down(x):
    return pltpu.roll(x, 1, 1)


RATIO = 64.0 / 3.0


def stencil(ref, factors, base, count, r, tiles, outs, lane, bf):
    before, before_v, after, after_v = factors
    rows = pl.ds(r, 8)
    parts = []
    for k in range(count):
        parts.append(([], [], [], [], []))
    for t in range(tiles):
        vs = [ref[base - 1 + k, t, rows, :] for k in range(count + 2)]
        fys = []
        for k in range(count + 2):
            if t in outs or 0 < k <= count:
                fys.append(
                    ref[base - 1 + k, t, pl.ds(r + 1, 8), :]
                    - ref[base - 1 + k, t, pl.ds(r - 1, 8), :]
                )
            else:
                fys.append(None)
        for k in range(count):
            centre, straight, drift, plus, minus = parts[k]
            p = base + k
            v, xm, xp, fy = vs[k + 1], vs[k], vs[k + 2], fys[k + 1]
            d = xp - xm
            m = d - fy
            plus.append(before_v[p, t, rows, :] * v + before[p, t, rows, :] * m)
            minus.append(after_v[p, t, rows, :] * v - after[p, t, rows, :] * m)
            centre.append(v)
            if t in outs:
                sy = ref[p, t, pl.ds(r + 1, 8), :] + ref[p, t, pl.ds(r - 1, 8), :]
                straight.append(24.0 * (xp + xm) + 20.0 * sy + (fys[k + 2] - fys[k]))
                drift.append((1.5 * bf) * d - (fy if bf == 1.0 else bf * fy))
            else:
                straight.append(None)
                drift.append(None)
    result = []
    for k in range(count):
        centre, straight, drift, plus, minus = parts[k]
        one = []
        for t in outs:
            b = (
                drift[t]
                + up(jnp.where(lane == 0, plus[(t + 1) % tiles], plus[t]))
                + down(jnp.where(lane == 127, minus[t - 1], minus[t]))
            )
            one.append((t, centre[t], straight[t], b))
        result.append(one)
    return result


def keep_factors(stores, p, rows, scales, lane, sf, bf):
    double, before, before_v, after, after_v = stores
    low, high = shifted_scales([(1.5 * sf) * c for c in scales], lane)
    for t in range(len(scales)):
        double[p, t, rows, :] = (2.0 * sf) * scales[t]
        before[p, t, rows, :] = low[t]
        before_v[p, t, rows, :] = RATIO * low[t] + 0.75 * bf
        after[p, t, rows, :] = high[t]
        after_v[p, t, rows, :] = RATIO * high[t] - 0.75 * bf


def shifted_scales(values, lane):
    count = len(values)
    before = [down(jnp.where(lane == 127, values[t - 1], values[t])) for t in range(count)]
    after = [up(jnp.where(lane == 0, values[(t + 1) % count], values[t])) for t in range(count)]
    return before, after


def kernel(g_hbm, c_hbm, sol_ref, res_ref, GC, PS, PR, SS, SR, W, F2, FB, FBV, FA, FAV, A, B, RX, CO, QS, QR,
           CW, K2, KB, KBV, KA, KAV, CA, CB, UPS, load_sem, f_send, f_recv, c_send, c_recv):
    gx, gy, gz = lax.axis_index("gx"), lax.axis_index("gy"), lax.axis_index("gz")

    def peer(dx, dy, dz):
        return (gx + dx, gy + dy, lax.rem(gz + dz, 2))

    def inside(dx, dy):
        tests = []
        if dx > 0:
            tests.append(gx < NXD - dx)
        if dx < 0:
            tests.append(gx >= -dx)
        if dy > 0:
            tests.append(gy < NYD - dy)
        if dy < 0:
            tests.append(gy >= -dy)
        if not tests:
            return None
        return tests[0] if len(tests) == 1 else tests[0] & tests[1]

    def guarded(dx, dy, act):
        test = inside(dx, dy)
        if test is None:
            act()
        else:
            pl.when(test)(act)

    loads = []
    for a, src in ((0, g_hbm), (1, c_hbm)):
        for t in range(2):
            cp = pltpu.make_async_copy(
                src.at[:, :, pl.ds(128 * t, 128)],
                GC.at[a, pl.ds(5, 8), t, pl.ds(8, 32), :],
                load_sem.at[2 * a + t],
            )
            cp.start()
            loads.append(cp)

    barrier = pltpu.get_barrier_semaphore()
    partners = 1
    for dx, dy, dz in ((1, 0, 0), (-1, 0, 0), (0, 1, 0), (0, -1, 0), (0, 0, 1)):

        def greet():
            pl.semaphore_signal(barrier, inc=1, device_id=peer(dx, dy, dz), device_id_type=MESH)

        guarded(dx, dy, greet)
        if not dz:
            partners = partners + jnp.where(inside(dx, dy), 1, 0)

    lane = lax.broadcasted_iota(jnp.int32, (8, 128), 1)
    sub = lax.broadcasted_iota(jnp.int32, (8, 128), 0)
    zfirst = 120 * gz
    zmask = (lane >= zfirst) & (lane < zfirst + 8)
    blank = jnp.zeros((8, 128), F32)

    def clear_fine(low, high, rows):
        def one(p, _):
            for a in range(2):
                for t in range(2):
                    for r in rows:
                        GC[a, p, t, pl.ds(r, 8), :] = blank
            return 0
        lax.fori_loop(low, high, one, 0)

    def clear_pack(slots, low, high):
        def one(p, _):
            for n in slots:
                PR[n, p] = blank
            return 0
        lax.fori_loop(low, high, one, 0)

    def clear_coarse(k, low, high, rows):
        def one(p, _):
            for r in rows:
                CO[k, p, 0, pl.ds(r, 8), :] = blank
            return 0
        lax.fori_loop(low, high, one, 0)

    def clear_edge(k, cols, rows):
        for n in cols:
            for m in rows:
                QR[k, n, m] = blank

    def clear_smooth(low):
        for p in (low, low + 1):
            for t in range(3):
                for r in (0, 8, 16, 24, 32, 40):
                    B[p, t, pl.ds(r, 8), :] = blank

    all_rows = (0, 8, 16, 24, 32, 40)
    coarse_rows = (0, 8, 16, 24)
    slots = (0, 1, 2)

    @pl.when(gx == 0)
    def _():
        clear_fine(2, 5, all_rows)
        clear_pack(slots, 2, 5)
        for k in range(2):
            clear_coarse(k, 0, 5, coarse_rows)
            clear_edge(k, (0, 1), slots)
        clear_smooth(2)

    @pl.when(gx == 1)
    def _():
        clear_coarse(0, 0, 1, coarse_rows)
        clear_edge(0, (0,), slots)

    @pl.when(gx == NXD - 1)
    def _():
        clear_fine(13, 16, all_rows)
        clear_pack(slots, 13, 16)
        for k in range(2):
            clear_coarse(k, 9, 14, coarse_rows)
            clear_edge(k, (3, 4), slots)
        clear_smooth(14)

    @pl.when(gx == NXD - 2)
    def _():
        clear_coarse(0, 13, 14, coarse_rows)
        clear_edge(0, (4,), slots)

    @pl.when(gy == 0)
    def _():
        clear_fine(5, 13, (0,))
        clear_pack((0,), 5, 13)
        clear_coarse(0, 0, 14, (0,))
        clear_coarse(1, 5, 9, (0,))
        clear_edge(0, (0, 1, 2, 3, 4), (0,))
        clear_edge(1, (2,), (0,))

    @pl.when(gy == NYD - 1)
    def _():
        clear_fine(5, 13, (40,))
        clear_pack((2,), 5, 13)
        clear_coarse(0, 0, 14, (24,))
        clear_coarse(1, 5, 9, (24,))
        clear_edge(0, (0, 1, 2, 3, 4), (2,))
        clear_edge(1, (2,), (2,))

    for cp in loads:
        cp.wait()

    def pack_plane(x, _):
        acc = blank
        for a in range(2):
            for j in range(4):
                m = 4 * a + j
                t0 = GC[a, 5 + x, 0, pl.ds(8 + 8 * j, 8), :]
                t1 = GC[a, 5 + x, 1, pl.ds(8 + 8 * j, 8), :]
                both = pltpu.roll(jnp.where(lane >= 64, t1, t0), (16 * m + 8) % 128, 1)
                acc = jnp.where((lane >= 16 * m) & (lane < 16 * m + 16), both, acc)
        PS[x] = acc
        return 0

    lax.fori_loop(0, 8, pack_plane, 0)

    row_i = lax.broadcasted_iota(jnp.int32, (256, 128), 0)
    col_i = lax.broadcasted_iota(jnp.int32, (256, 128), 1)
    pool = jnp.where(row_i // 2 == col_i, 0.125, 0.0).astype(F32)

    def coarsen_rows(k):
        pieces = []
        for i in range(4):
            cols = []
            for t in range(2):
                cols.append(RX[i, t, pl.ds(0, 16, stride=2), :] + RX[i, t, pl.ds(1, 16, stride=2), :])
            pieces.append(jnp.concatenate(cols, axis=1))
        allp = jnp.concatenate(pieces, axis=0)
        q = jnp.dot(allp, pool, preferred_element_type=F32, precision=lax.Precision.HIGHEST)
        acc = blank
        for i in range(4):
            CO[k, 5 + i, 0, pl.ds(8, 16), :] = q[16 * i : 16 * i + 16]
            for j in range(2):
                m = 2 * i + j
                turned = pltpu.roll(q[8 * m : 8 * m + 8], (16 * m + 8) % 128, 1)
                acc = jnp.where((lane >= 16 * m) & (lane < 16 * m + 16), turned, acc)
        QS[k] = acc

    def pair_scale(i, _):
        for t in range(2):
            RX[i, t] = GC[1, 5 + 2 * i, t, pl.ds(8, 32), :] + GC[1, 6 + 2 * i, t, pl.ds(8, 32), :]
        return 0

    lax.fori_loop(0, 4, pair_scale, 0)
    coarsen_rows(1)

    starts = [4, 12, 20, 28, 36]
    ylow = (gy * 32 + sub - 4) >= 0
    yhigh = (gy * 32 + sub + 28) < 512

    def place(where):
        kind = where[0]
        if kind == "PS":
            return PS.at[pl.ds(0, 8)]
        if kind == "PR":
            slot, planes, rows = where[1:]
            return PR.at[slot[0], ds(planes), ds(rows), :]
        if kind == "QS":
            return QS.at[where[1]]
        if kind == "QR":
            col, rows, subs = where[1:]
            if rows[1] == 1:
                return QR.at[1, col, rows[0], ds(subs), :]
            return QR.at[1, col, ds(rows), ds(subs), :]
        if kind == "CO":
            return CO.at[1, ds(where[1]), 0, ds(where[2]), :]
        if kind == "B":
            return B.at[ds(where[1]), pl.ds(0, 2), pl.ds(4, 40), :]
        if kind == "SS":
            return SS.at[where[1]]
        if kind == "SR":
            return SR.at[where[1]]
        return GC.at[where[1], ds(where[2]), pl.ds(0, 2), ds(where[3]), :]

    def fine_copy(i):
        _, dx, dy, dz, src, dst = FINE[i]
        return pltpu.make_async_remote_copy(
            src_ref=place(src),
            dst_ref=place(dst),
            send_sem=f_send.at[i],
            recv_sem=f_recv.at[i],
            device_id=peer(dx, dy, dz),
            device_id_type=MESH,
        )

    def coarse_copy(k, i):
        dx, dy, dz, ps, pd, rs, rd = COARSE[i]
        if dz:
            src, dst = QS.at[k, ds(rs), :], QR.at[k, 2 - dx, 1 - dy, ds(rs), :]
        else:
            src, dst = CO.at[k, ds(ps), 0, ds(rs), :], CO.at[k, ds(pd), 0, ds(rd), :]
        return pltpu.make_async_remote_copy(
            src_ref=src,
            dst_ref=dst,
            send_sem=c_send.at[i],
            recv_sem=c_recv.at[i],
            device_id=peer(dx, dy, dz),
            device_id_type=MESH,
        )

    FAR = [(2, 1), (2, -1), (-2, 1), (-2, -1), (1, 1), (1, -1), (-1, 1), (-1, -1),
           (2, 0), (-2, 0), (1, 0), (-1, 0), (0, 1), (0, -1), (0, 0)]
    NEAR = [(1, 0), (-1, 0), (0, 1), (0, -1), (0, 0)]

    def run(direction, copies, method, back):
        if copies:
            dx, dy = direction
            def act():
                for cp in copies:
                    getattr(cp, method)()
            guarded(-dx if back else dx, -dy if back else dy, act)

    def fine(phase, method):
        for d in NEAR:
            run(d, [fine_copy(i) for i in range(NF) if FINE[i][0] in phase and FINE[i][1:3] == d],
                method, method == "wait_recv")

    def coarse(k, method):
        for d in FAR:
            run(d, [coarse_copy(k, i) for i in range(NC) if COARSE[i][:2] == d],
                method, method == "wait_recv")

    pl.semaphore_wait(barrier, partners)

    fine(("z",), "start")
    fine(("y",), "start")
    fine(("x",), "start")

    def unpack(low, high):
        def unpack_plane(p, _):
            for a in range(2):
                for r in range(6):
                    slot, j = (0, 3) if r == 0 else (2, 0) if r == 5 else (1, r - 1)
                    m = 4 * a + j
                    v = pltpu.roll(PR[slot, p], (128 - 16 * m - 8) % 128, 1)
                    GC[a, p, 2, pl.ds(8 * r, 8), :] = jnp.where(zmask, v, 0.0)
            return 0

        lax.fori_loop(low, high, unpack_plane, 0)

    def weights(low, high):
        def one(p, _):
            at = gx * 8 + p - 5
            scale = jnp.where((at >= 0) & (at < 64), DAMP, 0.0).astype(F32)
            for r in starts:
                scales = [GC[1, p, t, pl.ds(r, 8), :] for t in range(3)]
                keep_factors((F2, FB, FBV, FA, FAV), p, pl.ds(r, 8), scales, lane, 1.0, 1.0)
                for t in range(3):
                    w = scale / (1.05 + 240.0 * scales[t])
                    if r == 4:
                        w = jnp.where(ylow, w, 0.0)
                    if r == 36:
                        w = jnp.where(yhigh, w, 0.0)
                    if t == 2:
                        w = jnp.where(zmask, w, 0.0)
                    W[p, t, pl.ds(r, 8), :] = w
            return 0

        lax.fori_loop(low, high, one, 0)

    fine_factors = (FB, FBV, FA, FAV)

    def fine_planes(view, dst, base, count):
        for r in starts:
            rows = pl.ds(r, 8)
            whole = stencil(view, fine_factors, base, count, r, 3, (0, 1, 2), lane, 1.0)
            for k in range(count):
                p = base + k
                for t, v, s, b in whole[k]:
                    dst[p, t, rows, :] = 0.4 * v + W[p, t, rows, :] * (
                        GC[0, p, t, rows, :] + F2[p, t, rows, :] * s + b
                    )

    def fine_sweep(src, dst, low, high, step, src_index=None):
        view = src if src_index is None else src.at[src_index]

        def one(n, _):
            fine_planes(view, dst, low + step * n, step)
            return 0

        lax.fori_loop(0, (high - low) // step, one, 0)

    def fine_sides(src, dst, low, high, count, src_index=None):
        view = src if src_index is None else src.at[src_index]

        def one(n, _):
            fine_planes(view, dst, low + (high - low) * n, count)
            return 0

        lax.fori_loop(0, 2, one, 0)

    def fine_residue(src, base, count):
        out = [[] for _ in range(count)]
        for r in (8, 16, 24, 32):
            rows = pl.ds(r, 8)
            whole = stencil(src, fine_factors, base, count, r, 3, (0, 1), lane, 1.0)
            for k in range(count):
                p = base + k
                for t, v, s, b in whole[k]:
                    out[k].append(
                        GC[0, p, t, rows, :] - 1.05 * v + F2[p, t, rows, :] * (s - 120.0 * v) + b
                    )
        return out

    fine(("z",), "wait_recv")
    fine(("yz", "xz"), "start")
    fine(("cy",), "start")
    fine(("y",), "wait_recv")
    fine(("xy",), "start")
    fine(("yz",), "wait_recv")
    fine(("xyz",), "start")
    fine(("cy",), "wait_recv")
    fine(("cx",), "start")
    unpack(5, 13)
    weights(5, 13)
    fine_sweep(GC, A, 6, 12, 3, 0)
    fine_sweep(A, B, 7, 11, 2)
    fine(("x", "xz", "xy", "xyz"), "wait_recv")
    unpack(2, 5)
    unpack(13, 16)
    weights(3, 5)
    weights(13, 15)
    fine_sides(GC, A, 3, 12, 3, 0)
    fine(("cx",), "wait_recv")
    fine(("cxx",), "start")
    fine_sides(A, B, 4, 11, 3)

    def residue_pair(i, _):
        one, two = fine_residue(B, 5 + 2 * i, 2)
        for n in range(8):
            RX[i, n % 2, pl.ds(8 * (n // 2), 8), :] = one[n] + two[n]
        return 0

    lax.fori_loop(0, 4, residue_pair, 0)
    coarsen_rows(0)

    coarse(0, "start")

    for side in range(2):
        for n in range(2):
            p = (10 if side == 0 else 6) + n
            acc = blank
            for j, r in enumerate(starts):
                turned = pltpu.roll(B[p, 2, pl.ds(r, 8), :], (16 * j + 8) % 128, 1)
                acc = jnp.where((lane >= 16 * j) & (lane < 16 * j + 16), turned, acc)
            SS[side, n] = acc
    fine(("s",), "start")

    cylow = (gy * 16 + sub - 8) >= 0
    cyhigh = (gy * 16 + sub + 16) < 256

    fine(("cxx",), "wait_recv")

    def coarse_unpack(k):
        for p in range(CX):
            col, i = [(0, 3), (1, 0), (1, 1), (1, 2), (1, 3), (2, 0), (2, 1), (2, 2), (2, 3),
                      (3, 0), (3, 1), (3, 2), (3, 3), (4, 0)][p]
            for r, (row, j) in enumerate(((0, 1), (1, 0), (1, 1), (2, 0))):
                m = 2 * i + j
                turned = pltpu.roll(QR[k, col, row], (128 - 16 * m - 8) % 128, 1)
                CO[k, p, 1, pl.ds(8 * r, 8), :] = jnp.where(zmask, turned, 0.0)

    coarse_unpack(1)

    def coarse_weights(p, _):
        at = gx * 4 + p - 5
        scale = jnp.where((at >= 0) & (at < 32), DAMP, 0.0).astype(F32)
        for n, r in enumerate((0, 8, 16, 24)):
            scales = [CO[1, p, t, pl.ds(r, 8), :] for t in range(2)]
            keep_factors((K2, KB, KBV, KA, KAV), p, pl.ds(r, 8), scales, lane, 0.25, 0.5)
            for t in range(2):
                w = scale / (1.05 + 60.0 * scales[t])
                if r == 0:
                    w = jnp.where(cylow, w, 0.0)
                if r == 24:
                    w = jnp.where(cyhigh, w, 0.0)
                if t == 1:
                    w = jnp.where(zmask, w, 0.0)
                CW[p, t, pl.ds(r, 8), :] = w
        return 0

    lax.fori_loop(0, CX, coarse_weights, 0)

    fine(("z", "x", "y", "xz", "yz", "xy", "xyz", "cy", "cx", "cxx"), "wait_send")
    coarse(0, "wait_recv")
    coarse_unpack(0)

    def coarse_first(p, _):
        for r in (0, 8, 16, 24):
            for t in range(2):
                rows = pl.ds(r, 8)
                CA[p, t, rows, :] = CW[p, t, rows, :] * CO[0, p, t, rows, :]
        return 0

    lax.fori_loop(0, CX, coarse_first, 0)

    def coarse_sweep(src, dst, low, high):
        def one(n, _):
            base = low + 2 * n
            for r in (4, 12, 20):
                rows = pl.ds(r, 8)
                whole = stencil(src, (KB, KBV, KA, KAV), base, 2, r, 2, (0, 1), lane, 0.5)
                for k in range(2):
                    p = base + k
                    for t, v, s, b in whole[k]:
                        dst[p, t, rows, :] = 0.4 * v + CW[p, t, rows, :] * (
                            CO[0, p, t, rows, :] + K2[p, t, rows, :] * s + b
                        )
            return 0

        lax.fori_loop(0, (high - low) // 2, one, 0)

    coarse_sweep(CA, CB, 1, 13)
    coarse_sweep(CB, CA, 2, 12)
    coarse_sweep(CA, CB, 3, 11)

    ri = lax.broadcasted_iota(jnp.int32, (128, 256), 0)
    ci = lax.broadcasted_iota(jnp.int32, (128, 256), 1)
    spread = jnp.where(ci // 2 == ri, 1.0, 0.0).astype(F32)
    rh = lax.broadcasted_iota(jnp.int32, (128, 128), 0)
    ch = lax.broadcasted_iota(jnp.int32, (128, 128), 1)
    source = ch // 2 + 64 * gz
    keep = (ch >= zfirst) & (ch < zfirst + 8)
    spread_h = jnp.where((source == rh) & keep, 1.0, 0.0).astype(F32)
    mine = jnp.concatenate([CB[3 + q, 0, pl.ds(4, 24), :] for q in range(8)], axis=0)
    other = jnp.concatenate([CB[3 + q, 1, pl.ds(4, 24), :] for q in range(8)], axis=0)
    wide = jnp.dot(mine, spread, preferred_element_type=F32, precision=lax.Precision.HIGHEST)
    wide_h = jnp.dot(other, spread_h, preferred_element_type=F32, precision=lax.Precision.HIGHEST)
    for q in range(8):
        for t in range(3):
            part = (wide[24 * q : 24 * q + 24, 128 * t : 128 * t + 128] if t < 2
                    else wide_h[24 * q : 24 * q + 24])
            UPS[q, t, pl.ds(0, 24, stride=2), :] = part
            UPS[q, t, pl.ds(1, 24, stride=2), :] = part

    fine(("s",), "wait_send")
    fine(("s",), "wait_recv")

    def spread_edge(side, first):
        for n in range(2):
            for j, r in enumerate(starts):
                turned = pltpu.roll(SR[side, n], (128 - 16 * j - 8) % 128, 1)
                B[first + n, 2, pl.ds(r, 8), :] = jnp.where(zmask, turned, 0.0)

    @pl.when(gx > 0)
    def _():
        spread_edge(0, 2)

    @pl.when(gx < NXD - 1)
    def _():
        spread_edge(1, 14)

    def add_up(q, _):
        for half in range(2):
            for r in range(6):
                for t in range(3):
                    rows = pl.ds(8 * r, 8)
                    p = 2 * q + 1 + half
                    A[p, t, rows, :] = B[p, t, rows, :] + UPS[q, t, rows, :]
        return 0

    lax.fori_loop(0, 8, add_up, 0)

    fine_sweep(A, B, 3, 15, 3)
    fine_sweep(B, A, 4, 14, 5)

    def finish(n, _):
        both = fine_residue(A, 5 + 2 * n, 2)
        for k in range(2):
            x = 2 * n + k
            for i in range(8):
                t, r = i % 2, 8 * (i // 2)
                res_ref[x, pl.ds(r, 8), pl.ds(128 * t, 128)] = both[k][i]
                sol_ref[x, pl.ds(r, 8), pl.ds(128 * t, 128)] = A[5 + x, t, pl.ds(8 + r, 8), :]
        return 0

    lax.fori_loop(0, 4, finish, 0)

    coarse(0, "wait_send")


def on_device(right_side, volscale):
    shape = pltpu.VMEM(right_side.shape, F32)
    fine = pltpu.VMEM((PX, 3, ROWS, 128), F32)
    coarse = pltpu.VMEM((CX, 2, CROWS, 128), F32)
    any_space = pl.BlockSpec(memory_space=pl.ANY)
    return pl.pallas_call(
        kernel,
        out_shape=(shape, shape),
        in_specs=[any_space] * 2,
        out_specs=(pl.BlockSpec(memory_space=pltpu.VMEM),) * 2,
        scratch_shapes=[
            pltpu.VMEM((2, PX, 3, ROWS, 128), F32),
            pltpu.VMEM((8, 8, 128), F32),
            pltpu.VMEM((3, PX, 8, 128), F32),
            pltpu.VMEM((2, 2, 8, 128), F32),
            pltpu.VMEM((2, 2, 8, 128), F32),
            *[fine] * 8,
            pltpu.VMEM((4, 2, 32, 128), F32),
            pltpu.VMEM((2, CX, 2, CROWS, 128), F32),
            pltpu.VMEM((2, 8, 128), F32),
            pltpu.VMEM((2, 5, 3, 8, 128), F32),
            *[coarse] * 8,
            pltpu.VMEM((8, 3, ROWS, 128), F32),
            pltpu.SemaphoreType.DMA((4,)),
            pltpu.SemaphoreType.DMA((NF,)),
            pltpu.SemaphoreType.DMA((NF,)),
            pltpu.SemaphoreType.DMA((NC,)),
            pltpu.SemaphoreType.DMA((NC,)),
        ],
        compiler_params=pltpu.CompilerParams(collective_id=0, has_side_effects=True),
    )(right_side, volscale)


def solution(mesh):
    placed = (P("gx", "gy", "gz"), P("gx", "gy", "gz"))
    return jax.shard_map(
        on_device,
        mesh=mesh,
        in_specs=placed,
        out_specs=(P("gx", "gy", "gz"), P("gx", "gy", "gz")),
        check_vma=False,
    )
```

```python
import jax
import jax.numpy as jnp
from jax import lax
from jax.experimental import pallas as pl
from jax.experimental.pallas import tpu as pltpu
from jax.sharding import PartitionSpec as P

MESH = pl.DeviceIdType.MESH
F32 = jnp.float32
NXD, NYD = 8, 16
BX, BY = 8, 32
HALO = 5
PX = BX + 2 * HALO
ROWS = BY + 16
CX = BX // 2 + 2 * HALO
CROWS = BY // 2 + 16
DAMP = 0.6


def fine_messages():
    lo, mid, hi = (3, 5), (8, 32), (40, 5)
    every = (0, 3)
    out = [
        ("z", 0, 0, 1, ("PS",), ("PR", (1, 1), (5, 8), (0, 8))),
        ("z", 0, 0, 1, ("QS", 1), ("QR", 2, (1, 1), (0, 8))),
    ]
    for dx in (1, -1):
        side, far = 2 - dx, 2 - 2 * dx
        sg, dg = ((10, 3), (2, 3)) if dx == 1 else ((5, 3), (13, 3))
        sc, dc = ((11, 2), (3, 2)) if dx == 1 else ((5, 2), (13, 2))
        out.append(("x", dx, 0, 0, ("GC", 0, sg, (3, 42)), ("GC", 0, dg, (3, 42))))
        out.append(("x", dx, 0, 0, ("GC", 1, sc, (3, 42)), ("GC", 1, dc, (3, 42))))
        out.append(("xz", dx, 0, 0, ("PR", (1, 1), sg, (0, 8)), ("PR", (1, 1), dg, (0, 8))))
        for rows in (lo, hi):
            pass
        for slot, rows in ((0, (3, 5)), (2, (0, 5))):
            out.append(("xyz", dx, 0, 0, ("PR", (slot, 1), sg, rows), ("PR", (slot, 1), dg, rows)))
        out.append(("cx", dx, 0, 0, ("CO", (5, 4), (3, 26)), ("CO", (1 if dx == 1 else 9, 4), (3, 26))))
        out.append(("cx", dx, 0, 0, ("QR", 2, every, (0, 8)), ("QR", side, every, (0, 8))))
        near, last = (4, 0) if dx == 1 else (9, 13)
        out.append(("cxx", dx, 0, 0, ("CO", (near, 1), (3, 26)), ("CO", (last, 1), (3, 26))))
        out.append(("cxx", dx, 0, 0, ("QR", side, every, (0, 8)), ("QR", far, every, (0, 8))))
        sb, db = ((10, 2), (2, 2)) if dx == 1 else ((6, 2), (14, 2))
        out.append(("s", dx, 0, 0, ("B", sb), ("B", db)))
        out.append(("s", dx, 0, 0, ("SS", (1 - dx) // 2), ("SR", (1 - dx) // 2)))
    for dy in (1, -1):
        rs, rd, pr = ((35, 5), lo, (3, 5)) if dy == 1 else ((8, 5), hi, (0, 5))
        cs, cd = ((19, 5), (3, 5)) if dy == 1 else ((8, 5), (24, 5))
        out.append(("y", 0, dy, 0, ("GC", 0, (5, 8), rs), ("GC", 0, (5, 8), rd)))
        out.append(("y", 0, dy, 0, ("GC", 1, (5, 8), rs), ("GC", 1, (5, 8), rd)))
        out.append(("yz", 0, dy, 0, ("PR", (1, 1), (5, 8), pr), ("PR", (1 - dy, 1), (5, 8), pr)))
        out.append(("cy", 0, dy, 0, ("CO", (5, 4), cs), ("CO", (5, 4), cd)))
        out.append(("cy", 0, dy, 0, ("QR", 2, (1, 1), pr), ("QR", 2, (1 - dy, 1), pr)))
    return out


def coarse_messages():
    out = []
    for dx in (2, 1, 0, -1, -2):
        for dy in (1, 0, -1):
            ps, pd = {
                0: ((5, 4), (5, 4)),
                1: ((5, 4), (1, 4)),
                -1: ((5, 4), (9, 4)),
                2: ((8, 1), (0, 1)),
                -2: ((5, 1), (13, 1)),
            }[dx]
            rs, rd = {0: ((8, 16), (8, 16)), 1: ((19, 5), (3, 5)), -1: ((8, 5), (24, 5))}[dy]
            if (dx, dy) != (0, 0):
                out.append((dx, dy, 0, ps, pd, rs, rd))
            out.append((dx, dy, 1, None, None, {0: (0, 8), 1: (3, 5), -1: (0, 5)}[dy], None))
    return out


FINE = fine_messages()
COARSE = coarse_messages()
NF, NC = len(FINE), len(COARSE)


def ds(pair):
    return pl.ds(pair[0], pair[1])


def up(x):
    return pltpu.roll(x, 127, 1)


def down(x):
    return pltpu.roll(x, 1, 1)


RATIO = 64.0 / 3.0


def stencil(ref, factors, base, count, r, tiles, outs, lane, bf):
    before, before_v, after, after_v = factors
    rows = pl.ds(r, 8)
    parts = []
    for k in range(count):
        parts.append(([], [], [], [], []))
    for t in range(tiles):
        vs = [ref[base - 1 + k, t, rows, :] for k in range(count + 2)]
        fys = []
        for k in range(count + 2):
            if t in outs or 0 < k <= count:
                fys.append(
                    ref[base - 1 + k, t, pl.ds(r + 1, 8), :]
                    - ref[base - 1 + k, t, pl.ds(r - 1, 8), :]
                )
            else:
                fys.append(None)
        for k in range(count):
            centre, straight, drift, plus, minus = parts[k]
            p = base + k
            v, xm, xp, fy = vs[k + 1], vs[k], vs[k + 2], fys[k + 1]
            d = xp - xm
            m = d - fy
            plus.append(before_v[p, t, rows, :] * v + before[p, t, rows, :] * m)
            minus.append(after_v[p, t, rows, :] * v - after[p, t, rows, :] * m)
            centre.append(v)
            if t in outs:
                sy = ref[p, t, pl.ds(r + 1, 8), :] + ref[p, t, pl.ds(r - 1, 8), :]
                straight.append(24.0 * (xp + xm) + 20.0 * sy + (fys[k + 2] - fys[k]))
                drift.append((1.5 * bf) * d - (fy if bf == 1.0 else bf * fy))
            else:
                straight.append(None)
                drift.append(None)
    result = []
    for k in range(count):
        centre, straight, drift, plus, minus = parts[k]
        one = []
        for t in outs:
            b = (
                drift[t]
                + up(jnp.where(lane == 0, plus[(t + 1) % tiles], plus[t]))
                + down(jnp.where(lane == 127, minus[t - 1], minus[t]))
            )
            one.append((t, centre[t], straight[t], b))
        result.append(one)
    return result


def keep_factors(stores, p, rows, scales, lane, sf, bf):
    double, before, before_v, after, after_v = stores
    low, high = shifted_scales([(1.5 * sf) * c for c in scales], lane)
    for t in range(len(scales)):
        double[p, t, rows, :] = (2.0 * sf) * scales[t]
        before[p, t, rows, :] = low[t]
        before_v[p, t, rows, :] = RATIO * low[t] + 0.75 * bf
        after[p, t, rows, :] = high[t]
        after_v[p, t, rows, :] = RATIO * high[t] - 0.75 * bf


def shifted_scales(values, lane):
    count = len(values)
    before = [down(jnp.where(lane == 127, values[t - 1], values[t])) for t in range(count)]
    after = [up(jnp.where(lane == 0, values[(t + 1) % count], values[t])) for t in range(count)]
    return before, after


def kernel(g_hbm, c_hbm, sol_ref, res_ref, GC, PS, PR, SS, SR, W, F2, FB, FBV, FA, FAV, A, B, RX, CO, QS, QR,
           CW, K2, KB, KBV, KA, KAV, CA, CB, UPS, load_sem, f_send, f_recv, c_send, c_recv):
    gx, gy, gz = lax.axis_index("gx"), lax.axis_index("gy"), lax.axis_index("gz")

    def peer(dx, dy, dz):
        return (gx + dx, gy + dy, lax.rem(gz + dz, 2))

    def inside(dx, dy):
        tests = []
        if dx > 0:
            tests.append(gx < NXD - dx)
        if dx < 0:
            tests.append(gx >= -dx)
        if dy > 0:
            tests.append(gy < NYD - dy)
        if dy < 0:
            tests.append(gy >= -dy)
        if not tests:
            return None
        return tests[0] if len(tests) == 1 else tests[0] & tests[1]

    def guarded(dx, dy, act):
        test = inside(dx, dy)
        if test is None:
            act()
        else:
            pl.when(test)(act)

    loads = []
    for a, src in ((0, g_hbm), (1, c_hbm)):
        for t in range(2):
            cp = pltpu.make_async_copy(
                src.at[:, :, pl.ds(128 * t, 128)],
                GC.at[a, pl.ds(5, 8), t, pl.ds(8, 32), :],
                load_sem.at[2 * a + t],
            )
            cp.start()
            loads.append(cp)

    barrier = pltpu.get_barrier_semaphore()
    partners = 1
    for dx, dy, dz in ((1, 0, 0), (-1, 0, 0), (0, 1, 0), (0, -1, 0), (0, 0, 1)):

        def greet():
            pl.semaphore_signal(barrier, inc=1, device_id=peer(dx, dy, dz), device_id_type=MESH)

        guarded(dx, dy, greet)
        if not dz:
            partners = partners + jnp.where(inside(dx, dy), 1, 0)

    lane = lax.broadcasted_iota(jnp.int32, (8, 128), 1)
    sub = lax.broadcasted_iota(jnp.int32, (8, 128), 0)
    zfirst = 120 * gz
    zmask = (lane >= zfirst) & (lane < zfirst + 8)
    blank = jnp.zeros((8, 128), F32)

    def clear_fine(low, high, rows):
        def one(p, _):
            for a in range(2):
                for t in range(2):
                    for r in rows:
                        GC[a, p, t, pl.ds(r, 8), :] = blank
            return 0
        lax.fori_loop(low, high, one, 0)

    def clear_pack(slots, low, high):
        def one(p, _):
            for n in slots:
                PR[n, p] = blank
            return 0
        lax.fori_loop(low, high, one, 0)

    def clear_coarse(k, low, high, rows):
        def one(p, _):
            for r in rows:
                CO[k, p, 0, pl.ds(r, 8), :] = blank
            return 0
        lax.fori_loop(low, high, one, 0)

    def clear_edge(k, cols, rows):
        for n in cols:
            for m in rows:
                QR[k, n, m] = blank

    def clear_smooth(low):
        for p in (low, low + 1):
            for t in range(3):
                for r in (0, 8, 16, 24, 32, 40):
                    B[p, t, pl.ds(r, 8), :] = blank

    all_rows = (0, 8, 16, 24, 32, 40)
    coarse_rows = (0, 8, 16, 24)
    slots = (0, 1, 2)

    @pl.when(gx == 0)
    def _():
        clear_fine(2, 5, all_rows)
        clear_pack(slots, 2, 5)
        for k in range(2):
            clear_coarse(k, 0, 5, coarse_rows)
            clear_edge(k, (0, 1), slots)
        clear_smooth(2)

    @pl.when(gx == 1)
    def _():
        clear_coarse(0, 0, 1, coarse_rows)
        clear_edge(0, (0,), slots)

    @pl.when(gx == NXD - 1)
    def _():
        clear_fine(13, 16, all_rows)
        clear_pack(slots, 13, 16)
        for k in range(2):
            clear_coarse(k, 9, 14, coarse_rows)
            clear_edge(k, (3, 4), slots)
        clear_smooth(14)

    @pl.when(gx == NXD - 2)
    def _():
        clear_coarse(0, 13, 14, coarse_rows)
        clear_edge(0, (4,), slots)

    @pl.when(gy == 0)
    def _():
        clear_fine(5, 13, (0,))
        clear_pack((0,), 5, 13)
        clear_coarse(0, 0, 14, (0,))
        clear_coarse(1, 5, 9, (0,))
        clear_edge(0, (0, 1, 2, 3, 4), (0,))
        clear_edge(1, (2,), (0,))

    @pl.when(gy == NYD - 1)
    def _():
        clear_fine(5, 13, (40,))
        clear_pack((2,), 5, 13)
        clear_coarse(0, 0, 14, (24,))
        clear_coarse(1, 5, 9, (24,))
        clear_edge(0, (0, 1, 2, 3, 4), (2,))
        clear_edge(1, (2,), (2,))

    for cp in loads:
        cp.wait()

    def pack_plane(x, _):
        acc = blank
        for a in range(2):
            for j in range(4):
                m = 4 * a + j
                t0 = GC[a, 5 + x, 0, pl.ds(8 + 8 * j, 8), :]
                t1 = GC[a, 5 + x, 1, pl.ds(8 + 8 * j, 8), :]
                both = pltpu.roll(jnp.where(lane >= 64, t1, t0), (16 * m + 8) % 128, 1)
                acc = jnp.where((lane >= 16 * m) & (lane < 16 * m + 16), both, acc)
        PS[x] = acc
        return 0

    lax.fori_loop(0, 8, pack_plane, 0)

    row_i = lax.broadcasted_iota(jnp.int32, (256, 128), 0)
    col_i = lax.broadcasted_iota(jnp.int32, (256, 128), 1)
    pool = jnp.where(row_i // 2 == col_i, 0.125, 0.0).astype(F32)

    def coarsen_rows(k):
        pieces = []
        for i in range(4):
            cols = []
            for t in range(2):
                cols.append(RX[i, t, pl.ds(0, 16, stride=2), :] + RX[i, t, pl.ds(1, 16, stride=2), :])
            pieces.append(jnp.concatenate(cols, axis=1))
        allp = jnp.concatenate(pieces, axis=0)
        q = jnp.dot(allp, pool, preferred_element_type=F32, precision=lax.Precision.HIGHEST)
        acc = blank
        for i in range(4):
            CO[k, 5 + i, 0, pl.ds(8, 16), :] = q[16 * i : 16 * i + 16]
            for j in range(2):
                m = 2 * i + j
                turned = pltpu.roll(q[8 * m : 8 * m + 8], (16 * m + 8) % 128, 1)
                acc = jnp.where((lane >= 16 * m) & (lane < 16 * m + 16), turned, acc)
        QS[k] = acc

    def pair_scale(i, _):
        for t in range(2):
            RX[i, t] = GC[1, 5 + 2 * i, t, pl.ds(8, 32), :] + GC[1, 6 + 2 * i, t, pl.ds(8, 32), :]
        return 0

    lax.fori_loop(0, 4, pair_scale, 0)
    coarsen_rows(1)

    starts = [4, 12, 20, 28, 36]
    ylow = (gy * 32 + sub - 4) >= 0
    yhigh = (gy * 32 + sub + 28) < 512

    def place(where):
        kind = where[0]
        if kind == "PS":
            return PS.at[pl.ds(0, 8)]
        if kind == "PR":
            slot, planes, rows = where[1:]
            return PR.at[slot[0], ds(planes), ds(rows), :]
        if kind == "QS":
            return QS.at[where[1]]
        if kind == "QR":
            col, rows, subs = where[1:]
            if rows[1] == 1:
                return QR.at[1, col, rows[0], ds(subs), :]
            return QR.at[1, col, ds(rows), ds(subs), :]
        if kind == "CO":
            return CO.at[1, ds(where[1]), 0, ds(where[2]), :]
        if kind == "B":
            return B.at[ds(where[1]), pl.ds(0, 2), pl.ds(4, 40), :]
        if kind == "SS":
            return SS.at[where[1]]
        if kind == "SR":
            return SR.at[where[1]]
        return GC.at[where[1], ds(where[2]), pl.ds(0, 2), ds(where[3]), :]

    def fine_copy(i):
        _, dx, dy, dz, src, dst = FINE[i]
        return pltpu.make_async_remote_copy(
            src_ref=place(src),
            dst_ref=place(dst),
            send_sem=f_send.at[i],
            recv_sem=f_recv.at[i],
            device_id=peer(dx, dy, dz),
            device_id_type=MESH,
        )

    def coarse_copy(k, i):
        dx, dy, dz, ps, pd, rs, rd = COARSE[i]
        if dz:
            src, dst = QS.at[k, ds(rs), :], QR.at[k, 2 - dx, 1 - dy, ds(rs), :]
        else:
            src, dst = CO.at[k, ds(ps), 0, ds(rs), :], CO.at[k, ds(pd), 0, ds(rd), :]
        return pltpu.make_async_remote_copy(
            src_ref=src,
            dst_ref=dst,
            send_sem=c_send.at[i],
            recv_sem=c_recv.at[i],
            device_id=peer(dx, dy, dz),
            device_id_type=MESH,
        )

    FAR = [(2, 1), (2, -1), (-2, 1), (-2, -1), (1, 1), (1, -1), (-1, 1), (-1, -1),
           (2, 0), (-2, 0), (1, 0), (-1, 0), (0, 1), (0, -1), (0, 0)]
    NEAR = [(1, 0), (-1, 0), (0, 1), (0, -1), (0, 0)]

    def run(direction, copies, method, back):
        if copies:
            dx, dy = direction
            def act():
                for cp in copies:
                    getattr(cp, method)()
            guarded(-dx if back else dx, -dy if back else dy, act)

    def fine(phase, method):
        for d in NEAR:
            run(d, [fine_copy(i) for i in range(NF) if FINE[i][0] in phase and FINE[i][1:3] == d],
                method, method == "wait_recv")

    def coarse(k, method):
        for d in FAR:
            run(d, [coarse_copy(k, i) for i in range(NC) if COARSE[i][:2] == d],
                method, method == "wait_recv")

    pl.semaphore_wait(barrier, partners)

    fine(("z",), "start")
    fine(("y",), "start")

    def unpack(low, high):
        def unpack_plane(p, _):
            for a in range(2):
                for r in range(6):
                    slot, j = (0, 3) if r == 0 else (2, 0) if r == 5 else (1, r - 1)
                    m = 4 * a + j
                    v = pltpu.roll(PR[slot, p], (128 - 16 * m - 8) % 128, 1)
                    GC[a, p, 2, pl.ds(8 * r, 8), :] = jnp.where(zmask, v, 0.0)
            return 0

        lax.fori_loop(low, high, unpack_plane, 0)

    def weights(low, high):
        def one(p, _):
            at = gx * 8 + p - 5
            scale = jnp.where((at >= 0) & (at < 64), DAMP, 0.0).astype(F32)
            for r in starts:
                scales = [GC[1, p, t, pl.ds(r, 8), :] for t in range(3)]
                keep_factors((F2, FB, FBV, FA, FAV), p, pl.ds(r, 8), scales, lane, 1.0, 1.0)
                for t in range(3):
                    w = scale / (1.05 + 240.0 * scales[t])
                    if r == 4:
                        w = jnp.where(ylow, w, 0.0)
                    if r == 36:
                        w = jnp.where(yhigh, w, 0.0)
                    if t == 2:
                        w = jnp.where(zmask, w, 0.0)
                    W[p, t, pl.ds(r, 8), :] = w
            return 0

        lax.fori_loop(low, high, one, 0)

    fine_factors = (FB, FBV, FA, FAV)

    def fine_planes(view, dst, base, count):
        for r in starts:
            rows = pl.ds(r, 8)
            whole = stencil(view, fine_factors, base, count, r, 3, (0, 1, 2), lane, 1.0)
            for k in range(count):
                p = base + k
                for t, v, s, b in whole[k]:
                    dst[p, t, rows, :] = 0.4 * v + W[p, t, rows, :] * (
                        GC[0, p, t, rows, :] + F2[p, t, rows, :] * s + b
                    )

    def fine_sweep(src, dst, low, high, step, src_index=None):
        view = src if src_index is None else src.at[src_index]

        def one(n, _):
            fine_planes(view, dst, low + step * n, step)
            return 0

        lax.fori_loop(0, (high - low) // step, one, 0)

    def fine_sides(src, dst, low, high, count, src_index=None):
        view = src if src_index is None else src.at[src_index]

        def one(n, _):
            fine_planes(view, dst, low + (high - low) * n, count)
            return 0

        lax.fori_loop(0, 2, one, 0)

    def fine_residue(src, base, count):
        out = [[] for _ in range(count)]
        for r in (8, 16, 24, 32):
            rows = pl.ds(r, 8)
            whole = stencil(src, fine_factors, base, count, r, 3, (0, 1), lane, 1.0)
            for k in range(count):
                p = base + k
                for t, v, s, b in whole[k]:
                    out[k].append(
                        GC[0, p, t, rows, :] - 1.05 * v + F2[p, t, rows, :] * (s - 120.0 * v) + b
                    )
        return out

    fine(("z",), "wait_recv")
    fine(("yz", "xz"), "start")
    fine(("cy",), "start")
    fine(("y",), "wait_recv")
    fine(("x",), "start")
    fine(("yz",), "wait_recv")
    fine(("xyz",), "start")
    unpack(5, 13)
    weights(5, 13)
    fine_sweep(GC, A, 6, 12, 3, 0)
    fine_sweep(A, B, 7, 11, 2)
    fine(("cy",), "wait_recv")
    fine(("cx",), "start")
    fine(("x", "xz", "xy", "xyz"), "wait_recv")
    unpack(2, 5)
    unpack(13, 16)
    weights(3, 5)
    weights(13, 15)
    fine_sides(GC, A, 3, 12, 3, 0)
    fine(("cx",), "wait_recv")
    fine(("cxx",), "start")
    fine_sides(A, B, 4, 11, 3)

    def residue_pair(i, _):
        one, two = fine_residue(B, 5 + 2 * i, 2)
        for n in range(8):
            RX[i, n % 2, pl.ds(8 * (n // 2), 8), :] = one[n] + two[n]
        return 0

    lax.fori_loop(0, 4, residue_pair, 0)
    coarsen_rows(0)

    coarse(0, "start")

    for side in range(2):
        for n in range(2):
            p = (10 if side == 0 else 6) + n
            acc = blank
            for j, r in enumerate(starts):
                turned = pltpu.roll(B[p, 2, pl.ds(r, 8), :], (16 * j + 8) % 128, 1)
                acc = jnp.where((lane >= 16 * j) & (lane < 16 * j + 16), turned, acc)
            SS[side, n] = acc
    fine(("s",), "start")

    cylow = (gy * 16 + sub - 8) >= 0
    cyhigh = (gy * 16 + sub + 16) < 256

    fine(("cxx",), "wait_recv")

    def coarse_unpack(k):
        for p in range(CX):
            col, i = [(0, 3), (1, 0), (1, 1), (1, 2), (1, 3), (2, 0), (2, 1), (2, 2), (2, 3),
                      (3, 0), (3, 1), (3, 2), (3, 3), (4, 0)][p]
            for r, (row, j) in enumerate(((0, 1), (1, 0), (1, 1), (2, 0))):
                m = 2 * i + j
                turned = pltpu.roll(QR[k, col, row], (128 - 16 * m - 8) % 128, 1)
                CO[k, p, 1, pl.ds(8 * r, 8), :] = jnp.where(zmask, turned, 0.0)

    coarse_unpack(1)

    def coarse_weights(p, _):
        at = gx * 4 + p - 5
        scale = jnp.where((at >= 0) & (at < 32), DAMP, 0.0).astype(F32)
        for n, r in enumerate((0, 8, 16, 24)):
            scales = [CO[1, p, t, pl.ds(r, 8), :] for t in range(2)]
            keep_factors((K2, KB, KBV, KA, KAV), p, pl.ds(r, 8), scales, lane, 0.25, 0.5)
            for t in range(2):
                w = scale / (1.05 + 60.0 * scales[t])
                if r == 0:
                    w = jnp.where(cylow, w, 0.0)
                if r == 24:
                    w = jnp.where(cyhigh, w, 0.0)
                if t == 1:
                    w = jnp.where(zmask, w, 0.0)
                CW[p, t, pl.ds(r, 8), :] = w
        return 0

    lax.fori_loop(0, CX, coarse_weights, 0)

    fine(("z", "x", "y", "xz", "yz", "xy", "xyz", "cy", "cx", "cxx"), "wait_send")
    coarse(0, "wait_recv")
    coarse_unpack(0)

    def coarse_first(p, _):
        for r in (0, 8, 16, 24):
            for t in range(2):
                rows = pl.ds(r, 8)
                CA[p, t, rows, :] = CW[p, t, rows, :] * CO[0, p, t, rows, :]
        return 0

    lax.fori_loop(0, CX, coarse_first, 0)

    def coarse_sweep(src, dst, low, high):
        def one(n, _):
            base = low + 2 * n
            for r in (4, 12, 20):
                rows = pl.ds(r, 8)
                whole = stencil(src, (KB, KBV, KA, KAV), base, 2, r, 2, (0, 1), lane, 0.5)
                for k in range(2):
                    p = base + k
                    for t, v, s, b in whole[k]:
                        dst[p, t, rows, :] = 0.4 * v + CW[p, t, rows, :] * (
                            CO[0, p, t, rows, :] + K2[p, t, rows, :] * s + b
                        )
            return 0

        lax.fori_loop(0, (high - low) // 2, one, 0)

    coarse_sweep(CA, CB, 1, 13)
    coarse_sweep(CB, CA, 2, 12)
    coarse_sweep(CA, CB, 3, 11)

    ri = lax.broadcasted_iota(jnp.int32, (128, 256), 0)
    ci = lax.broadcasted_iota(jnp.int32, (128, 256), 1)
    spread = jnp.where(ci // 2 == ri, 1.0, 0.0).astype(F32)
    rh = lax.broadcasted_iota(jnp.int32, (128, 128), 0)
    ch = lax.broadcasted_iota(jnp.int32, (128, 128), 1)
    source = ch // 2 + 64 * gz
    keep = (ch >= zfirst) & (ch < zfirst + 8)
    spread_h = jnp.where((source == rh) & keep, 1.0, 0.0).astype(F32)
    mine = jnp.concatenate([CB[3 + q, 0, pl.ds(4, 24), :] for q in range(8)], axis=0)
    other = jnp.concatenate([CB[3 + q, 1, pl.ds(4, 24), :] for q in range(8)], axis=0)
    wide = jnp.dot(mine, spread, preferred_element_type=F32, precision=lax.Precision.HIGHEST)
    wide_h = jnp.dot(other, spread_h, preferred_element_type=F32, precision=lax.Precision.HIGHEST)
    for q in range(8):
        for t in range(3):
            part = (wide[24 * q : 24 * q + 24, 128 * t : 128 * t + 128] if t < 2
                    else wide_h[24 * q : 24 * q + 24])
            UPS[q, t, pl.ds(0, 24, stride=2), :] = part
            UPS[q, t, pl.ds(1, 24, stride=2), :] = part

    fine(("s",), "wait_send")
    fine(("s",), "wait_recv")

    def spread_edge(side, first):
        for n in range(2):
            for j, r in enumerate(starts):
                turned = pltpu.roll(SR[side, n], (128 - 16 * j - 8) % 128, 1)
                B[first + n, 2, pl.ds(r, 8), :] = jnp.where(zmask, turned, 0.0)

    @pl.when(gx > 0)
    def _():
        spread_edge(0, 2)

    @pl.when(gx < NXD - 1)
    def _():
        spread_edge(1, 14)

    def add_up(q, _):
        for half in range(2):
            for r in range(6):
                for t in range(3):
                    rows = pl.ds(8 * r, 8)
                    p = 2 * q + 1 + half
                    A[p, t, rows, :] = B[p, t, rows, :] + UPS[q, t, rows, :]
        return 0

    lax.fori_loop(0, 8, add_up, 0)

    fine_sweep(A, B, 3, 15, 3)
    fine_sweep(B, A, 4, 14, 5)

    def finish(n, _):
        both = fine_residue(A, 5 + 2 * n, 2)
        for k in range(2):
            x = 2 * n + k
            for i in range(8):
                t, r = i % 2, 8 * (i // 2)
                res_ref[x, pl.ds(r, 8), pl.ds(128 * t, 128)] = both[k][i]
                sol_ref[x, pl.ds(r, 8), pl.ds(128 * t, 128)] = A[5 + x, t, pl.ds(8 + r, 8), :]
        return 0

    lax.fori_loop(0, 4, finish, 0)

    coarse(0, "wait_send")


def closing(sol_ref, res_ref, sol_hbm, res_hbm, sems):
    copies = [
        pltpu.make_async_copy(sol_ref, sol_hbm, sems.at[0]),
        pltpu.make_async_copy(res_ref, res_hbm, sems.at[1]),
    ]
    for cp in copies:
        cp.start()
    for cp in copies:
        cp.wait()


def on_device(right_side, volscale):
    shape = pltpu.VMEM(right_side.shape, F32)
    fine = pltpu.VMEM((PX, 3, ROWS, 128), F32)
    coarse = pltpu.VMEM((CX, 2, CROWS, 128), F32)
    any_space = pl.BlockSpec(memory_space=pl.ANY)
    sol, res = pl.pallas_call(
        kernel,
        out_shape=(shape, shape),
        in_specs=[any_space] * 2,
        out_specs=(pl.BlockSpec(memory_space=pltpu.VMEM),) * 2,
        scratch_shapes=[
            pltpu.VMEM((2, PX, 3, ROWS, 128), F32),
            pltpu.VMEM((8, 8, 128), F32),
            pltpu.VMEM((3, PX, 8, 128), F32),
            pltpu.VMEM((2, 2, 8, 128), F32),
            pltpu.VMEM((2, 2, 8, 128), F32),
            *[fine] * 8,
            pltpu.VMEM((4, 2, 32, 128), F32),
            pltpu.VMEM((2, CX, 2, CROWS, 128), F32),
            pltpu.VMEM((2, 8, 128), F32),
            pltpu.VMEM((2, 5, 3, 8, 128), F32),
            *[coarse] * 8,
            pltpu.VMEM((8, 3, ROWS, 128), F32),
            pltpu.SemaphoreType.DMA((4,)),
            pltpu.SemaphoreType.DMA((NF,)),
            pltpu.SemaphoreType.DMA((NF,)),
            pltpu.SemaphoreType.DMA((NC,)),
            pltpu.SemaphoreType.DMA((NC,)),
        ],
        compiler_params=pltpu.CompilerParams(collective_id=0, has_side_effects=True),
    )(right_side, volscale)
    plain = jax.ShapeDtypeStruct(right_side.shape, F32)
    in_vmem = pl.BlockSpec(memory_space=pltpu.VMEM)
    sol = pltpu.with_memory_space_constraint(sol, pltpu.VMEM)
    res = pltpu.with_memory_space_constraint(res, pltpu.VMEM)
    return pl.pallas_call(
        closing,
        out_shape=(plain, plain),
        in_specs=[in_vmem] * 2,
        out_specs=(any_space, any_space),
        scratch_shapes=[pltpu.SemaphoreType.DMA((2,))],
        compiler_params=pltpu.CompilerParams(vmem_limit_bytes=1 << 20),
    )(sol, res)


def solution(mesh):
    placed = (P("gx", "gy", "gz"), P("gx", "gy", "gz"))
    return jax.shard_map(
        on_device,
        mesh=mesh,
        in_specs=placed,
        out_specs=(P("gx", "gy", "gz"), P("gx", "gy", "gz")),
        check_vma=False,
    )
```

```python
import jax
import jax.numpy as jnp
from jax import lax
from jax.experimental import pallas as pl
from jax.experimental.pallas import tpu as pltpu
from jax.sharding import PartitionSpec as P

MESH = pl.DeviceIdType.MESH
F32 = jnp.float32
NXD, NYD = 8, 16
BX, BY = 8, 32
HALO = 5
PX = BX + 2 * HALO
ROWS = BY + 16
CX = BX // 2 + 2 * HALO
CROWS = BY // 2 + 16
DAMP = 0.6


def fine_messages():
    lo, mid, hi = (3, 5), (8, 32), (40, 5)
    every = (0, 3)
    out = [
        ("z", 0, 0, 1, ("PS",), ("PR", (1, 1), (5, 8), (0, 8))),
        ("z", 0, 0, 1, ("QS", 1), ("QR", 2, (1, 1), (0, 8))),
    ]
    for dx in (1, -1):
        side, far = 2 - dx, 2 - 2 * dx
        sg, dg = ((10, 3), (2, 3)) if dx == 1 else ((5, 3), (13, 3))
        sc, dc = ((11, 2), (3, 2)) if dx == 1 else ((5, 2), (13, 2))
        out.append(("x", dx, 0, 0, ("GC", 0, sg, (3, 42)), ("GC", 0, dg, (3, 42))))
        out.append(("x", dx, 0, 0, ("GC", 1, sc, (3, 42)), ("GC", 1, dc, (3, 42))))
        out.append(("xz", dx, 0, 0, ("PR", (1, 1), sg, (0, 8)), ("PR", (1, 1), dg, (0, 8))))
        for rows in (lo, hi):
            pass
        for slot, rows in ((0, (3, 5)), (2, (0, 5))):
            out.append(("xyz", dx, 0, 0, ("PR", (slot, 1), sg, rows), ("PR", (slot, 1), dg, rows)))
        out.append(("cx", dx, 0, 0, ("CO", (5, 4), (3, 26)), ("CO", (1 if dx == 1 else 9, 4), (3, 26))))
        out.append(("cx", dx, 0, 0, ("QR", 2, every, (0, 8)), ("QR", side, every, (0, 8))))
        near, last = (4, 0) if dx == 1 else (9, 13)
        out.append(("cxx", dx, 0, 0, ("CO", (near, 1), (3, 26)), ("CO", (last, 1), (3, 26))))
        out.append(("cxx", dx, 0, 0, ("QR", side, every, (0, 8)), ("QR", far, every, (0, 8))))
        sb, db = ((10, 2), (2, 2)) if dx == 1 else ((6, 2), (14, 2))
        out.append(("s", dx, 0, 0, ("B", sb), ("B", db)))
        out.append(("s", dx, 0, 0, ("SS", (1 - dx) // 2), ("SR", (1 - dx) // 2)))
    for dy in (1, -1):
        rs, rd, pr = ((35, 5), lo, (3, 5)) if dy == 1 else ((8, 5), hi, (0, 5))
        cs, cd = ((19, 5), (3, 5)) if dy == 1 else ((8, 5), (24, 5))
        out.append(("y", 0, dy, 0, ("GC", 0, (5, 8), rs), ("GC", 0, (5, 8), rd)))
        out.append(("y", 0, dy, 0, ("GC", 1, (5, 8), rs), ("GC", 1, (5, 8), rd)))
        out.append(("yz", 0, dy, 0, ("PR", (1, 1), (5, 8), pr), ("PR", (1 - dy, 1), (5, 8), pr)))
        out.append(("cy", 0, dy, 0, ("CO", (5, 4), cs), ("CO", (5, 4), cd)))
        out.append(("cy", 0, dy, 0, ("QR", 2, (1, 1), pr), ("QR", 2, (1 - dy, 1), pr)))
    return out


def coarse_messages():
    out = []
    for dx in (2, 1, 0, -1, -2):
        for dy in (1, 0, -1):
            ps, pd = {
                0: ((5, 4), (5, 4)),
                1: ((5, 4), (1, 4)),
                -1: ((5, 4), (9, 4)),
                2: ((8, 1), (0, 1)),
                -2: ((5, 1), (13, 1)),
            }[dx]
            rs, rd = {0: ((8, 16), (8, 16)), 1: ((19, 5), (3, 5)), -1: ((8, 5), (24, 5))}[dy]
            if (dx, dy) != (0, 0):
                out.append((dx, dy, 0, ps, pd, rs, rd))
            out.append((dx, dy, 1, None, None, {0: (0, 8), 1: (3, 5), -1: (0, 5)}[dy], None))
    return out


FINE = fine_messages()
COARSE = coarse_messages()
NF, NC = len(FINE), len(COARSE)


def ds(pair):
    return pl.ds(pair[0], pair[1])


def up(x):
    return pltpu.roll(x, 127, 1)


def down(x):
    return pltpu.roll(x, 1, 1)


RATIO = 64.0 / 3.0


def stencil(ref, factors, base, count, r, tiles, outs, lane, bf):
    before, before_v, after, after_v = factors
    rows = pl.ds(r, 8)
    parts = []
    for k in range(count):
        parts.append(([], [], [], [], []))
    for t in range(tiles):
        vs = [ref[base - 1 + k, t, rows, :] for k in range(count + 2)]
        fys = []
        for k in range(count + 2):
            if t in outs or 0 < k <= count:
                fys.append(
                    ref[base - 1 + k, t, pl.ds(r + 1, 8), :]
                    - ref[base - 1 + k, t, pl.ds(r - 1, 8), :]
                )
            else:
                fys.append(None)
        for k in range(count):
            centre, straight, drift, plus, minus = parts[k]
            p = base + k
            v, xm, xp, fy = vs[k + 1], vs[k], vs[k + 2], fys[k + 1]
            d = xp - xm
            m = d - fy
            plus.append(before_v[p, t, rows, :] * v + before[p, t, rows, :] * m)
            minus.append(after_v[p, t, rows, :] * v - after[p, t, rows, :] * m)
            centre.append(v)
            if t in outs:
                sy = ref[p, t, pl.ds(r + 1, 8), :] + ref[p, t, pl.ds(r - 1, 8), :]
                straight.append(24.0 * (xp + xm) + 20.0 * sy + (fys[k + 2] - fys[k]))
                drift.append((1.5 * bf) * d - (fy if bf == 1.0 else bf * fy))
            else:
                straight.append(None)
                drift.append(None)
    result = []
    for k in range(count):
        centre, straight, drift, plus, minus = parts[k]
        one = []
        for t in outs:
            b = (
                drift[t]
                + up(jnp.where(lane == 0, plus[(t + 1) % tiles], plus[t]))
                + down(jnp.where(lane == 127, minus[t - 1], minus[t]))
            )
            one.append((t, centre[t], straight[t], b))
        result.append(one)
    return result


def keep_factors(stores, p, rows, scales, lane, sf, bf):
    double, before, before_v, after, after_v = stores
    low, high = shifted_scales([(1.5 * sf) * c for c in scales], lane)
    for t in range(len(scales)):
        double[p, t, rows, :] = (2.0 * sf) * scales[t]
        before[p, t, rows, :] = low[t]
        before_v[p, t, rows, :] = RATIO * low[t] + 0.75 * bf
        after[p, t, rows, :] = high[t]
        after_v[p, t, rows, :] = RATIO * high[t] - 0.75 * bf


def shifted_scales(values, lane):
    count = len(values)
    before = [down(jnp.where(lane == 127, values[t - 1], values[t])) for t in range(count)]
    after = [up(jnp.where(lane == 0, values[(t + 1) % count], values[t])) for t in range(count)]
    return before, after


def kernel(g_hbm, c_hbm, sol_ref, res_ref, GC, PS, PR, SS, SR, W, F2, FB, FBV, FA, FAV, A, B, RX, CO, QS, QR,
           CW, K2, KB, KBV, KA, KAV, CA, CB, UPS, load_sem, f_send, f_recv, c_send, c_recv):
    gx, gy, gz = lax.axis_index("gx"), lax.axis_index("gy"), lax.axis_index("gz")

    def peer(dx, dy, dz):
        return (gx + dx, gy + dy, lax.rem(gz + dz, 2))

    def inside(dx, dy):
        tests = []
        if dx > 0:
            tests.append(gx < NXD - dx)
        if dx < 0:
            tests.append(gx >= -dx)
        if dy > 0:
            tests.append(gy < NYD - dy)
        if dy < 0:
            tests.append(gy >= -dy)
        if not tests:
            return None
        return tests[0] if len(tests) == 1 else tests[0] & tests[1]

    def guarded(dx, dy, act):
        test = inside(dx, dy)
        if test is None:
            act()
        else:
            pl.when(test)(act)

    loads = []
    for a, src in ((0, g_hbm), (1, c_hbm)):
        for t in range(2):
            cp = pltpu.make_async_copy(
                src.at[:, :, pl.ds(128 * t, 128)],
                GC.at[a, pl.ds(5, 8), t, pl.ds(8, 32), :],
                load_sem.at[2 * a + t],
            )
            cp.start()
            loads.append(cp)

    barrier = pltpu.get_barrier_semaphore()
    partners = 1
    for dx, dy, dz in ((1, 0, 0), (-1, 0, 0), (0, 1, 0), (0, -1, 0), (0, 0, 1)):

        def greet():
            pl.semaphore_signal(barrier, inc=1, device_id=peer(dx, dy, dz), device_id_type=MESH)

        guarded(dx, dy, greet)
        if not dz:
            partners = partners + jnp.where(inside(dx, dy), 1, 0)

    lane = lax.broadcasted_iota(jnp.int32, (8, 128), 1)
    sub = lax.broadcasted_iota(jnp.int32, (8, 128), 0)
    zfirst = 120 * gz
    zmask = (lane >= zfirst) & (lane < zfirst + 8)
    blank = jnp.zeros((8, 128), F32)

    def clear_fine(low, high, rows):
        def one(p, _):
            for a in range(2):
                for t in range(2):
                    for r in rows:
                        GC[a, p, t, pl.ds(r, 8), :] = blank
            return 0
        lax.fori_loop(low, high, one, 0)

    def clear_pack(slots, low, high):
        def one(p, _):
            for n in slots:
                PR[n, p] = blank
            return 0
        lax.fori_loop(low, high, one, 0)

    def clear_coarse(k, low, high, rows):
        def one(p, _):
            for r in rows:
                CO[k, p, 0, pl.ds(r, 8), :] = blank
            return 0
        lax.fori_loop(low, high, one, 0)

    def clear_edge(k, cols, rows):
        for n in cols:
            for m in rows:
                QR[k, n, m] = blank

    def clear_smooth(low):
        for p in (low, low + 1):
            for t in range(3):
                for r in (0, 8, 16, 24, 32, 40):
                    B[p, t, pl.ds(r, 8), :] = blank

    all_rows = (0, 8, 16, 24, 32, 40)
    coarse_rows = (0, 8, 16, 24)
    slots = (0, 1, 2)

    @pl.when(gx == 0)
    def _():
        clear_fine(2, 5, all_rows)
        clear_pack(slots, 2, 5)
        for k in range(2):
            clear_coarse(k, 0, 5, coarse_rows)
            clear_edge(k, (0, 1), slots)
        clear_smooth(2)

    @pl.when(gx == 1)
    def _():
        clear_coarse(0, 0, 1, coarse_rows)
        clear_edge(0, (0,), slots)

    @pl.when(gx == NXD - 1)
    def _():
        clear_fine(13, 16, all_rows)
        clear_pack(slots, 13, 16)
        for k in range(2):
            clear_coarse(k, 9, 14, coarse_rows)
            clear_edge(k, (3, 4), slots)
        clear_smooth(14)

    @pl.when(gx == NXD - 2)
    def _():
        clear_coarse(0, 13, 14, coarse_rows)
        clear_edge(0, (4,), slots)

    @pl.when(gy == 0)
    def _():
        clear_fine(5, 13, (0,))
        clear_pack((0,), 5, 13)
        clear_coarse(0, 0, 14, (0,))
        clear_coarse(1, 5, 9, (0,))
        clear_edge(0, (0, 1, 2, 3, 4), (0,))
        clear_edge(1, (2,), (0,))

    @pl.when(gy == NYD - 1)
    def _():
        clear_fine(5, 13, (40,))
        clear_pack((2,), 5, 13)
        clear_coarse(0, 0, 14, (24,))
        clear_coarse(1, 5, 9, (24,))
        clear_edge(0, (0, 1, 2, 3, 4), (2,))
        clear_edge(1, (2,), (2,))

    for cp in loads:
        cp.wait()

    def pack_plane(x, _):
        acc = blank
        for a in range(2):
            for j in range(4):
                m = 4 * a + j
                t0 = GC[a, 5 + x, 0, pl.ds(8 + 8 * j, 8), :]
                t1 = GC[a, 5 + x, 1, pl.ds(8 + 8 * j, 8), :]
                both = pltpu.roll(jnp.where(lane >= 64, t1, t0), (16 * m + 8) % 128, 1)
                acc = jnp.where((lane >= 16 * m) & (lane < 16 * m + 16), both, acc)
        PS[x] = acc
        return 0

    lax.fori_loop(0, 8, pack_plane, 0)

    row_i = lax.broadcasted_iota(jnp.int32, (256, 128), 0)
    col_i = lax.broadcasted_iota(jnp.int32, (256, 128), 1)
    pool = jnp.where(row_i // 2 == col_i, 0.125, 0.0).astype(F32)

    def coarsen_rows(k):
        pieces = []
        for i in range(4):
            cols = []
            for t in range(2):
                cols.append(RX[i, t, pl.ds(0, 16, stride=2), :] + RX[i, t, pl.ds(1, 16, stride=2), :])
            pieces.append(jnp.concatenate(cols, axis=1))
        allp = jnp.concatenate(pieces, axis=0)
        q = jnp.dot(allp, pool, preferred_element_type=F32, precision=lax.Precision.HIGHEST)
        acc = blank
        for i in range(4):
            CO[k, 5 + i, 0, pl.ds(8, 16), :] = q[16 * i : 16 * i + 16]
            for j in range(2):
                m = 2 * i + j
                turned = pltpu.roll(q[8 * m : 8 * m + 8], (16 * m + 8) % 128, 1)
                acc = jnp.where((lane >= 16 * m) & (lane < 16 * m + 16), turned, acc)
        QS[k] = acc

    def pair_scale(i, _):
        for t in range(2):
            RX[i, t] = GC[1, 5 + 2 * i, t, pl.ds(8, 32), :] + GC[1, 6 + 2 * i, t, pl.ds(8, 32), :]
        return 0

    lax.fori_loop(0, 4, pair_scale, 0)
    coarsen_rows(1)

    starts = [4, 12, 20, 28, 36]
    ylow = (gy * 32 + sub - 4) >= 0
    yhigh = (gy * 32 + sub + 28) < 512

    def place(where):
        kind = where[0]
        if kind == "PS":
            return PS.at[pl.ds(0, 8)]
        if kind == "PR":
            slot, planes, rows = where[1:]
            return PR.at[slot[0], ds(planes), ds(rows), :]
        if kind == "QS":
            return QS.at[where[1]]
        if kind == "QR":
            col, rows, subs = where[1:]
            if rows[1] == 1:
                return QR.at[1, col, rows[0], ds(subs), :]
            return QR.at[1, col, ds(rows), ds(subs), :]
        if kind == "CO":
            return CO.at[1, ds(where[1]), 0, ds(where[2]), :]
        if kind == "B":
            return B.at[ds(where[1]), pl.ds(0, 2), pl.ds(4, 40), :]
        if kind == "SS":
            return SS.at[where[1]]
        if kind == "SR":
            return SR.at[where[1]]
        return GC.at[where[1], ds(where[2]), pl.ds(0, 2), ds(where[3]), :]

    def fine_copy(i):
        _, dx, dy, dz, src, dst = FINE[i]
        return pltpu.make_async_remote_copy(
            src_ref=place(src),
            dst_ref=place(dst),
            send_sem=f_send.at[i],
            recv_sem=f_recv.at[i],
            device_id=peer(dx, dy, dz),
            device_id_type=MESH,
        )

    def coarse_copy(k, i):
        dx, dy, dz, ps, pd, rs, rd = COARSE[i]
        if dz:
            src, dst = QS.at[k, ds(rs), :], QR.at[k, 2 - dx, 1 - dy, ds(rs), :]
        else:
            src, dst = CO.at[k, ds(ps), 0, ds(rs), :], CO.at[k, ds(pd), 0, ds(rd), :]
        return pltpu.make_async_remote_copy(
            src_ref=src,
            dst_ref=dst,
            send_sem=c_send.at[i],
            recv_sem=c_recv.at[i],
            device_id=peer(dx, dy, dz),
            device_id_type=MESH,
        )

    FAR = [(2, 1), (2, -1), (-2, 1), (-2, -1), (1, 1), (1, -1), (-1, 1), (-1, -1),
           (2, 0), (-2, 0), (1, 0), (-1, 0), (0, 1), (0, -1), (0, 0)]
    NEAR = [(1, 0), (-1, 0), (0, 1), (0, -1), (0, 0)]

    def run(direction, copies, method, back):
        if copies:
            dx, dy = direction
            def act():
                for cp in copies:
                    getattr(cp, method)()
            guarded(-dx if back else dx, -dy if back else dy, act)

    def fine(phase, method):
        for d in NEAR:
            run(d, [fine_copy(i) for i in range(NF) if FINE[i][0] in phase and FINE[i][1:3] == d],
                method, method == "wait_recv")

    def coarse(k, method):
        for d in FAR:
            run(d, [coarse_copy(k, i) for i in range(NC) if COARSE[i][:2] == d],
                method, method == "wait_recv")

    pl.semaphore_wait(barrier, partners)

    fine(("z",), "start")
    fine(("y",), "start")

    def unpack(low, high):
        def unpack_plane(p, _):
            for a in range(2):
                for r in range(6):
                    slot, j = (0, 3) if r == 0 else (2, 0) if r == 5 else (1, r - 1)
                    m = 4 * a + j
                    v = pltpu.roll(PR[slot, p], (128 - 16 * m - 8) % 128, 1)
                    GC[a, p, 2, pl.ds(8 * r, 8), :] = jnp.where(zmask, v, 0.0)
            return 0

        lax.fori_loop(low, high, unpack_plane, 0)

    def weights(low, high):
        def one(p, _):
            at = gx * 8 + p - 5
            scale = jnp.where((at >= 0) & (at < 64), DAMP, 0.0).astype(F32)
            for r in starts:
                scales = [GC[1, p, t, pl.ds(r, 8), :] for t in range(3)]
                keep_factors((F2, FB, FBV, FA, FAV), p, pl.ds(r, 8), scales, lane, 1.0, 1.0)
                for t in range(3):
                    w = scale / (1.05 + 240.0 * scales[t])
                    if r == 4:
                        w = jnp.where(ylow, w, 0.0)
                    if r == 36:
                        w = jnp.where(yhigh, w, 0.0)
                    if t == 2:
                        w = jnp.where(zmask, w, 0.0)
                    W[p, t, pl.ds(r, 8), :] = w
            return 0

        lax.fori_loop(low, high, one, 0)

    fine_factors = (FB, FBV, FA, FAV)

    def fine_planes(view, dst, base, count):
        for r in starts:
            rows = pl.ds(r, 8)
            whole = stencil(view, fine_factors, base, count, r, 3, (0, 1, 2), lane, 1.0)
            for k in range(count):
                p = base + k
                for t, v, s, b in whole[k]:
                    dst[p, t, rows, :] = 0.4 * v + W[p, t, rows, :] * (
                        GC[0, p, t, rows, :] + F2[p, t, rows, :] * s + b
                    )

    def fine_sweep(src, dst, low, high, step, src_index=None):
        view = src if src_index is None else src.at[src_index]

        def one(n, _):
            fine_planes(view, dst, low + step * n, step)
            return 0

        lax.fori_loop(0, (high - low) // step, one, 0)

    def fine_sides(src, dst, low, high, count, src_index=None):
        view = src if src_index is None else src.at[src_index]

        def one(n, _):
            fine_planes(view, dst, low + (high - low) * n, count)
            return 0

        lax.fori_loop(0, 2, one, 0)

    def fine_residue(src, base, count):
        out = [[] for _ in range(count)]
        for r in (8, 16, 24, 32):
            rows = pl.ds(r, 8)
            whole = stencil(src, fine_factors, base, count, r, 3, (0, 1), lane, 1.0)
            for k in range(count):
                p = base + k
                for t, v, s, b in whole[k]:
                    out[k].append(
                        GC[0, p, t, rows, :] - 1.05 * v + F2[p, t, rows, :] * (s - 120.0 * v) + b
                    )
        return out

    fine(("z",), "wait_recv")
    fine(("yz", "xz"), "start")
    fine(("cy",), "start")
    fine(("y",), "wait_recv")
    fine(("x",), "start")
    fine(("yz",), "wait_recv")
    fine(("xyz",), "start")
    unpack(5, 13)
    weights(5, 13)
    fine_sweep(GC, A, 6, 12, 3, 0)
    fine_sweep(A, B, 7, 11, 2)
    fine(("cy",), "wait_recv")
    fine(("cx",), "start")
    fine(("x", "xz", "xy", "xyz"), "wait_recv")
    unpack(2, 5)
    unpack(13, 16)
    weights(3, 5)
    weights(13, 15)
    fine_sides(GC, A, 3, 12, 3, 0)
    fine(("cx",), "wait_recv")
    fine(("cxx",), "start")
    fine_sides(A, B, 4, 11, 3)

    def residue_pair(i, _):
        one, two = fine_residue(B, 5 + 2 * i, 2)
        for n in range(8):
            RX[i, n % 2, pl.ds(8 * (n // 2), 8), :] = one[n] + two[n]
        return 0

    lax.fori_loop(0, 4, residue_pair, 0)
    coarsen_rows(0)

    coarse(0, "start")

    for side in range(2):
        for n in range(2):
            p = (10 if side == 0 else 6) + n
            acc = blank
            for j, r in enumerate(starts):
                turned = pltpu.roll(B[p, 2, pl.ds(r, 8), :], (16 * j + 8) % 128, 1)
                acc = jnp.where((lane >= 16 * j) & (lane < 16 * j + 16), turned, acc)
            SS[side, n] = acc
    fine(("s",), "start")

    cylow = (gy * 16 + sub - 8) >= 0
    cyhigh = (gy * 16 + sub + 16) < 256

    fine(("cxx",), "wait_recv")

    def coarse_unpack(k):
        for p in range(CX):
            col, i = [(0, 3), (1, 0), (1, 1), (1, 2), (1, 3), (2, 0), (2, 1), (2, 2), (2, 3),
                      (3, 0), (3, 1), (3, 2), (3, 3), (4, 0)][p]
            for r, (row, j) in enumerate(((0, 1), (1, 0), (1, 1), (2, 0))):
                m = 2 * i + j
                turned = pltpu.roll(QR[k, col, row], (128 - 16 * m - 8) % 128, 1)
                CO[k, p, 1, pl.ds(8 * r, 8), :] = jnp.where(zmask, turned, 0.0)

    coarse_unpack(1)

    def coarse_weights(p, _):
        at = gx * 4 + p - 5
        scale = jnp.where((at >= 0) & (at < 32), DAMP, 0.0).astype(F32)
        for n, r in enumerate((0, 8, 16, 24)):
            scales = [CO[1, p, t, pl.ds(r, 8), :] for t in range(2)]
            keep_factors((K2, KB, KBV, KA, KAV), p, pl.ds(r, 8), scales, lane, 0.25, 0.5)
            for t in range(2):
                w = scale / (1.05 + 60.0 * scales[t])
                if r == 0:
                    w = jnp.where(cylow, w, 0.0)
                if r == 24:
                    w = jnp.where(cyhigh, w, 0.0)
                if t == 1:
                    w = jnp.where(zmask, w, 0.0)
                CW[p, t, pl.ds(r, 8), :] = w
        return 0

    lax.fori_loop(0, CX, coarse_weights, 0)

    fine(("z", "x", "y", "xz", "yz", "xy", "xyz", "cy", "cx", "cxx"), "wait_send")
    coarse(0, "wait_recv")
    coarse_unpack(0)

    def coarse_first(p, _):
        for r in (0, 8, 16, 24):
            for t in range(2):
                rows = pl.ds(r, 8)
                CA[p, t, rows, :] = CW[p, t, rows, :] * CO[0, p, t, rows, :]
        return 0

    lax.fori_loop(0, CX, coarse_first, 0)

    def coarse_sweep(src, dst, low, high, step):
        def one(n, _):
            base = low + step * n
            for r in (4, 12, 20):
                rows = pl.ds(r, 8)
                whole = stencil(src, (KB, KBV, KA, KAV), base, step, r, 2, (0, 1), lane, 0.5)
                for k in range(step):
                    p = base + k
                    for t, v, s, b in whole[k]:
                        dst[p, t, rows, :] = 0.4 * v + CW[p, t, rows, :] * (
                            CO[0, p, t, rows, :] + K2[p, t, rows, :] * s + b
                        )
            return 0

        lax.fori_loop(0, (high - low) // step, one, 0)

    coarse_sweep(CA, CB, 1, 13, 4)
    coarse_sweep(CB, CA, 2, 12, 5)
    coarse_sweep(CA, CB, 3, 11, 4)

    ri = lax.broadcasted_iota(jnp.int32, (128, 256), 0)
    ci = lax.broadcasted_iota(jnp.int32, (128, 256), 1)
    spread = jnp.where(ci // 2 == ri, 1.0, 0.0).astype(F32)
    rh = lax.broadcasted_iota(jnp.int32, (128, 128), 0)
    ch = lax.broadcasted_iota(jnp.int32, (128, 128), 1)
    source = ch // 2 + 64 * gz
    keep = (ch >= zfirst) & (ch < zfirst + 8)
    spread_h = jnp.where((source == rh) & keep, 1.0, 0.0).astype(F32)
    mine = jnp.concatenate([CB[3 + q, 0, pl.ds(4, 24), :] for q in range(8)], axis=0)
    other = jnp.concatenate([CB[3 + q, 1, pl.ds(4, 24), :] for q in range(8)], axis=0)
    wide = jnp.dot(mine, spread, preferred_element_type=F32, precision=lax.Precision.HIGHEST)
    wide_h = jnp.dot(other, spread_h, preferred_element_type=F32, precision=lax.Precision.HIGHEST)
    for q in range(8):
        for t in range(3):
            part = (wide[24 * q : 24 * q + 24, 128 * t : 128 * t + 128] if t < 2
                    else wide_h[24 * q : 24 * q + 24])
            UPS[q, t, pl.ds(0, 24, stride=2), :] = part
            UPS[q, t, pl.ds(1, 24, stride=2), :] = part

    fine(("s",), "wait_send")
    fine(("s",), "wait_recv")

    def spread_edge(side, first):
        for n in range(2):
            for j, r in enumerate(starts):
                turned = pltpu.roll(SR[side, n], (128 - 16 * j - 8) % 128, 1)
                B[first + n, 2, pl.ds(r, 8), :] = jnp.where(zmask, turned, 0.0)

    @pl.when(gx > 0)
    def _():
        spread_edge(0, 2)

    @pl.when(gx < NXD - 1)
    def _():
        spread_edge(1, 14)

    def add_up(q, _):
        for half in range(2):
            for r in range(6):
                for t in range(3):
                    rows = pl.ds(8 * r, 8)
                    p = 2 * q + 1 + half
                    A[p, t, rows, :] = B[p, t, rows, :] + UPS[q, t, rows, :]
        return 0

    lax.fori_loop(0, 8, add_up, 0)

    fine_sweep(A, B, 3, 15, 3)
    fine_sweep(B, A, 4, 14, 5)

    def finish(n, _):
        both = fine_residue(A, 5 + 4 * n, 4)
        for k in range(4):
            x = 4 * n + k
            for i in range(8):
                t, r = i % 2, 8 * (i // 2)
                res_ref[x, pl.ds(r, 8), pl.ds(128 * t, 128)] = both[k][i]
                sol_ref[x, pl.ds(r, 8), pl.ds(128 * t, 128)] = A[5 + x, t, pl.ds(8 + r, 8), :]
        return 0

    lax.fori_loop(0, 2, finish, 0)

    coarse(0, "wait_send")


def closing(sol_ref, res_ref, sol_hbm, res_hbm, sems):
    copies = [
        pltpu.make_async_copy(sol_ref, sol_hbm, sems.at[0]),
        pltpu.make_async_copy(res_ref, res_hbm, sems.at[1]),
    ]
    for cp in copies:
        cp.start()
    for cp in copies:
        cp.wait()


def on_device(right_side, volscale):
    shape = pltpu.VMEM(right_side.shape, F32)
    fine = pltpu.VMEM((PX, 3, ROWS, 128), F32)
    coarse = pltpu.VMEM((CX, 2, CROWS, 128), F32)
    any_space = pl.BlockSpec(memory_space=pl.ANY)
    sol, res = pl.pallas_call(
        kernel,
        out_shape=(shape, shape),
        in_specs=[any_space] * 2,
        out_specs=(pl.BlockSpec(memory_space=pltpu.VMEM),) * 2,
        scratch_shapes=[
            pltpu.VMEM((2, PX, 3, ROWS, 128), F32),
            pltpu.VMEM((8, 8, 128), F32),
            pltpu.VMEM((3, PX, 8, 128), F32),
            pltpu.VMEM((2, 2, 8, 128), F32),
            pltpu.VMEM((2, 2, 8, 128), F32),
            *[fine] * 8,
            pltpu.VMEM((4, 2, 32, 128), F32),
            pltpu.VMEM((2, CX, 2, CROWS, 128), F32),
            pltpu.VMEM((2, 8, 128), F32),
            pltpu.VMEM((2, 5, 3, 8, 128), F32),
            *[coarse] * 8,
            pltpu.VMEM((8, 3, ROWS, 128), F32),
            pltpu.SemaphoreType.DMA((4,)),
            pltpu.SemaphoreType.DMA((NF,)),
            pltpu.SemaphoreType.DMA((NF,)),
            pltpu.SemaphoreType.DMA((NC,)),
            pltpu.SemaphoreType.DMA((NC,)),
        ],
        compiler_params=pltpu.CompilerParams(collective_id=0, has_side_effects=True),
    )(right_side, volscale)
    plain = jax.ShapeDtypeStruct(right_side.shape, F32)
    in_vmem = pl.BlockSpec(memory_space=pltpu.VMEM)
    sol = pltpu.with_memory_space_constraint(sol, pltpu.VMEM)
    res = pltpu.with_memory_space_constraint(res, pltpu.VMEM)
    return pl.pallas_call(
        closing,
        out_shape=(plain, plain),
        in_specs=[in_vmem] * 2,
        out_specs=(any_space, any_space),
        scratch_shapes=[pltpu.SemaphoreType.DMA((2,))],
        compiler_params=pltpu.CompilerParams(vmem_limit_bytes=1 << 20),
    )(sol, res)


def solution(mesh):
    placed = (P("gx", "gy", "gz"), P("gx", "gy", "gz"))
    return jax.shard_map(
        on_device,
        mesh=mesh,
        in_specs=placed,
        out_specs=(P("gx", "gy", "gz"), P("gx", "gy", "gz")),
        check_vma=False,
    )
```

```python
import jax
import jax.numpy as jnp
from jax import lax
from jax.experimental import pallas as pl
from jax.experimental.pallas import tpu as pltpu
from jax.sharding import PartitionSpec as P

MESH = pl.DeviceIdType.MESH
F32 = jnp.float32
NXD, NYD = 8, 16
BX, BY = 8, 32
HALO = 5
PX = BX + 2 * HALO
ROWS = BY + 16
CX = BX // 2 + 2 * HALO
CROWS = BY // 2 + 16
DAMP = 0.6


def fine_messages():
    lo, mid, hi = (3, 5), (8, 32), (40, 5)
    every = (0, 3)
    out = [
        ("z", 0, 0, 1, ("PS",), ("PR", (1, 1), (5, 8), (0, 8))),
        ("z", 0, 0, 1, ("QS", 1), ("QR", 2, (1, 1), (0, 8))),
    ]
    for dx in (1, -1):
        side, far = 2 - dx, 2 - 2 * dx
        sg, dg = ((10, 3), (2, 3)) if dx == 1 else ((5, 3), (13, 3))
        sc, dc = ((11, 2), (3, 2)) if dx == 1 else ((5, 2), (13, 2))
        out.append(("x", dx, 0, 0, ("GC", 0, sg, (3, 42)), ("GC", 0, dg, (3, 42))))
        out.append(("x", dx, 0, 0, ("GC", 1, sc, (3, 42)), ("GC", 1, dc, (3, 42))))
        out.append(("xz", dx, 0, 0, ("PR", (1, 1), sg, (0, 8)), ("PR", (1, 1), dg, (0, 8))))
        for rows in (lo, hi):
            pass
        for slot, rows in ((0, (3, 5)), (2, (0, 5))):
            out.append(("xyz", dx, 0, 0, ("PR", (slot, 1), sg, rows), ("PR", (slot, 1), dg, rows)))
        out.append(("cx", dx, 0, 0, ("CO", (5, 4), (3, 26)), ("CO", (1 if dx == 1 else 9, 4), (3, 26))))
        out.append(("cx", dx, 0, 0, ("QR", 2, every, (0, 8)), ("QR", side, every, (0, 8))))
        near, last = (4, 0) if dx == 1 else (9, 13)
        out.append(("cxx", dx, 0, 0, ("CO", (near, 1), (3, 26)), ("CO", (last, 1), (3, 26))))
        out.append(("cxx", dx, 0, 0, ("QR", side, every, (0, 8)), ("QR", far, every, (0, 8))))
        sb, db = ((10, 2), (2, 2)) if dx == 1 else ((6, 2), (14, 2))
        out.append(("s", dx, 0, 0, ("B", sb), ("B", db)))
        out.append(("s", dx, 0, 0, ("SS", (1 - dx) // 2), ("SR", (1 - dx) // 2)))
    for dy in (1, -1):
        rs, rd, pr = ((35, 5), lo, (3, 5)) if dy == 1 else ((8, 5), hi, (0, 5))
        cs, cd = ((19, 5), (3, 5)) if dy == 1 else ((8, 5), (24, 5))
        out.append(("y", 0, dy, 0, ("GC", 0, (5, 8), rs), ("GC", 0, (5, 8), rd)))
        out.append(("y", 0, dy, 0, ("GC", 1, (5, 8), rs), ("GC", 1, (5, 8), rd)))
        out.append(("yz", 0, dy, 0, ("PR", (1, 1), (5, 8), pr), ("PR", (1 - dy, 1), (5, 8), pr)))
        out.append(("cy", 0, dy, 0, ("CO", (5, 4), cs), ("CO", (5, 4), cd)))
        out.append(("cy", 0, dy, 0, ("QR", 2, (1, 1), pr), ("QR", 2, (1 - dy, 1), pr)))
    return out


def coarse_messages():
    out = []
    for dx in (2, 1, 0, -1, -2):
        for dy in (1, 0, -1):
            ps, pd = {
                0: ((5, 4), (5, 4)),
                1: ((5, 4), (1, 4)),
                -1: ((5, 4), (9, 4)),
                2: ((8, 1), (0, 1)),
                -2: ((5, 1), (13, 1)),
            }[dx]
            rs, rd = {0: ((8, 16), (8, 16)), 1: ((19, 5), (3, 5)), -1: ((8, 5), (24, 5))}[dy]
            if (dx, dy) != (0, 0):
                out.append((dx, dy, 0, ps, pd, rs, rd))
            out.append((dx, dy, 1, None, None, {0: (0, 8), 1: (3, 5), -1: (0, 5)}[dy], None))
    return out


FINE = fine_messages()
COARSE = coarse_messages()
NF, NC = len(FINE), len(COARSE)


def ds(pair):
    return pl.ds(pair[0], pair[1])


def up(x):
    return pltpu.roll(x, 127, 1)


def down(x):
    return pltpu.roll(x, 1, 1)


RATIO = 64.0 / 3.0


def stencil(ref, factors, base, count, r, tiles, outs, lane, bf):
    before, before_v, after, after_v = factors
    rows = pl.ds(r, 8)
    parts = []
    for k in range(count):
        parts.append(([], [], [], [], []))
    for t in range(tiles):
        vs = [ref[base - 1 + k, t, rows, :] for k in range(count + 2)]
        fys = []
        for k in range(count + 2):
            if t in outs or 0 < k <= count:
                fys.append(
                    ref[base - 1 + k, t, pl.ds(r + 1, 8), :]
                    - ref[base - 1 + k, t, pl.ds(r - 1, 8), :]
                )
            else:
                fys.append(None)
        for k in range(count):
            centre, straight, drift, plus, minus = parts[k]
            p = base + k
            v, xm, xp, fy = vs[k + 1], vs[k], vs[k + 2], fys[k + 1]
            d = xp - xm
            m = d - fy
            plus.append(before_v[p, t, rows, :] * v + before[p, t, rows, :] * m)
            minus.append(after_v[p, t, rows, :] * v - after[p, t, rows, :] * m)
            centre.append(v)
            if t in outs:
                sy = ref[p, t, pl.ds(r + 1, 8), :] + ref[p, t, pl.ds(r - 1, 8), :]
                straight.append(24.0 * (xp + xm) + 20.0 * sy + (fys[k + 2] - fys[k]))
                drift.append((1.5 * bf) * d - (fy if bf == 1.0 else bf * fy))
            else:
                straight.append(None)
                drift.append(None)
    result = []
    for k in range(count):
        centre, straight, drift, plus, minus = parts[k]
        one = []
        for t in outs:
            b = (
                drift[t]
                + up(jnp.where(lane == 0, plus[(t + 1) % tiles], plus[t]))
                + down(jnp.where(lane == 127, minus[t - 1], minus[t]))
            )
            one.append((t, centre[t], straight[t], b))
        result.append(one)
    return result


def keep_factors(stores, p, rows, scales, lane, sf, bf):
    double, before, before_v, after, after_v = stores
    low, high = shifted_scales([(1.5 * sf) * c for c in scales], lane)
    for t in range(len(scales)):
        double[p, t, rows, :] = (2.0 * sf) * scales[t]
        before[p, t, rows, :] = low[t]
        before_v[p, t, rows, :] = RATIO * low[t] + 0.75 * bf
        after[p, t, rows, :] = high[t]
        after_v[p, t, rows, :] = RATIO * high[t] - 0.75 * bf


def shifted_scales(values, lane):
    count = len(values)
    before = [down(jnp.where(lane == 127, values[t - 1], values[t])) for t in range(count)]
    after = [up(jnp.where(lane == 0, values[(t + 1) % count], values[t])) for t in range(count)]
    return before, after


def kernel(g_hbm, c_hbm, sol_ref, res_ref, GC, PS, PR, SS, SR, W, F2, FB, FBV, FA, FAV, A, B, RX, CO, QS, QR,
           CW, K2, KB, KBV, KA, KAV, CA, CB, UPS, load_sem, f_send, f_recv, c_send, c_recv):
    gx, gy, gz = lax.axis_index("gx"), lax.axis_index("gy"), lax.axis_index("gz")

    def peer(dx, dy, dz):
        return (gx + dx, gy + dy, lax.rem(gz + dz, 2))

    def inside(dx, dy):
        tests = []
        if dx > 0:
            tests.append(gx < NXD - dx)
        if dx < 0:
            tests.append(gx >= -dx)
        if dy > 0:
            tests.append(gy < NYD - dy)
        if dy < 0:
            tests.append(gy >= -dy)
        if not tests:
            return None
        return tests[0] if len(tests) == 1 else tests[0] & tests[1]

    def guarded(dx, dy, act):
        test = inside(dx, dy)
        if test is None:
            act()
        else:
            pl.when(test)(act)

    loads = []
    for a, src in ((0, g_hbm), (1, c_hbm)):
        for t in range(2):
            cp = pltpu.make_async_copy(
                src.at[:, :, pl.ds(128 * t, 128)],
                GC.at[a, pl.ds(5, 8), t, pl.ds(8, 32), :],
                load_sem.at[2 * a + t],
            )
            cp.start()
            loads.append(cp)

    barrier = pltpu.get_barrier_semaphore()
    partners = 1
    for dx, dy, dz in ((1, 0, 0), (-1, 0, 0), (0, 1, 0), (0, -1, 0), (0, 0, 1)):

        def greet():
            pl.semaphore_signal(barrier, inc=1, device_id=peer(dx, dy, dz), device_id_type=MESH)

        guarded(dx, dy, greet)
        if not dz:
            partners = partners + jnp.where(inside(dx, dy), 1, 0)

    lane = lax.broadcasted_iota(jnp.int32, (8, 128), 1)
    sub = lax.broadcasted_iota(jnp.int32, (8, 128), 0)
    zfirst = 120 * gz
    zmask = (lane >= zfirst) & (lane < zfirst + 8)
    blank = jnp.zeros((8, 128), F32)

    def clear_fine(low, high, rows):
        def one(p, _):
            for a in range(2):
                for t in range(2):
                    for r in rows:
                        GC[a, p, t, pl.ds(r, 8), :] = blank
            return 0
        lax.fori_loop(low, high, one, 0)

    def clear_pack(slots, low, high):
        def one(p, _):
            for n in slots:
                PR[n, p] = blank
            return 0
        lax.fori_loop(low, high, one, 0)

    def clear_coarse(k, low, high, rows):
        def one(p, _):
            for r in rows:
                CO[k, p, 0, pl.ds(r, 8), :] = blank
            return 0
        lax.fori_loop(low, high, one, 0)

    def clear_edge(k, cols, rows):
        for n in cols:
            for m in rows:
                QR[k, n, m] = blank

    def clear_smooth(low):
        for p in (low, low + 1):
            for t in range(3):
                for r in (0, 8, 16, 24, 32, 40):
                    B[p, t, pl.ds(r, 8), :] = blank

    all_rows = (0, 8, 16, 24, 32, 40)
    coarse_rows = (0, 8, 16, 24)
    slots = (0, 1, 2)

    @pl.when(gx == 0)
    def _():
        clear_fine(2, 5, all_rows)
        clear_pack(slots, 2, 5)
        for k in range(2):
            clear_coarse(k, 0, 5, coarse_rows)
            clear_edge(k, (0, 1), slots)
        clear_smooth(2)

    @pl.when(gx == 1)
    def _():
        clear_coarse(0, 0, 1, coarse_rows)
        clear_edge(0, (0,), slots)

    @pl.when(gx == NXD - 1)
    def _():
        clear_fine(13, 16, all_rows)
        clear_pack(slots, 13, 16)
        for k in range(2):
            clear_coarse(k, 9, 14, coarse_rows)
            clear_edge(k, (3, 4), slots)
        clear_smooth(14)

    @pl.when(gx == NXD - 2)
    def _():
        clear_coarse(0, 13, 14, coarse_rows)
        clear_edge(0, (4,), slots)

    @pl.when(gy == 0)
    def _():
        clear_fine(5, 13, (0,))
        clear_pack((0,), 5, 13)
        clear_coarse(0, 0, 14, (0,))
        clear_coarse(1, 5, 9, (0,))
        clear_edge(0, (0, 1, 2, 3, 4), (0,))
        clear_edge(1, (2,), (0,))

    @pl.when(gy == NYD - 1)
    def _():
        clear_fine(5, 13, (40,))
        clear_pack((2,), 5, 13)
        clear_coarse(0, 0, 14, (24,))
        clear_coarse(1, 5, 9, (24,))
        clear_edge(0, (0, 1, 2, 3, 4), (2,))
        clear_edge(1, (2,), (2,))

    for cp in loads:
        cp.wait()

    def pack_plane(x, _):
        acc = blank
        for a in range(2):
            for j in range(4):
                m = 4 * a + j
                t0 = GC[a, 5 + x, 0, pl.ds(8 + 8 * j, 8), :]
                t1 = GC[a, 5 + x, 1, pl.ds(8 + 8 * j, 8), :]
                both = pltpu.roll(jnp.where(lane >= 64, t1, t0), (16 * m + 8) % 128, 1)
                acc = jnp.where((lane >= 16 * m) & (lane < 16 * m + 16), both, acc)
        PS[x] = acc
        return 0

    lax.fori_loop(0, 8, pack_plane, 0)

    row_i = lax.broadcasted_iota(jnp.int32, (256, 128), 0)
    col_i = lax.broadcasted_iota(jnp.int32, (256, 128), 1)
    pool = jnp.where(row_i // 2 == col_i, 0.125, 0.0).astype(F32)

    def coarsen_rows(k):
        pieces = []
        for i in range(4):
            cols = []
            for t in range(2):
                cols.append(RX[i, t, pl.ds(0, 16, stride=2), :] + RX[i, t, pl.ds(1, 16, stride=2), :])
            pieces.append(jnp.concatenate(cols, axis=1))
        allp = jnp.concatenate(pieces, axis=0)
        q = jnp.dot(allp, pool, preferred_element_type=F32, precision=lax.Precision.HIGHEST)
        acc = blank
        for i in range(4):
            CO[k, 5 + i, 0, pl.ds(8, 16), :] = q[16 * i : 16 * i + 16]
            for j in range(2):
                m = 2 * i + j
                turned = pltpu.roll(q[8 * m : 8 * m + 8], (16 * m + 8) % 128, 1)
                acc = jnp.where((lane >= 16 * m) & (lane < 16 * m + 16), turned, acc)
        QS[k] = acc

    def pair_scale(i, _):
        for t in range(2):
            RX[i, t] = GC[1, 5 + 2 * i, t, pl.ds(8, 32), :] + GC[1, 6 + 2 * i, t, pl.ds(8, 32), :]
        return 0

    lax.fori_loop(0, 4, pair_scale, 0)
    coarsen_rows(1)

    starts = [4, 12, 20, 28, 36]
    ylow = (gy * 32 + sub - 4) >= 0
    yhigh = (gy * 32 + sub + 28) < 512

    def place(where):
        kind = where[0]
        if kind == "PS":
            return PS.at[pl.ds(0, 8)]
        if kind == "PR":
            slot, planes, rows = where[1:]
            return PR.at[slot[0], ds(planes), ds(rows), :]
        if kind == "QS":
            return QS.at[where[1]]
        if kind == "QR":
            col, rows, subs = where[1:]
            if rows[1] == 1:
                return QR.at[1, col, rows[0], ds(subs), :]
            return QR.at[1, col, ds(rows), ds(subs), :]
        if kind == "CO":
            return CO.at[1, ds(where[1]), 0, ds(where[2]), :]
        if kind == "B":
            return B.at[ds(where[1]), pl.ds(0, 2), pl.ds(4, 40), :]
        if kind == "SS":
            return SS.at[where[1]]
        if kind == "SR":
            return SR.at[where[1]]
        return GC.at[where[1], ds(where[2]), pl.ds(0, 2), ds(where[3]), :]

    def fine_copy(i):
        _, dx, dy, dz, src, dst = FINE[i]
        return pltpu.make_async_remote_copy(
            src_ref=place(src),
            dst_ref=place(dst),
            send_sem=f_send.at[i],
            recv_sem=f_recv.at[i],
            device_id=peer(dx, dy, dz),
            device_id_type=MESH,
        )

    def coarse_copy(k, i):
        dx, dy, dz, ps, pd, rs, rd = COARSE[i]
        if dz:
            src, dst = QS.at[k, ds(rs), :], QR.at[k, 2 - dx, 1 - dy, ds(rs), :]
        else:
            src, dst = CO.at[k, ds(ps), 0, ds(rs), :], CO.at[k, ds(pd), 0, ds(rd), :]
        return pltpu.make_async_remote_copy(
            src_ref=src,
            dst_ref=dst,
            send_sem=c_send.at[i],
            recv_sem=c_recv.at[i],
            device_id=peer(dx, dy, dz),
            device_id_type=MESH,
        )

    FAR = [(2, 1), (2, -1), (-2, 1), (-2, -1), (1, 1), (1, -1), (-1, 1), (-1, -1),
           (2, 0), (-2, 0), (1, 0), (-1, 0), (0, 1), (0, -1), (0, 0)]
    NEAR = [(1, 0), (-1, 0), (0, 1), (0, -1), (0, 0)]

    def run(direction, copies, method, back):
        if copies:
            dx, dy = direction
            def act():
                for cp in copies:
                    getattr(cp, method)()
            guarded(-dx if back else dx, -dy if back else dy, act)

    def fine(phase, method):
        for d in NEAR:
            run(d, [fine_copy(i) for i in range(NF) if FINE[i][0] in phase and FINE[i][1:3] == d],
                method, method == "wait_recv")

    def coarse(k, method):
        for d in FAR:
            run(d, [coarse_copy(k, i) for i in range(NC) if COARSE[i][:2] == d],
                method, method == "wait_recv")

    pl.semaphore_wait(barrier, partners)

    fine(("z",), "start")
    fine(("y",), "start")

    def unpack(low, high):
        def unpack_plane(p, _):
            for a in range(2):
                for r in range(6):
                    slot, j = (0, 3) if r == 0 else (2, 0) if r == 5 else (1, r - 1)
                    m = 4 * a + j
                    v = pltpu.roll(PR[slot, p], (128 - 16 * m - 8) % 128, 1)
                    GC[a, p, 2, pl.ds(8 * r, 8), :] = jnp.where(zmask, v, 0.0)
            return 0

        lax.fori_loop(low, high, unpack_plane, 0)

    def weights(low, high):
        def one(p, _):
            at = gx * 8 + p - 5
            scale = jnp.where((at >= 0) & (at < 64), DAMP, 0.0).astype(F32)
            for r in starts:
                scales = [GC[1, p, t, pl.ds(r, 8), :] for t in range(3)]
                keep_factors((F2, FB, FBV, FA, FAV), p, pl.ds(r, 8), scales, lane, 1.0, 1.0)
                for t in range(3):
                    w = scale / (1.05 + 240.0 * scales[t])
                    if r == 4:
                        w = jnp.where(ylow, w, 0.0)
                    if r == 36:
                        w = jnp.where(yhigh, w, 0.0)
                    if t == 2:
                        w = jnp.where(zmask, w, 0.0)
                    W[p, t, pl.ds(r, 8), :] = w
            return 0

        lax.fori_loop(low, high, one, 0)

    fine_factors = (FB, FBV, FA, FAV)

    def fine_planes(view, dst, base, count):
        for r in starts:
            rows = pl.ds(r, 8)
            whole = stencil(view, fine_factors, base, count, r, 3, (0, 1, 2), lane, 1.0)
            for k in range(count):
                p = base + k
                for t, v, s, b in whole[k]:
                    dst[p, t, rows, :] = 0.4 * v + W[p, t, rows, :] * (
                        GC[0, p, t, rows, :] + F2[p, t, rows, :] * s + b
                    )

    def fine_sweep(src, dst, low, high, step, src_index=None):
        view = src if src_index is None else src.at[src_index]

        def one(n, _):
            fine_planes(view, dst, low + step * n, step)
            return 0

        lax.fori_loop(0, (high - low) // step, one, 0)

    def fine_sides(src, dst, low, high, count, src_index=None):
        view = src if src_index is None else src.at[src_index]

        def one(n, _):
            fine_planes(view, dst, low + (high - low) * n, count)
            return 0

        lax.fori_loop(0, 2, one, 0)

    def fine_residue(src, base, count):
        out = [[] for _ in range(count)]
        for r in (8, 16, 24, 32):
            rows = pl.ds(r, 8)
            whole = stencil(src, fine_factors, base, count, r, 3, (0, 1), lane, 1.0)
            for k in range(count):
                p = base + k
                for t, v, s, b in whole[k]:
                    out[k].append(
                        GC[0, p, t, rows, :] - 1.05 * v + F2[p, t, rows, :] * (s - 120.0 * v) + b
                    )
        return out

    fine(("z",), "wait_recv")
    fine(("yz", "xz"), "start")
    fine(("cy",), "start")
    fine(("y",), "wait_recv")
    fine(("x",), "start")
    fine(("yz",), "wait_recv")
    fine(("xyz",), "start")
    unpack(5, 13)
    weights(5, 13)
    fine_sweep(GC, A, 6, 12, 3, 0)
    fine_sweep(A, B, 7, 11, 2)
    fine(("cy",), "wait_recv")
    fine(("cx",), "start")
    fine(("x", "xz", "xy", "xyz"), "wait_recv")
    unpack(2, 5)
    unpack(13, 16)
    weights(3, 5)
    weights(13, 15)
    fine_sides(GC, A, 3, 12, 3, 0)
    fine(("cx",), "wait_recv")
    fine(("cxx",), "start")
    fine_sides(A, B, 4, 11, 3)

    def residue_pairs(n, _):
        four = fine_residue(B, 5 + 4 * n, 4)
        for half in range(2):
            one, two = four[2 * half], four[2 * half + 1]
            for k in range(8):
                RX[2 * n + half, k % 2, pl.ds(8 * (k // 2), 8), :] = one[k] + two[k]
        return 0

    lax.fori_loop(0, 2, residue_pairs, 0)
    coarsen_rows(0)

    coarse(0, "start")

    for side in range(2):
        for n in range(2):
            p = (10 if side == 0 else 6) + n
            acc = blank
            for j, r in enumerate(starts):
                turned = pltpu.roll(B[p, 2, pl.ds(r, 8), :], (16 * j + 8) % 128, 1)
                acc = jnp.where((lane >= 16 * j) & (lane < 16 * j + 16), turned, acc)
            SS[side, n] = acc
    fine(("s",), "start")

    cylow = (gy * 16 + sub - 8) >= 0
    cyhigh = (gy * 16 + sub + 16) < 256

    fine(("cxx",), "wait_recv")

    def coarse_unpack(k):
        for p in range(CX):
            col, i = [(0, 3), (1, 0), (1, 1), (1, 2), (1, 3), (2, 0), (2, 1), (2, 2), (2, 3),
                      (3, 0), (3, 1), (3, 2), (3, 3), (4, 0)][p]
            for r, (row, j) in enumerate(((0, 1), (1, 0), (1, 1), (2, 0))):
                m = 2 * i + j
                turned = pltpu.roll(QR[k, col, row], (128 - 16 * m - 8) % 128, 1)
                CO[k, p, 1, pl.ds(8 * r, 8), :] = jnp.where(zmask, turned, 0.0)

    coarse_unpack(1)

    def coarse_weights(p, _):
        at = gx * 4 + p - 5
        scale = jnp.where((at >= 0) & (at < 32), DAMP, 0.0).astype(F32)
        for n, r in enumerate((0, 8, 16, 24)):
            scales = [CO[1, p, t, pl.ds(r, 8), :] for t in range(2)]
            keep_factors((K2, KB, KBV, KA, KAV), p, pl.ds(r, 8), scales, lane, 0.25, 0.5)
            for t in range(2):
                w = scale / (1.05 + 60.0 * scales[t])
                if r == 0:
                    w = jnp.where(cylow, w, 0.0)
                if r == 24:
                    w = jnp.where(cyhigh, w, 0.0)
                if t == 1:
                    w = jnp.where(zmask, w, 0.0)
                CW[p, t, pl.ds(r, 8), :] = w
        return 0

    lax.fori_loop(0, CX, coarse_weights, 0)

    fine(("z", "x", "y", "xz", "yz", "xy", "xyz", "cy", "cx", "cxx"), "wait_send")
    coarse(0, "wait_recv")
    coarse_unpack(0)

    def coarse_first(p, _):
        for r in (0, 8, 16, 24):
            for t in range(2):
                rows = pl.ds(r, 8)
                CA[p, t, rows, :] = CW[p, t, rows, :] * CO[0, p, t, rows, :]
        return 0

    lax.fori_loop(0, CX, coarse_first, 0)

    def coarse_sweep(src, dst, low, high, step):
        def one(n, _):
            base = low + step * n
            for r in (4, 12, 20):
                rows = pl.ds(r, 8)
                whole = stencil(src, (KB, KBV, KA, KAV), base, step, r, 2, (0, 1), lane, 0.5)
                for k in range(step):
                    p = base + k
                    for t, v, s, b in whole[k]:
                        dst[p, t, rows, :] = 0.4 * v + CW[p, t, rows, :] * (
                            CO[0, p, t, rows, :] + K2[p, t, rows, :] * s + b
                        )
            return 0

        lax.fori_loop(0, (high - low) // step, one, 0)

    coarse_sweep(CA, CB, 1, 13, 4)
    coarse_sweep(CB, CA, 2, 12, 5)
    coarse_sweep(CA, CB, 3, 11, 4)

    ri = lax.broadcasted_iota(jnp.int32, (128, 256), 0)
    ci = lax.broadcasted_iota(jnp.int32, (128, 256), 1)
    spread = jnp.where(ci // 2 == ri, 1.0, 0.0).astype(F32)
    rh = lax.broadcasted_iota(jnp.int32, (128, 128), 0)
    ch = lax.broadcasted_iota(jnp.int32, (128, 128), 1)
    source = ch // 2 + 64 * gz
    keep = (ch >= zfirst) & (ch < zfirst + 8)
    spread_h = jnp.where((source == rh) & keep, 1.0, 0.0).astype(F32)
    mine = jnp.concatenate([CB[3 + q, 0, pl.ds(4, 24), :] for q in range(8)], axis=0)
    other = jnp.concatenate([CB[3 + q, 1, pl.ds(4, 24), :] for q in range(8)], axis=0)
    wide = jnp.dot(mine, spread, preferred_element_type=F32, precision=lax.Precision.HIGHEST)
    wide_h = jnp.dot(other, spread_h, preferred_element_type=F32, precision=lax.Precision.HIGHEST)
    for q in range(8):
        for t in range(3):
            part = (wide[24 * q : 24 * q + 24, 128 * t : 128 * t + 128] if t < 2
                    else wide_h[24 * q : 24 * q + 24])
            UPS[q, t, pl.ds(0, 24, stride=2), :] = part
            UPS[q, t, pl.ds(1, 24, stride=2), :] = part

    fine(("s",), "wait_send")
    fine(("s",), "wait_recv")

    def spread_edge(side, first):
        for n in range(2):
            for j, r in enumerate(starts):
                turned = pltpu.roll(SR[side, n], (128 - 16 * j - 8) % 128, 1)
                B[first + n, 2, pl.ds(r, 8), :] = jnp.where(zmask, turned, 0.0)

    @pl.when(gx > 0)
    def _():
        spread_edge(0, 2)

    @pl.when(gx < NXD - 1)
    def _():
        spread_edge(1, 14)

    def add_up(q, _):
        for half in range(2):
            for r in range(6):
                for t in range(3):
                    rows = pl.ds(8 * r, 8)
                    p = 2 * q + 1 + half
                    A[p, t, rows, :] = B[p, t, rows, :] + UPS[q, t, rows, :]
        return 0

    lax.fori_loop(0, 8, add_up, 0)

    fine_sweep(A, B, 3, 15, 3)
    fine_sweep(B, A, 4, 14, 5)

    def finish(n, _):
        both = fine_residue(A, 5 + 4 * n, 4)
        for k in range(4):
            x = 4 * n + k
            for i in range(8):
                t, r = i % 2, 8 * (i // 2)
                res_ref[x, pl.ds(r, 8), pl.ds(128 * t, 128)] = both[k][i]
                sol_ref[x, pl.ds(r, 8), pl.ds(128 * t, 128)] = A[5 + x, t, pl.ds(8 + r, 8), :]
        return 0

    lax.fori_loop(0, 2, finish, 0)

    coarse(0, "wait_send")


def closing(sol_ref, res_ref, sol_hbm, res_hbm, sems):
    copies = [
        pltpu.make_async_copy(sol_ref, sol_hbm, sems.at[0]),
        pltpu.make_async_copy(res_ref, res_hbm, sems.at[1]),
    ]
    for cp in copies:
        cp.start()
    for cp in copies:
        cp.wait()


def on_device(right_side, volscale):
    shape = pltpu.VMEM(right_side.shape, F32)
    fine = pltpu.VMEM((PX, 3, ROWS, 128), F32)
    coarse = pltpu.VMEM((CX, 2, CROWS, 128), F32)
    any_space = pl.BlockSpec(memory_space=pl.ANY)
    sol, res = pl.pallas_call(
        kernel,
        out_shape=(shape, shape),
        in_specs=[any_space] * 2,
        out_specs=(pl.BlockSpec(memory_space=pltpu.VMEM),) * 2,
        scratch_shapes=[
            pltpu.VMEM((2, PX, 3, ROWS, 128), F32),
            pltpu.VMEM((8, 8, 128), F32),
            pltpu.VMEM((3, PX, 8, 128), F32),
            pltpu.VMEM((2, 2, 8, 128), F32),
            pltpu.VMEM((2, 2, 8, 128), F32),
            *[fine] * 8,
            pltpu.VMEM((4, 2, 32, 128), F32),
            pltpu.VMEM((2, CX, 2, CROWS, 128), F32),
            pltpu.VMEM((2, 8, 128), F32),
            pltpu.VMEM((2, 5, 3, 8, 128), F32),
            *[coarse] * 8,
            pltpu.VMEM((8, 3, ROWS, 128), F32),
            pltpu.SemaphoreType.DMA((4,)),
            pltpu.SemaphoreType.DMA((NF,)),
            pltpu.SemaphoreType.DMA((NF,)),
            pltpu.SemaphoreType.DMA((NC,)),
            pltpu.SemaphoreType.DMA((NC,)),
        ],
        compiler_params=pltpu.CompilerParams(collective_id=0, has_side_effects=True),
    )(right_side, volscale)
    plain = jax.ShapeDtypeStruct(right_side.shape, F32)
    in_vmem = pl.BlockSpec(memory_space=pltpu.VMEM)
    sol = pltpu.with_memory_space_constraint(sol, pltpu.VMEM)
    res = pltpu.with_memory_space_constraint(res, pltpu.VMEM)
    return pl.pallas_call(
        closing,
        out_shape=(plain, plain),
        in_specs=[in_vmem] * 2,
        out_specs=(any_space, any_space),
        scratch_shapes=[pltpu.SemaphoreType.DMA((2,))],
        compiler_params=pltpu.CompilerParams(vmem_limit_bytes=1 << 20),
    )(sol, res)


def solution(mesh):
    placed = (P("gx", "gy", "gz"), P("gx", "gy", "gz"))
    return jax.shard_map(
        on_device,
        mesh=mesh,
        in_specs=placed,
        out_specs=(P("gx", "gy", "gz"), P("gx", "gy", "gz")),
        check_vma=False,
    )
```
